32 devices in a mesh: dp: 8 (over z, x), tensor: 4 (over y, core).
Axes of the slice: x: 2, y: 2, z: 4, core: 2. Of those that a mesh axis runs over, the one named last changes fastest.
Arguments:
- tokens: bfloat16 [8192, 2048], P('dp'), may hold values from -12 to 12, as said below
- attention_gain: bfloat16 [2048], P('dp'), may hold values from 0.5 to 1.5
- query_matrix: bfloat16 [2048, 2048], P('dp', 'tensor'), may hold values from -2 to 2, as said below
- key_matrix: bfloat16 [2048, 512], P('dp', 'tensor'), may hold values from -2 to 2, as said below
- value_matrix: bfloat16 [2048, 512], P('dp', 'tensor'), may hold values from -0.125 to 0.125
- output_weight: bfloat16 [2048, 2048], P('tensor', 'dp'), may hold values from -0.5 to 0.5
- feed_gain: bfloat16 [2048], P('dp'), may hold values from 0.5 to 1.5
- gate_weight: bfloat16 [2048, 8192], P('dp', 'tensor'), may hold values from -0.125 to 0.125
- up_weight: bfloat16 [2048, 8192], P('dp', 'tensor'), may hold values from -0.125 to 0.125
- down_weight: bfloat16 [8192, 2048], P('tensor', 'dp'), may hold values from -0.0625 to 0.0625
- sequence_lengths: int32 [8, 8], P('dp'), may hold values from 0 to 1024, as said below
- block_mask: int32 [64, 8], P('dp'), may hold values from 0 to 1, as said below
- cotangent: bfloat16 [8192, 2048], P('dp'), may hold values from -6 to 6
Outputs:
- block_output: bfloat16 [8192, 2048], P('dp')
- input_grad: float32 [8192, 2048], P('dp')
- attention_gain_grad: float32 [2048], P('dp')
- query_grad: float32 [2048, 2048], P('dp', 'tensor')
- key_grad: float32 [2048, 512], P('dp', 'tensor')
- value_grad: float32 [2048, 512], P('dp', 'tensor')
- output_grad: float32 [2048, 2048], P('tensor', 'dp')
- feed_gain_grad: float32 [2048], P('dp')
- gate_grad: float32 [2048, 8192], P('dp', 'tensor')
- up_grad: float32 [2048, 8192], P('dp', 'tensor')
- down_grad: float32 [8192, 2048], P('tensor', 'dp')
The draws below stay inside these ranges and needn't reach their ends.
Inputs may be any that keep to these rules, and one draw needn't show every extreme that they name: `sequence_lengths`: row d lists, in order, the lengths of the sequences packed into the token slots of index d of dp: nonzero lengths of 128 or more come first, zeros fill the rest, and the sequences' whole blocks of 128 slots together are at most 8. `block_mask`: entry (d * 8 + i, j) is 1 exactly where query block i and key block j of index d of dp lie in the same sequence and j <= i. `tokens`: real values of the layer's input. `query_matrix`: real values of the query projection. `key_matrix`: real values of the key projection.
All inputs are finite; a program needn't handle non-finite values.
Results may differ from the reference program's by a relative error of at most 0.024.
Values may be sent and summed in bfloat16 or wider, within the bound.
A program may use at most 256 MiB of HBM per device.

```python
import jax
import jax.numpy as jnp
from jax import lax

MODEL_WIDTH = 2048
QUERY_HEADS = 32
KEY_VALUE_HEADS = 8
HEAD_SIZE = 64
FF = 8192
BLOCK = 128
MIN_LEN = 128
NBLK = 8
TOK_DEV = 1024
TOKENS = 8192
N_DP = 8


def layout_draw(key):
    key = jax.random.fold_in(key, 4127)
    key_used, key_starts, key_tail = jax.random.split(key, 3)
    block_index = jnp.arange(NBLK, dtype=jnp.int32)
    device_index = jnp.arange(N_DP, dtype=jnp.int32)
    used = jax.random.randint(key_used, (N_DP,), (NBLK + 1) // 2, NBLK + 1).astype(jnp.int32)
    used = jnp.where(device_index == 0, NBLK, used).astype(jnp.int32)
    starts = jax.random.randint(key_starts, (N_DP, NBLK), 0, 3) == 0
    starts = starts & (device_index[:, None] > 0) & (block_index[None, :] < used[:, None])
    starts = starts | (block_index[None, :] == 0)
    block_seq = (jnp.cumsum(starts.astype(jnp.int32), axis=1) - 1).astype(jnp.int32)
    live = block_index[None, :] < used[:, None]
    member = (block_seq[:, :, None] == block_index[None, None, :]) & live[:, :, None]
    counts = jnp.sum(member.astype(jnp.int32), axis=1).astype(jnp.int32)
    tail = jax.random.randint(key_tail, (N_DP, NBLK), 1, BLOCK + 1).astype(jnp.int32)
    tail = jnp.where(device_index[:, None] == 0, BLOCK, tail).astype(jnp.int32)
    lengths = jnp.where(counts > 0, jnp.maximum(MIN_LEN, BLOCK * (counts - 1) + tail), 0).astype(jnp.int32)
    same = block_seq[:, :, None] == block_seq[:, None, :]
    causal = block_index[None, None, :] <= block_index[None, :, None]
    both_live = live[:, :, None] & live[:, None, :]
    masks = (same & causal & both_live).astype(jnp.int32)
    return (lengths, masks.reshape(N_DP * NBLK, NBLK))


def draw_sequence_lengths(key, part):
    lengths, masks = layout_draw(key)
    return lengths


def draw_block_mask(key, part):
    lengths, masks = layout_draw(key)
    return masks


def draw_tokens(key, part):
    key = jax.random.fold_in(key, 6271)
    key_noise = jax.random.fold_in(key, 0)
    value_vectors = jnp.clip(jax.random.normal(key_noise, (TOKENS, MODEL_WIDTH), jnp.float32), -6.0, 6.0)
    return value_vectors.astype(jnp.bfloat16)


def projection_sample(key, columns):
    raw = jnp.clip(jax.random.normal(key, (MODEL_WIDTH, columns), jnp.float32), -6.0, 6.0)
    value_vectors = raw * MODEL_WIDTH ** (-0.5)
    return value_vectors.astype(jnp.bfloat16)


def draw_query_matrix(key, part):
    return projection_sample(jax.random.fold_in(key, 811), QUERY_HEADS * HEAD_SIZE)


def draw_key_matrix(key, part):
    return projection_sample(jax.random.fold_in(key, 907), KEY_VALUE_HEADS * HEAD_SIZE)


def block_scale(key, extent, cuts, smallest, top_value):
    gain = 1.0
    for axis_at, blocks in cuts:
        heights = jax.random.uniform(jax.random.fold_in(jax.random.fold_in(key, 6), axis_at), (blocks,), jnp.float32, smallest / len(cuts), top_value / len(cuts))
        gain = gain * jnp.repeat(jnp.exp(heights), extent[axis_at] // blocks).reshape((-1,) + (1,) * (len(extent) - 1 - axis_at))
    return gain


def centred(stream_key, shape, width, bound, pieces=(), kind=jnp.bfloat16):
    drawn = jax.random.normal(stream_key, shape, jnp.float32) * width
    if len(pieces) > 0:
        drawn = block_scale(stream_key, shape, pieces, -0.22, 0.18) * drawn
    return jnp.clip(drawn, min=-bound, max=bound).astype(kind)


def setup_inputs(seed: int = 0) -> dict:
    key_of = jax.random.split(jax.random.key(seed), 14)
    tokens = draw_tokens(jax.random.fold_in(key_of[13], 71), 0)
    attention_gain = jnp.clip(1.0 + 0.1 * jax.random.normal(key_of[1], (MODEL_WIDTH,), jnp.float32), 0.5, 1.5).astype(jnp.bfloat16)
    query_matrix = draw_query_matrix(jax.random.fold_in(key_of[13], 71), 0)
    key_matrix = draw_key_matrix(jax.random.fold_in(key_of[13], 71), 0)
    value_matrix = centred(key_of[4], (MODEL_WIDTH, KEY_VALUE_HEADS * HEAD_SIZE), MODEL_WIDTH ** -0.5, 0.125, ((0, 8), (1, 4)))
    output_weight = centred(key_of[5], (QUERY_HEADS * HEAD_SIZE, MODEL_WIDTH), (QUERY_HEADS * HEAD_SIZE // 16) ** -0.5, 0.5, ((0, 4), (1, 8)))
    feed_gain = jnp.clip(1.0 + 0.1 * jax.random.normal(key_of[6], (MODEL_WIDTH,), jnp.float32), 0.5, 1.5).astype(jnp.bfloat16)
    gate_weight = centred(key_of[7], (MODEL_WIDTH, FF), MODEL_WIDTH ** -0.5, 0.125, ((0, 8), (1, 4)))
    up_weight = centred(key_of[8], (MODEL_WIDTH, FF), MODEL_WIDTH ** -0.5, 0.125, ((0, 8), (1, 4)))
    down_weight = centred(key_of[9], (FF, MODEL_WIDTH), FF ** -0.5, 0.0625, ((0, 4), (1, 8)))
    sequence_lengths = draw_sequence_lengths(jax.random.fold_in(key_of[13], 71), 0)
    block_mask = draw_block_mask(jax.random.fold_in(key_of[13], 71), 0)
    cotangent = centred(key_of[12], (TOKENS, MODEL_WIDTH), 1.0, 6.0, ((0, 8),))
    return dict(tokens=tokens, attention_gain=attention_gain, query_matrix=query_matrix, key_matrix=key_matrix, value_matrix=value_matrix, output_weight=output_weight, feed_gain=feed_gain, gate_weight=gate_weight, up_weight=up_weight, down_weight=down_weight, sequence_lengths=sequence_lengths, block_mask=block_mask, cotangent=cotangent)


EPS_NORM = 1e-05
THETA_BASE = 500000.0
NEG_FILL = -1e+30
HIGHEST = lax.Precision.HIGHEST

@jax.custom_vjp
def low(v):
    return lax.optimization_barrier(v.astype(jnp.bfloat16)).astype(jnp.float32)

@jax.custom_vjp
def low_back(v):
    return v

def low_keep(v):
    return (low(v), None)

def low_pass(kept, grad):
    return (grad,)

def back_keep(v):
    return (v, None)

def back_low(kept, grad):
    return (low(grad),)
low.defvjp(low_keep, low_pass)
low_back.defvjp(back_keep, back_low)

def token_layout(lengths_row, total, block):
    lengths_row = lengths_row.astype(jnp.int32)
    blocks_per = ((lengths_row + block - 1) // block).astype(jnp.int32)
    offsets = (jnp.cumsum(blocks_per) - blocks_per).astype(jnp.int32)
    first_token = (offsets * block).astype(jnp.int32)
    indices = jnp.arange(total, dtype=jnp.int32)
    member = (indices[:, None] >= first_token[None, :]) & (blocks_per[None, :] > 0)
    sequence = (lax.optimization_barrier(jnp.sum(member.astype(jnp.int32), axis=1)) - 1).astype(jnp.int32)
    select = sequence[:, None] == jnp.arange(lengths_row.shape[0], dtype=jnp.int32)[None, :]
    begins = lax.optimization_barrier(jnp.sum(jnp.where(select, first_token[None, :], 0), axis=1)).astype(jnp.int32)
    limits = lax.optimization_barrier(jnp.sum(jnp.where(select, lengths_row[None, :], 0), axis=1)).astype(jnp.int32)
    position = (indices - begins).astype(jnp.int32)
    return (sequence, position, position < limits)

def allowed_pairs(sequence, position, valid, mask_blocks, begin_row, rows, block):
    total = sequence.shape[0]
    blocks_all = total // block
    query_seq = sequence[begin_row:begin_row + rows]
    query_pos = position[begin_row:begin_row + rows]
    mask_rows = mask_blocks[begin_row // block:(begin_row + rows) // block]
    tiled = jnp.broadcast_to(mask_rows[:, None, :, None] > 0, (rows // block, block, blocks_all, block)).reshape(rows, total)
    same = query_seq[:, None] == sequence[None, :]
    causal = position[None, :] <= query_pos[:, None]
    diagonal = (begin_row + jnp.arange(rows, dtype=jnp.int32))[:, None] == jnp.arange(total, dtype=jnp.int32)[None, :]
    return tiled & same & causal & valid[None, :] | diagonal

def rope_tables(position, head_dim):
    freqs = THETA_BASE ** (-jnp.arange(head_dim // 2, dtype=jnp.float32) * 2.0 / head_dim)
    angles = position.astype(jnp.float32)[:, None] * freqs[None, :]
    return (jnp.cos(angles), jnp.sin(angles))

def rotate(value_vectors, cosine, sine):
    half = value_vectors.shape[-1] // 2
    first = value_vectors[..., :half]
    second = value_vectors[..., half:]
    return jnp.concatenate([first * cosine - second * sine, second * cosine + first * sine], axis=-1)

def matrix_multiply(left, right):
    return jnp.dot(left, right, precision=HIGHEST, preferred_element_type=jnp.float32)

def normalize(stream):
    return stream * lax.rsqrt(lax.optimization_barrier(jnp.mean(stream * stream, axis=-1, keepdims=True)) + EPS_NORM)

def device_layer(params, stream, lengths_row, mask_blocks):
    attention_gain, query_matrix, key_matrix, value_matrix, output_weight, feed_gain, gate_weight, up_weight, down_weight = params
    token_positions = stream.shape[0]
    head_groups = QUERY_HEADS // KEY_VALUE_HEADS
    sequence, position, valid = token_layout(lengths_row, token_positions, BLOCK)
    cosine, sine = rope_tables(position, HEAD_SIZE)
    normalized_input = low(normalize(stream) * attention_gain)
    query_vectors = matrix_multiply(normalized_input, query_matrix).reshape(token_positions, KEY_VALUE_HEADS, head_groups, HEAD_SIZE)
    key_vectors = matrix_multiply(normalized_input, key_matrix).reshape(token_positions, KEY_VALUE_HEADS, HEAD_SIZE)
    value_vectors = matrix_multiply(normalized_input, value_matrix).reshape(token_positions, KEY_VALUE_HEADS, HEAD_SIZE)
    query_vectors = low(rotate(low_back(query_vectors), cosine[:, None, None, :], sine[:, None, None, :]))
    key_vectors = low(rotate(low_back(key_vectors), cosine[:, None, :], sine[:, None, :]))
    value_vectors = low(low_back(value_vectors))
    scores = low_back(jnp.einsum('qkgd,skd->kgqs', query_vectors, key_vectors, precision=HIGHEST) * HEAD_SIZE ** (-0.5))
    allowed = allowed_pairs(sequence, position, valid, mask_blocks, 0, token_positions, BLOCK)
    scores = jnp.where(allowed[None, None], scores, NEG_FILL)
    weights = low(jax.nn.softmax(scores, axis=-1))
    attended = jnp.einsum('kgqs,skd->qkgd', weights, value_vectors, precision=HIGHEST)
    attended = low(low_back(attended.reshape(token_positions, QUERY_HEADS * HEAD_SIZE)))
    middle = stream + low_back(matrix_multiply(attended, output_weight))
    normed_two = low(normalize(middle) * feed_gain)
    gate = low_back(matrix_multiply(normed_two, gate_weight))
    upper = low_back(matrix_multiply(normed_two, up_weight))
    hidden = low(jax.nn.silu(gate) * upper)
    return middle + low_back(matrix_multiply(hidden, down_weight))

def reference(tokens, attention_gain, query_matrix, key_matrix, value_matrix, output_weight, feed_gain, gate_weight, up_weight, down_weight, sequence_lengths, block_mask, cotangent):
    params = tuple((w.astype(jnp.float32) for w in (attention_gain, query_matrix, key_matrix, value_matrix, output_weight, feed_gain, gate_weight, up_weight, down_weight)))
    streams = tokens.astype(jnp.float32).reshape(N_DP, TOK_DEV, MODEL_WIDTH)
    masks = block_mask.reshape(N_DP, NBLK, NBLK)
    layer_saved = jax.checkpoint(device_layer)

    def forward(streams, params):

        def step(carry, item):
            return (carry, layer_saved(params, item[0], item[1], item[2]))
        _, outputs = lax.scan(step, jnp.zeros((), jnp.float32), (streams, sequence_lengths, masks))
        return outputs
    outputs, pullback = jax.vjp(forward, streams, params)
    stream_grad, grads = pullback(cotangent.astype(jnp.float32).reshape(N_DP, TOK_DEV, MODEL_WIDTH))
    return (outputs.reshape(TOKENS, MODEL_WIDTH).astype(jnp.bfloat16), stream_grad.reshape(TOKENS, MODEL_WIDTH), grads[0], grads[1], grads[2], grads[3], grads[4], grads[5], grads[6], grads[7], grads[8])
```

```python
import jax
import jax.numpy as jnp
from jax import lax
from jax.sharding import PartitionSpec as P

HEAD_SIZE = 64
BLOCK = 128


EPS_NORM = 1e-05
THETA_BASE = 500000.0
NEG_FILL = -1e30


def token_layout(lengths_row, total, block):
    blocks_per = (lengths_row + block - 1) // block
    offsets = jnp.cumsum(blocks_per) - blocks_per
    first_token = offsets * block
    indices = jnp.arange(total, dtype=jnp.int32)
    member = (indices[:, None] >= first_token[None, :]) & (blocks_per[None, :] > 0)
    sequence = jnp.sum(member.astype(jnp.int32), axis=1) - 1
    select = sequence[:, None] == jnp.arange(lengths_row.shape[0], dtype=jnp.int32)[None, :]
    begins = jnp.sum(jnp.where(select, first_token[None, :], 0), axis=1)
    limits = jnp.sum(jnp.where(select, lengths_row[None, :], 0), axis=1)
    position = indices - begins
    return (sequence, position, position < limits)


def allowed_pairs(sequence, position, valid, mask_blocks, begin_row, rows, block):
    total = sequence.shape[0]
    blocks_all = total // block
    query_seq = sequence[begin_row : begin_row + rows]
    query_pos = position[begin_row : begin_row + rows]
    mask_rows = mask_blocks[begin_row // block : (begin_row + rows) // block]
    tiled = jnp.broadcast_to(
        mask_rows[:, None, :, None] > 0, (rows // block, block, blocks_all, block)
    ).reshape(rows, total)
    same = query_seq[:, None] == sequence[None, :]
    causal = position[None, :] <= query_pos[:, None]
    diagonal = (begin_row + jnp.arange(rows, dtype=jnp.int32))[:, None] == jnp.arange(
        total, dtype=jnp.int32
    )[None, :]
    return tiled & same & causal & valid[None, :] | diagonal


def rope_tables(position, head_dim):
    freqs = THETA_BASE ** (-jnp.arange(head_dim // 2, dtype=jnp.float32) * 2.0 / head_dim)
    angles = position.astype(jnp.float32)[:, None] * freqs[None, :]
    return (jnp.cos(angles), jnp.sin(angles))


def rotate(value_vectors, cosine, sine):
    half = value_vectors.shape[-1] // 2
    first = value_vectors[..., :half]
    second = value_vectors[..., half:]
    return jnp.concatenate(
        [first * cosine - second * sine, second * cosine + first * sine], axis=-1
    )


def rotate_back(value_vectors, cosine, sine):
    half = value_vectors.shape[-1] // 2
    first = value_vectors[..., :half]
    second = value_vectors[..., half:]
    return jnp.concatenate(
        [first * cosine + second * sine, second * cosine - first * sine], axis=-1
    )


def contract_rows(left, right):
    return lax.dot_general(
        left, right, (((0,), (0,)), ((), ())), preferred_element_type=jnp.float32
    )


def contract_cols(left, right):
    return lax.dot_general(
        left, right, (((1,), (1,)), ((), ())), preferred_element_type=jnp.float32
    )


def norm_parts(stream):
    inverse = lax.rsqrt(jnp.mean(stream * stream, axis=-1, keepdims=True) + EPS_NORM)
    return (stream * inverse, inverse)


def norm_back(grad_normed, gain, normalized_input, inverse):
    scaled = grad_normed * gain[None, :]
    return inverse * (
        scaled - normalized_input * jnp.mean(scaled * normalized_input, axis=-1, keepdims=True)
    )


def block_rows():
    return 512


def block_scores(query_block, key_vectors, layout, mask_blocks, begin_row, rows):
    sequence, position, valid = layout
    allowed = allowed_pairs(sequence, position, valid, mask_blocks, begin_row, rows, BLOCK)
    scores = jnp.einsum(
        "qkgd,skd->kgqs", query_block, key_vectors, preferred_element_type=jnp.float32
    ) * HEAD_SIZE ** (-0.5)
    return jnp.where(allowed[None, None], scores, NEG_FILL)


def attention_forward(query_vectors, key_vectors, value_vectors, layout, mask_blocks):
    token_positions = query_vectors.shape[0]
    rows = block_rows()
    outputs = []
    totals = []
    for begin_row in range(0, token_positions, rows):
        scores = block_scores(
            query_vectors[begin_row : begin_row + rows],
            key_vectors,
            layout,
            mask_blocks,
            begin_row,
            rows,
        )
        highest = jnp.max(scores, axis=-1, keepdims=True)
        expo = jnp.exp(scores - highest)
        summed = jnp.sum(expo, axis=-1, keepdims=True)
        weights = (expo / summed).astype(jnp.bfloat16)
        outputs.append(
            jnp.einsum("kgqs,skd->qkgd", weights, value_vectors, preferred_element_type=jnp.float32)
        )
        totals.append(highest + jnp.log(summed))
    return (jnp.concatenate(outputs, axis=0), totals)


def attention_backward(
    query_vectors, key_vectors, value_vectors, grad_out, totals, layout, mask_blocks
):
    token_positions = query_vectors.shape[0]
    rows = block_rows()
    grad_queries = []
    grad_keys = jnp.zeros(key_vectors.shape, jnp.float32)
    grad_values = jnp.zeros(value_vectors.shape, jnp.float32)
    for number, begin_row in enumerate(range(0, token_positions, rows)):
        query_block = query_vectors[begin_row : begin_row + rows]
        grad_block = grad_out[begin_row : begin_row + rows]
        scores = block_scores(query_block, key_vectors, layout, mask_blocks, begin_row, rows)
        probs = jnp.exp(scores - totals[number])
        grad_probs = jnp.einsum(
            "qkgd,skd->kgqs", grad_block, value_vectors, preferred_element_type=jnp.float32
        )
        centre = jnp.sum(probs * grad_probs, axis=-1, keepdims=True)
        grad_scores = (probs * (grad_probs - centre)).astype(jnp.bfloat16)
        grad_queries.append(
            jnp.einsum(
                "kgqs,skd->qkgd", grad_scores, key_vectors, preferred_element_type=jnp.float32
            )
            * HEAD_SIZE ** (-0.5)
        )
        grad_keys = grad_keys + jnp.einsum(
            "kgqs,qkgd->skd", grad_scores, query_block, preferred_element_type=jnp.float32
        ) * HEAD_SIZE ** (-0.5)
        grad_values = grad_values + jnp.einsum(
            "kgqs,qkgd->skd",
            probs.astype(jnp.bfloat16),
            grad_block,
            preferred_element_type=jnp.float32,
        )
    return (jnp.concatenate(grad_queries, axis=0), grad_keys, grad_values)


def tensor_sum(partial):
    rows = partial.shape[0] // 2
    core = lax.axis_index("tensor") % 2
    count = lax.axis_size("tensor")
    flip_core = [(i, i ^ 1) for i in range(count)]
    flip_y = [(i, i ^ 2) for i in range(count)]
    mine = lax.dynamic_slice_in_dim(partial, core * rows, rows, axis=0)
    other = lax.dynamic_slice_in_dim(partial, (1 - core) * rows, rows, axis=0)
    received = lax.ppermute(other, "tensor", flip_core)
    chip = (mine.astype(jnp.float32) + received.astype(jnp.float32)).astype(jnp.bfloat16)
    across = lax.ppermute(chip, "tensor", flip_y)
    total = (chip.astype(jnp.float32) + across.astype(jnp.float32)).astype(jnp.bfloat16)
    back = lax.ppermute(total, "tensor", flip_core)
    return jnp.where(
        core == 0,
        jnp.concatenate([total, back], axis=0),
        jnp.concatenate([back, total], axis=0),
    )


def shards(
    tokens,
    attention_gain,
    query_matrix,
    key_matrix,
    value_matrix,
    output_weight,
    feed_gain,
    gate_weight,
    up_weight,
    down_weight,
    sequence_lengths,
    block_mask,
    cotangent,
):
    token_positions = tokens.shape[0]
    local_heads = query_matrix.shape[1] // HEAD_SIZE
    local_kv = key_matrix.shape[1] // HEAD_SIZE
    head_groups = local_heads // local_kv
    stream = tokens.astype(jnp.float32)
    layout = token_layout(sequence_lengths[0], token_positions, BLOCK)
    cosine, sine = rope_tables(layout[1], HEAD_SIZE)
    cos_query, sin_query = (cosine[:, None, None, :], sine[:, None, None, :])
    cos_key, sin_key = (cosine[:, None, :], sine[:, None, :])
    wide_q, wide_k = query_matrix.shape[1], key_matrix.shape[1]
    packed_full = lax.all_gather(
        jnp.concatenate([query_matrix, key_matrix, value_matrix], axis=1), "dp", axis=0, tiled=True
    )
    query_full = packed_full[:, :wide_q]
    key_full = packed_full[:, wide_q : wide_q + wide_k]
    value_full = packed_full[:, wide_q + wide_k :]
    output_full, gain_one = (
        lax.all_gather(output_weight, "dp", axis=1, tiled=True),
        lax.all_gather(attention_gain, "dp", axis=0, tiled=True),
    )
    gain_first = gain_one.astype(jnp.float32)
    normalized_input, inverse = norm_parts(stream)
    normed_low = (normalized_input * gain_first[None, :]).astype(jnp.bfloat16)
    query_vectors = jnp.dot(normed_low, query_full, preferred_element_type=jnp.float32).reshape(
        token_positions, local_kv, head_groups, HEAD_SIZE
    )
    key_vectors = jnp.dot(normed_low, key_full, preferred_element_type=jnp.float32).reshape(
        token_positions, local_kv, HEAD_SIZE
    )
    value_vectors = (
        jnp.dot(normed_low, value_full, preferred_element_type=jnp.float32)
        .reshape(token_positions, local_kv, HEAD_SIZE)
        .astype(jnp.bfloat16)
    )
    query_vectors = rotate(query_vectors, cos_query, sin_query).astype(jnp.bfloat16)
    key_vectors = rotate(key_vectors, cos_key, sin_key).astype(jnp.bfloat16)
    attended, totals = attention_forward(
        query_vectors, key_vectors, value_vectors, layout, block_mask
    )
    attended = attended.reshape(token_positions, local_heads * HEAD_SIZE).astype(jnp.bfloat16)
    attention_part = jnp.dot(attended, output_full, preferred_element_type=jnp.float32)
    gate_full, up_full, down_full, gain_two = (
        lax.all_gather(gate_weight, "dp", axis=0, tiled=True),
        lax.all_gather(up_weight, "dp", axis=0, tiled=True),
        lax.all_gather(down_weight, "dp", axis=1, tiled=True),
        lax.all_gather(feed_gain, "dp", axis=0, tiled=True),
    )
    gain_second = gain_two.astype(jnp.float32)
    middle = stream + tensor_sum(attention_part.astype(jnp.bfloat16)).astype(jnp.float32)
    normed_two, inverse_two = norm_parts(middle)
    normed_two_low = (normed_two * gain_second[None, :]).astype(jnp.bfloat16)
    gate = jnp.dot(normed_two_low, gate_full, preferred_element_type=jnp.float32)
    upper = jnp.dot(normed_two_low, up_full, preferred_element_type=jnp.float32)
    hidden = (jax.nn.silu(gate) * upper).astype(jnp.bfloat16)
    feed_part = jnp.dot(hidden, down_full, preferred_element_type=jnp.float32)
    block_output = (
        middle + tensor_sum(feed_part.astype(jnp.bfloat16)).astype(jnp.float32)
    ).astype(jnp.bfloat16)
    grad_out = cotangent.astype(jnp.float32)
    down_grad = contract_rows(hidden, cotangent)
    grad_hidden = contract_cols(cotangent, down_full)
    sigmoid = jax.nn.sigmoid(gate)
    grad_gate = (grad_hidden * upper * sigmoid * (1.0 + gate * (1.0 - sigmoid))).astype(
        jnp.bfloat16
    )
    grad_up = (grad_hidden * gate * sigmoid).astype(jnp.bfloat16)
    gate_grad = contract_rows(normed_two_low, grad_gate)
    up_grad = contract_rows(normed_two_low, grad_up)
    feed_partial = contract_cols(grad_gate, gate_full) + contract_cols(grad_up, up_full)
    grad_normed_two = tensor_sum(feed_partial.astype(jnp.bfloat16)).astype(jnp.float32)
    feed_gain_full = jnp.sum(grad_normed_two * normed_two, axis=0)
    grad_middle = grad_out + norm_back(grad_normed_two, gain_second, normed_two, inverse_two)
    gate_grad, up_grad, down_grad, feed_gain_grad = (
        lax.psum_scatter(
            gate_grad.astype(jnp.bfloat16), "dp", scatter_dimension=0, tiled=True
        ).astype(jnp.float32),
        lax.psum_scatter(
            up_grad.astype(jnp.bfloat16), "dp", scatter_dimension=0, tiled=True
        ).astype(jnp.float32),
        lax.psum_scatter(
            down_grad.astype(jnp.bfloat16), "dp", scatter_dimension=1, tiled=True
        ).astype(jnp.float32),
        lax.psum_scatter(
            feed_gain_full.astype(jnp.bfloat16), "dp", scatter_dimension=0, tiled=True
        ).astype(jnp.float32),
    )
    grad_middle_low = grad_middle.astype(jnp.bfloat16)
    output_grad = contract_rows(attended, grad_middle_low)
    grad_attended = (
        contract_cols(grad_middle_low, output_full)
        .astype(jnp.bfloat16)
        .reshape(token_positions, local_kv, head_groups, HEAD_SIZE)
    )
    grad_queries, grad_keys, grad_values = attention_backward(
        query_vectors, key_vectors, value_vectors, grad_attended, totals, layout, block_mask
    )
    grad_queries = (
        rotate_back(grad_queries, cos_query, sin_query)
        .astype(jnp.bfloat16)
        .reshape(token_positions, local_heads * HEAD_SIZE)
    )
    grad_keys = (
        rotate_back(grad_keys, cos_key, sin_key)
        .astype(jnp.bfloat16)
        .reshape(token_positions, local_kv * HEAD_SIZE)
    )
    grad_values = grad_values.astype(jnp.bfloat16).reshape(token_positions, local_kv * HEAD_SIZE)
    query_grad = contract_rows(normed_low, grad_queries)
    key_grad = contract_rows(normed_low, grad_keys)
    value_grad = contract_rows(normed_low, grad_values)
    grad_normed = (
        contract_cols(grad_queries, query_full)
        + contract_cols(grad_keys, key_full)
        + contract_cols(grad_values, value_full)
    )
    grad_normed = tensor_sum(grad_normed.astype(jnp.bfloat16)).astype(jnp.float32)
    attention_gain_full = jnp.sum(grad_normed * normalized_input, axis=0)
    input_grad = grad_middle + norm_back(grad_normed, gain_first, normalized_input, inverse)
    packed_grad = lax.psum_scatter(
        jnp.concatenate([query_grad, key_grad, value_grad], axis=1).astype(jnp.bfloat16),
        "dp",
        scatter_dimension=0,
        tiled=True,
    ).astype(jnp.float32)
    query_grad = packed_grad[:, :wide_q]
    key_grad = packed_grad[:, wide_q : wide_q + wide_k]
    value_grad = packed_grad[:, wide_q + wide_k :]
    output_grad, attention_gain_grad = (
        lax.psum_scatter(
            output_grad.astype(jnp.bfloat16), "dp", scatter_dimension=1, tiled=True
        ).astype(jnp.float32),
        lax.psum_scatter(
            attention_gain_full.astype(jnp.bfloat16), "dp", scatter_dimension=0, tiled=True
        ).astype(jnp.float32),
    )
    return (
        block_output,
        input_grad,
        attention_gain_grad,
        query_grad,
        key_grad,
        value_grad,
        output_grad,
        feed_gain_grad,
        gate_grad,
        up_grad,
        down_grad,
    )


def solution(mesh):
    in_specs = (
        P("dp", None),
        P("dp"),
        P("dp", "tensor"),
        P("dp", "tensor"),
        P("dp", "tensor"),
        P("tensor", "dp"),
        P("dp"),
        P("dp", "tensor"),
        P("dp", "tensor"),
        P("tensor", "dp"),
        P("dp", None),
        P("dp", None),
        P("dp", None),
    )
    out_specs = (
        P("dp", None),
        P("dp", None),
        P("dp"),
        P("dp", "tensor"),
        P("dp", "tensor"),
        P("dp", "tensor"),
        P("tensor", "dp"),
        P("dp"),
        P("dp", "tensor"),
        P("dp", "tensor"),
        P("tensor", "dp"),
    )
    return jax.shard_map(shards, mesh=mesh, in_specs=in_specs, out_specs=out_specs, check_vma=False)
```

```python
import functools

import jax
import jax.numpy as jnp
from jax import lax
from jax.experimental import pallas as pl
from jax.experimental.pallas import tpu as pltpu
from jax.sharding import PartitionSpec as P

HEAD_SIZE = 64
BLOCK = 128
LANES = 128
EPS_NORM = 1e-05
THETA_BASE = 500000.0
NEG_FILL = -1e30
UNIT = 256
ROWS = 256
FOLD = 2
XFIRST = 6
MESH = pl.DeviceIdType.MESH
VMEM = pltpu.VMEM
DMA = pltpu.SemaphoreType.DMA
HBM_SPEC = pl.BlockSpec(memory_space=pl.ANY)
VMEM_SPEC = pl.BlockSpec(memory_space=pltpu.VMEM)
F32 = jnp.float32
BF16 = jnp.bfloat16


def token_layout(lengths_row, total, block):
    blocks_per = (lengths_row + block - 1) // block
    offsets = jnp.cumsum(blocks_per) - blocks_per
    first_token = offsets * block
    indices = jnp.arange(total, dtype=jnp.int32)
    member = (indices[:, None] >= first_token[None, :]) & (blocks_per[None, :] > 0)
    sequence = jnp.sum(member.astype(jnp.int32), axis=1) - 1
    select = sequence[:, None] == jnp.arange(lengths_row.shape[0], dtype=jnp.int32)[None, :]
    begins = jnp.sum(jnp.where(select, first_token[None, :], 0), axis=1)
    limits = jnp.sum(jnp.where(select, lengths_row[None, :], 0), axis=1)
    position = indices - begins
    return (sequence, position, position < limits)


def allowed_pairs(sequence, position, valid, mask_blocks, block):
    total = sequence.shape[0]
    blocks = total // block
    tiled = jnp.broadcast_to(
        mask_blocks[:, None, :, None] > 0, (blocks, block, blocks, block)
    ).reshape(total, total)
    same = sequence[:, None] == sequence[None, :]
    causal = position[None, :] <= position[:, None]
    row = jnp.arange(total, dtype=jnp.int32)
    diagonal = row[:, None] == row[None, :]
    return tiled & same & causal & valid[None, :] | diagonal


def rope_tables(position, head_dim):
    freqs = THETA_BASE ** (-jnp.arange(head_dim // 2, dtype=F32) * 2.0 / head_dim)
    angles = position.astype(F32)[:, None] * freqs[None, :]
    return (jnp.cos(angles), jnp.sin(angles))


def dot(left, right):
    return jnp.dot(left, right, preferred_element_type=F32)


def dot_nt(left, right):
    return lax.dot_general(left, right, (((1,), (1,)), ((), ())), preferred_element_type=F32)


def dot_tn(left, right):
    return lax.dot_general(left, right, (((0,), (0,)), ((), ())), preferred_element_type=F32)


class Place:
    def __init__(self, depth):
        self.depth = depth
        self.me = lax.axis_index("dp")
        self.z = self.me // FOLD
        self.x = self.me % FOLD
        self.right = self.me + FOLD
        self.left = self.me - FOLD
        self.partner = self.z * FOLD + (1 - self.x)
        member = lax.axis_index("tensor")
        self.core = member % 2
        row = member // 2
        self.other = row * 2 + (1 - self.core)
        self.across = (1 - row) * 2 + self.core

    def enter(self):
        count = self.depth * FOLD
        barrier = pltpu.get_barrier_semaphore()
        for step in range(1, count):
            pl.semaphore_signal(
                barrier,
                1,
                device_id={"dp": lax.rem(self.me + step, count)},
                device_id_type=MESH,
            )
        for peer in (self.other, self.across):
            pl.semaphore_signal(barrier, 1, device_id={"tensor": peer}, device_id_type=MESH)
        pl.semaphore_wait(barrier, count + 1)


class Gather:
    def __init__(self, place, g_ref, rows, units, sems, first=0):
        self.place, self.g, self.rows, self.units, self.first = place, g_ref, rows, units, first
        self.z_send, self.z_recv, self.x_send, self.x_recv = sems

    @staticmethod
    def scratch(units, depth):
        return [
            DMA((units, 2, depth)),
            DMA((units, depth)),
            DMA((units, depth)),
            DMA((units, depth)),
        ]

    def block(self, unit, index, count=1):
        start = pl.multiple_of(index * self.rows, self.rows)
        return self.g.at[unit, pl.ds(start, count * self.rows)]

    def along(self, unit, zz, way, wide):
        p = self.place
        if wide:
            ref = self.block(unit, zz * FOLD, FOLD)
        else:
            ref = self.block(unit, zz * FOLD + p.x)
        return pltpu.make_async_remote_copy(
            ref,
            ref,
            self.z_send.at[unit, way, zz],
            self.z_recv.at[unit, zz],
            device_id={"dp": p.left if way else p.right},
            device_id_type=MESH,
        )

    def over(self, unit, zz, incoming=False):
        p = self.place
        ref = self.block(unit, zz * FOLD + (1 - p.x if incoming else p.x))
        return pltpu.make_async_remote_copy(
            ref,
            ref,
            self.x_send.at[unit, zz],
            self.x_recv.at[unit, zz],
            device_id={"dp": p.partner},
            device_id_type=MESH,
        )

    def send_both(self, unit, zz, wide):
        p, last = self.place, self.place.depth - 1

        @pl.when(p.z < last)
        def _():
            self.along(unit, zz, 0, wide).start()

        @pl.when(p.z > 0)
        def _():
            self.along(unit, zz, 1, wide).start()

    def forward(self, unit, step, wide, across):
        p, last = self.place, self.place.depth - 1

        @pl.when(p.z >= step)
        def _():
            zz = p.z - step
            self.along(unit, zz, 0, wide).wait_recv()

            @pl.when(p.z < last)
            def _():
                self.along(unit, zz, 0, wide).start()

            if across:
                self.over(unit, zz).start()

        @pl.when(p.z + step <= last)
        def _():
            zz = p.z + step
            self.along(unit, zz, 1, wide).wait_recv()

            @pl.when(p.z > 0)
            def _():
                self.along(unit, zz, 1, wide).start()

            if across:
                self.over(unit, zz).start()

    def drain(self, unit, wide):
        p, last = self.place, self.place.depth - 1
        for zz in range(p.depth):

            @pl.when((p.z >= zz) & (p.z < last))
            def _():
                self.along(unit, zz, 0, wide).wait_send()

            @pl.when((p.z <= zz) & (p.z > 0))
            def _():
                self.along(unit, zz, 1, wide).wait_send()

    def stage(self, step, unit):
        p, depth = self.place, self.place.depth

        def slow_first():
            if step == 0:
                self.send_both(unit, p.z, False)
                self.over(unit, p.z).start()
            elif step < depth:
                self.forward(unit, step, False, True)
            else:
                for zz in range(depth):
                    self.over(unit, zz, True).wait_recv()
                for zz in range(depth):
                    self.over(unit, zz).wait_send()
                self.drain(unit, False)

        def fast_first():
            if step == 0:
                self.over(unit, p.z).start()
            elif step == 1:
                self.over(unit, p.z, True).wait_recv()
                self.send_both(unit, p.z, True)
            else:
                self.forward(unit, step - 1, True, False)
                if step == depth:
                    self.over(unit, p.z).wait_send()
                    self.drain(unit, True)

        inside = (unit >= 0) & (unit < self.units)
        fast = lax.rem(unit + self.first, XFIRST) == XFIRST - 1
        pl.when(inside & jnp.logical_not(fast))(slow_first)
        pl.when(inside & fast)(fast_first)

    def latency(self):
        return self.place.depth + 1

    def tick(self, time):
        depth = self.place.depth
        for step in range(depth):
            self.stage(step, time - step)
        self.stage(depth, time - depth - 1)


class TensorSum:
    def __init__(self, place, part, bufs, sems):
        self.place, self.part = place, part
        self.half_in, self.half, self.far_in, self.total, self.back = bufs
        self.sends, self.recvs = sems

    @staticmethod
    def scratch(blocks, half, width):
        return [VMEM((blocks, half, width), BF16)] * 5, [DMA((3, blocks)), DMA((3, blocks))]

    def copy(self, step, src, dst, blk):
        p = self.place
        return pltpu.make_async_remote_copy(
            src,
            dst.at[blk],
            self.sends.at[step, blk],
            self.recvs.at[step, blk],
            device_id={"tensor": p.across if step == 1 else p.other},
            device_id_type=MESH,
        )

    def first(self, blk):
        half = self.half.shape[1]
        start = pl.multiple_of((1 - self.place.core) * half, half)
        return self.copy(0, self.part.at[blk, pl.ds(start, half)], self.half_in, blk)

    def second(self, blk):
        return self.copy(1, self.half.at[blk], self.far_in, blk)

    def third(self, blk):
        return self.copy(2, self.total.at[blk], self.back, blk)

    def begin(self, blk):
        self.first(blk).start()

    def middle(self, blk):
        half = self.half.shape[1]
        self.first(blk).wait_recv()
        start = pl.multiple_of(self.place.core * half, half)
        mine = self.part[blk, pl.ds(start, half), :].astype(F32)
        self.half[blk] = (mine + self.half_in[blk].astype(F32)).astype(BF16)
        self.second(blk).start()

    def late(self, blk):
        self.second(blk).wait_recv()
        self.total[blk] = (self.half[blk].astype(F32) + self.far_in[blk].astype(F32)).astype(BF16)
        self.third(blk).start()

    def end(self, blk):
        half = self.half.shape[1]
        self.third(blk).wait_recv()
        core = self.place.core
        return (
            (pl.multiple_of(blk * 2 * half + core * half, half), self.total),
            (pl.multiple_of(blk * 2 * half + (1 - core) * half, half), self.back),
        )

    def drain(self, blk):
        self.first(blk).wait_send()
        self.second(blk).wait_send()
        self.third(blk).wait_send()


def turn(values, cosine, sine, back=False):
    half = HEAD_SIZE // 2
    lane = lax.broadcasted_iota(jnp.int32, (1, LANES), 1)
    low = lax.rem(lane, HEAD_SIZE) < half
    tiles = []
    for start in range(0, values.shape[1], LANES):
        tile = values[:, start : start + LANES]
        swapped = jnp.where(low, pltpu.roll(tile, LANES - half, 1), pltpu.roll(tile, half, 1))
        if back:
            tiles.append(tile * cosine - swapped * sine)
        else:
            tiles.append(tile * cosine + swapped * sine)
    return tiles[0] if len(tiles) == 1 else jnp.concatenate(tiles, axis=1)


def probabilities(query, keys, allowed):
    scores = dot_nt(query, keys) * HEAD_SIZE ** (-0.5)
    scores = jnp.where(allowed, scores, NEG_FILL)
    expo = jnp.exp(scores - jnp.max(scores, axis=-1, keepdims=True))
    return expo / jnp.sum(expo, axis=-1, keepdims=True)


def normed(stream):
    return stream * lax.rsqrt(jnp.mean(stream * stream, axis=-1, keepdims=True) + EPS_NORM)


def attend_kernel(cfg, *refs):
    (
        x_ref,
        w_ref,
        gain_ref,
        mask_ref,
        cos_ref,
        sin_ref,
        g_ref,
        a_ref,
        q_ref,
        k_ref,
        v_ref,
        att_ref,
        sum_ref,
        b_ref,
        gain_in,
        gains,
        weights,
        part,
        half_in,
        half,
        far_in,
        total,
        back,
        sum_sends,
        sum_recvs,
        z_send,
        z_recv,
        x_send,
        x_recv,
        gain_send,
        gain_recv,
        local_sem,
    ) = refs
    depth, units, q_units, o_units = cfg
    place = Place(depth)
    count = depth * FOLD
    token_count, width = x_ref.shape
    rows = w_ref.shape[1]
    blocks = token_count // ROWS
    fill = pltpu.make_async_copy(
        w_ref, g_ref.at[:, pl.ds(pl.multiple_of(place.me * rows, rows), rows)], local_sem
    )
    fill.start()
    place.enter()
    fill.wait()
    gather = Gather(place, g_ref, rows, units, (z_send, z_recv, x_send, x_recv))
    summer = TensorSum(place, part, (half_in, half, far_in, total, back), (sum_sends, sum_recvs))

    def gain_copy(step):
        return pltpu.make_async_remote_copy(
            gain_ref,
            gain_in.at[place.me],
            gain_send.at[step],
            gain_recv.at[place.me],
            device_id={"dp": lax.rem(place.me + step, count)},
            device_id_type=MESH,
        )

    def gain_arrival(source):
        return pltpu.make_async_remote_copy(
            gain_ref,
            gain_in.at[source],
            gain_send.at[0],
            gain_recv.at[source],
            device_id={"dp": place.partner},
            device_id_type=MESH,
        )

    lane = lax.broadcasted_iota(jnp.int32, (1, LANES), 1)
    low_half = lane < HEAD_SIZE

    def spread_gains():
        gain_in[place.me] = gain_ref[...]
        for step in range(1, count):
            gain_arrival(lax.rem(place.me + step, count)).wait_recv()
        for source in range(count):
            gains[:, source * rows : (source + 1) * rows] = gain_in[source]

    def norm_block(blk):
        rows_at = pl.ds(pl.multiple_of(blk * ROWS, ROWS), ROWS)
        stream = x_ref[rows_at, :].astype(F32)
        a_ref[rows_at, :] = (normed(stream) * gains[0:1, :]).astype(BF16)

    def load(unit):
        copy = pltpu.make_async_copy(g_ref.at[unit], weights.at[unit], local_sem)
        copy.start()
        copy.wait()

    def project(unit):
        load(unit)

        def block(blk, _):
            rows_at = pl.ds(pl.multiple_of(blk * ROWS, ROWS), ROWS)
            cosine, sine = cos_ref[rows_at, :], sin_ref[rows_at, :]
            out = dot(a_ref[rows_at, :], weights[unit])
            if unit < q_units:
                q_ref[rows_at, unit * UNIT : (unit + 1) * UNIT] = turn(out, cosine, sine).astype(
                    BF16
                )
            else:
                kv = k_ref.shape[1]
                k_ref[rows_at, :] = turn(out[:, :kv], cosine, sine).astype(BF16)
                v_ref[rows_at, :] = out[:, kv:].astype(BF16)
            return 0

        lax.fori_loop(0, blocks, block, 0)

    def attend(blk):
        start, stop = blk * ROWS, (blk + 1) * ROWS
        allowed = mask_ref[start:stop, :stop] > 0
        keys, values = k_ref[:stop, :], v_ref[:stop, :]

        def pair(index, _):
            lanes = pl.ds(pl.multiple_of(index * LANES, LANES), LANES)
            query = q_ref[start:stop, lanes]
            outs = []
            for first in (True, False):
                keep = low_half if first else jnp.logical_not(low_half)
                masked = jnp.where(keep, query, jnp.zeros_like(query))
                probs = probabilities(masked, keys, allowed).astype(BF16)
                outs.append(dot(probs, values))
            att_ref[start:stop, lanes] = jnp.where(low_half, outs[0], outs[1]).astype(BF16)
            return 0

        lax.fori_loop(0, q_ref.shape[1] // LANES, pair, 0)

    def emit(blk):
        first = q_units + 1
        out = None
        for number in range(o_units):
            cols = slice(number * UNIT, (number + 1) * UNIT)
            piece = dot_nt(att_ref[blk * ROWS : (blk + 1) * ROWS, cols], weights[first + number])
            out = piece if out is None else out + piece
        part[blk] = out.astype(BF16)
        summer.begin(blk)

    def finish(blk):
        for row, values in summer.end(blk):
            rows_at = pl.ds(row, ROWS // 2)
            added = values[blk]
            sum_ref[rows_at, :] = added
            stream = x_ref[rows_at, :].astype(F32) + added.astype(F32)
            b_ref[rows_at, :] = (normed(stream) * gains[1:2, :]).astype(BF16)

    ready = gather.latency()
    schedule = []
    for unit in range(q_units + 1):
        schedule.append((ready + unit, functools.partial(project, unit)))
    for unit in range(q_units + 1, q_units + 1 + o_units):
        schedule.append((ready + unit, functools.partial(load, unit)))
    base = ready + q_units + 1
    for blk in range(blocks):
        schedule.append((base + blk, functools.partial(attend, blk)))
        schedule.append((base + o_units + blk, functools.partial(emit, blk)))
        schedule.append((base + o_units + blk + 1, functools.partial(summer.middle, blk)))
        schedule.append((base + o_units + blk + 3, functools.partial(summer.late, blk)))
        schedule.append((base + o_units + blk + 4, functools.partial(finish, blk)))
    schedule.sort(key=lambda item: item[0])
    length = max(units + ready, base + o_units + blocks + 4)

    for step in range(1, count):
        gain_copy(step).start()

    def body(time, _):
        gather.tick(time)
        pl.when(time == 0)(spread_gains)

        @pl.when(time < blocks)
        def _():
            norm_block(time)

        for when, work in schedule:
            pl.when(time == when)(work)
        return 0

    lax.fori_loop(0, length, body, 0)
    for blk in range(blocks):
        summer.drain(blk)
    for step in range(1, count):
        gain_copy(step).wait_send()


def attend(tokens, own, gain_rows, mask, cosine, sine, depth, q_units, o_units):
    token_count, width = tokens.shape
    units, rows, cols = own.shape
    blocks, half = token_count // ROWS, ROWS // 2
    q_width = q_units * UNIT
    kv_width = UNIT // 2
    sum_bufs, sum_sems = TensorSum.scratch(blocks, half, width)
    count = depth * FOLD

    def out(*shape):
        return jax.ShapeDtypeStruct(shape, BF16)

    return pl.pallas_call(
        functools.partial(attend_kernel, (depth, units, q_units, o_units)),
        out_shape=(
            out(units, width, cols),
            out(token_count, width),
            out(token_count, q_width),
            out(token_count, kv_width),
            out(token_count, kv_width),
            out(token_count, q_width),
            out(token_count, width),
            out(token_count, width),
        ),
        in_specs=[VMEM_SPEC] * 6,
        out_specs=[HBM_SPEC] + [VMEM_SPEC] * 7,
        scratch_shapes=[
            VMEM((count, 8, rows), F32),
            VMEM((8, width), F32),
            VMEM((q_units + 1 + o_units, width, cols), BF16),
            VMEM((blocks, ROWS, width), BF16),
            *sum_bufs,
            *sum_sems,
            *Gather.scratch(units, depth),
            DMA((count,)),
            DMA((count,)),
            DMA,
        ],
        compiler_params=pltpu.CompilerParams(
            collective_id=0, has_side_effects=True, vmem_limit_bytes=60 << 20
        ),
        name="attend",
    )(tokens, own, gain_rows, mask, cosine, sine)


class Scatter:
    SLOTS = 4

    def __init__(self, place, rows, units, refs, first=0):
        self.place, self.rows, self.units, self.first = place, rows, units, first
        (
            self.grads,
            self.x_in,
            self.z_in,
            self.kept,
            self.mine,
            self.theirs,
            self.summed,
            self.x_send,
            self.x_recv,
            self.z_send,
            self.z_recv,
            self.load_sem,
            self.keep_sem,
        ) = refs

    @staticmethod
    def scratch(units, depth, rows):
        return [
            VMEM((depth, rows, UNIT), BF16),
            VMEM((depth, rows, UNIT), BF16),
            VMEM((Scatter.SLOTS, depth, rows, UNIT), BF16),
            DMA((units, depth)),
            DMA((units, depth)),
            DMA((units, depth)),
            DMA((units, depth)),
            DMA((2, depth)),
            DMA((Scatter.SLOTS,)),
        ]

    @staticmethod
    def outputs(units, depth, rows):
        return (
            jax.ShapeDtypeStruct((units, depth, rows, UNIT), BF16),
            jax.ShapeDtypeStruct((units, depth, rows, UNIT), BF16),
            jax.ShapeDtypeStruct((units, rows, UNIT), BF16),
        )

    def block(self, unit, index):
        start = pl.multiple_of(index * self.rows, self.rows)
        return self.grads.at[unit + self.first, pl.ds(start, self.rows)]

    def over(self, unit, zz):
        p = self.place
        return pltpu.make_async_remote_copy(
            self.block(unit, zz * FOLD + 1 - p.x),
            self.x_in.at[unit, zz],
            self.x_send.at[unit, zz],
            self.x_recv.at[unit, zz],
            device_id={"dp": p.partner},
            device_id_type=MESH,
        )

    def along(self, unit, step):
        p = self.place
        dest = lax.rem(p.z + step, p.depth)
        slot = lax.rem(unit, self.SLOTS)
        return pltpu.make_async_remote_copy(
            self.summed.at[slot, dest],
            self.z_in.at[unit, step],
            self.z_send.at[unit, step],
            self.z_recv.at[unit, step],
            device_id={"dp": dest * FOLD + p.x},
            device_id_type=MESH,
        )

    def keep(self, unit):
        slot = lax.rem(unit, self.SLOTS)
        return pltpu.make_async_copy(
            self.summed.at[slot, self.place.z], self.kept.at[unit], self.keep_sem.at[slot]
        )

    def stage(self, step, unit):
        p = self.place

        @pl.when((unit >= 0) & (unit < self.units))
        def _():
            if step == 0:
                for zz in range(p.depth):
                    self.over(unit, zz).start()
            elif step == 1:
                loads = []
                for zz in range(p.depth):
                    loads.append(
                        pltpu.make_async_copy(
                            self.block(unit, zz * FOLD + p.x),
                            self.mine.at[zz],
                            self.load_sem.at[0, zz],
                        )
                    )
                    loads[-1].start()
                for zz in range(p.depth):
                    self.over(unit, zz).wait_recv()
                    loads.append(
                        pltpu.make_async_copy(
                            self.x_in.at[unit, zz], self.theirs.at[zz], self.load_sem.at[1, zz]
                        )
                    )
                    loads[-1].start()
                for copy in loads:
                    copy.wait()
                slot = lax.rem(unit, self.SLOTS)
                for zz in range(p.depth):
                    self.summed[slot, zz] = (
                        self.mine[zz].astype(F32) + self.theirs[zz].astype(F32)
                    ).astype(BF16)
                for way in range(1, p.depth):
                    self.along(unit, way).start()
                self.keep(unit).start()
            else:
                for zz in range(p.depth):
                    self.over(unit, zz).wait_send()
                for way in range(1, p.depth):
                    self.along(unit, way).wait_send()
                self.keep(unit).wait()

    def tick(self, time):
        self.stage(2, time - 1 - (self.SLOTS - 1))
        self.stage(0, time)
        self.stage(1, time - 1)

    def latency(self):
        return 1 + self.SLOTS

    def finish(self):
        def unit_end(unit, _):
            for way in range(1, self.place.depth):
                self.along(unit, way).wait_recv()
            return 0

        lax.fori_loop(0, self.units, unit_end, 0)


def feed_kernel(cfg, *refs):
    (
        b_ref,
        cot_ref,
        g_ref,
        grads_ref,
        x_in,
        z_in,
        kept,
        out_ref,
        db_ref,
        acc_out,
        acc_db,
        weights,
        grad_buf,
        hidden,
        dgu,
        part,
        half_in,
        half,
        far_in,
        total,
        back,
        sum_sends,
        sum_recvs,
        weight_sem,
        grad_sem,
        local_sem,
        *scatter_refs,
    ) = refs
    depth, first_unit, chunks, pace, scatter_units = cfg
    place = Place(depth)
    token_count, width = b_ref.shape
    rows = x_in.shape[2]
    blocks = token_count // ROWS
    tall = 2 * ROWS
    scatter = Scatter(place, rows, scatter_units, (grads_ref, x_in, z_in, kept, *scatter_refs))
    summer = TensorSum(place, part, (half_in, half, far_in, total, back), (sum_sends, sum_recvs))

    def load(chunk, matrix):
        slot = lax.rem(chunk, 2)
        return pltpu.make_async_copy(
            g_ref.at[first_unit + 3 * chunk + matrix],
            weights.at[slot, matrix],
            weight_sem.at[slot, matrix],
        )

    def save(chunk, matrix):
        slot = lax.rem(chunk, 2)
        return pltpu.make_async_copy(
            grad_buf.at[slot, matrix],
            grads_ref.at[3 * chunk + matrix],
            grad_sem.at[slot, matrix],
        )

    for matrix in range(3):
        load(0, matrix).start()
    place.enter()

    def clear(blk, _):
        rows_at = pl.ds(pl.multiple_of(blk * ROWS, ROWS), ROWS)
        acc_out[rows_at, :] = jnp.zeros((ROWS, width), F32)
        acc_db[rows_at, :] = jnp.zeros((ROWS, width), F32)
        return 0

    lax.fori_loop(0, blocks, clear, 0)

    def compute(chunk, slot):
        def hidden_rows(blk, _):
            rows_at = pl.ds(pl.multiple_of(blk * tall, tall), tall)
            stream, cot = b_ref[rows_at, :], cot_ref[rows_at, :]
            gate = dot(stream, weights[slot, 0])
            upper = dot(stream, weights[slot, 1])
            grad_hidden = dot(cot, weights[slot, 2])
            sigmoid = jax.nn.sigmoid(gate)
            silu = gate * sigmoid
            hid = (silu * upper).astype(BF16)
            grad_gate = (grad_hidden * upper * sigmoid * (1.0 + gate * (1.0 - sigmoid))).astype(
                BF16
            )
            grad_up = (grad_hidden * silu).astype(BF16)
            hidden[rows_at, :] = hid
            dgu[rows_at, :UNIT] = grad_gate
            dgu[rows_at, UNIT:] = grad_up

            def spread(piece, _):
                cols = pl.ds(pl.multiple_of(piece * tall, tall), tall)
                acc_out[rows_at, cols] += dot_nt(hidden[rows_at, :], weights[slot, 2, cols, :])
                acc_db[rows_at, cols] += dot_nt(
                    dgu[rows_at, :UNIT], weights[slot, 0, cols, :]
                ) + dot_nt(dgu[rows_at, UNIT:], weights[slot, 1, cols, :])
                return 0

            lax.fori_loop(0, width // tall, spread, 0)
            return 0

        lax.fori_loop(0, token_count // tall, hidden_rows, 0)

        def grad_rows(blk, _):
            cols = pl.ds(pl.multiple_of(blk * ROWS, ROWS), ROWS)
            both = dot_tn(b_ref[:, cols], dgu[...])
            grad_buf[slot, 0, cols, :] = both[:, :UNIT].astype(BF16)
            grad_buf[slot, 1, cols, :] = both[:, UNIT:].astype(BF16)
            grad_buf[slot, 2, cols, :] = dot_tn(cot_ref[:, cols], hidden[...]).astype(BF16)
            return 0

        lax.fori_loop(0, width // ROWS, grad_rows, 0)

    def step(chunk, _):
        slot = lax.rem(chunk, 2)
        for matrix in range(3):
            load(chunk, matrix).wait()

        @pl.when(chunk + 1 < chunks)
        def _():
            for matrix in range(3):
                load(chunk + 1, matrix).start()

        compute(chunk, slot)
        for matrix in range(3):
            save(chunk, matrix).start()
        for matrix in range(3):
            save(chunk, matrix).wait()
        for number in range(pace):
            scatter.tick(chunk * pace + number)
        return 0

    lax.fori_loop(0, chunks, step, 0)
    time = chunks * pace
    length = scatter_units + scatter.latency()
    for blk in range(blocks):
        rows_at = slice(blk * ROWS, (blk + 1) * ROWS)
        part[blk] = acc_out[rows_at, :].astype(BF16)
        copy = pltpu.make_async_copy(part.at[blk], out_ref.at[pl.ds(blk * ROWS, ROWS)], local_sem)
        copy.start()
        copy.wait()
        part[blk] = acc_db[rows_at, :].astype(BF16)
        summer.begin(blk)
    schedule = []
    for blk in range(blocks):
        schedule.append((blk, functools.partial(summer.middle, blk)))
        schedule.append((blk + 2, functools.partial(summer.late, blk)))

        def finish(blk=blk):
            copies = []
            for (row, values), sem in zip(summer.end(blk), (0, 1)):
                copies.append(
                    pltpu.make_async_copy(
                        values.at[blk], db_ref.at[pl.ds(row, ROWS // 2)], grad_sem.at[sem, 0]
                    )
                )
                copies[-1].start()
            for copy in copies:
                copy.wait()

        schedule.append((blk + 3, finish))
    schedule.sort(key=lambda item: item[0])

    def tail(now, _):
        scatter.tick(time + now)
        for when, work in schedule:
            pl.when(now == when)(work)
        return 0

    lax.fori_loop(0, max(length - time, blocks + 3), tail, 0)
    scatter.finish()
    for blk in range(blocks):
        summer.drain(blk)


def feed(b, cotangent, gathered, depth, first_unit, chunks, pace, scatter_units):
    token_count, width = b.shape
    rows = width // (depth * FOLD)
    blocks, half = token_count // ROWS, ROWS // 2
    sum_bufs, sum_sems = TensorSum.scratch(blocks, half, width)
    full = jax.ShapeDtypeStruct((token_count, width), BF16)
    return pl.pallas_call(
        functools.partial(feed_kernel, (depth, first_unit, chunks, pace, scatter_units)),
        out_shape=(
            jax.ShapeDtypeStruct((3 * chunks, width, UNIT), BF16),
            *Scatter.outputs(scatter_units, depth, rows),
            full,
            full,
        ),
        in_specs=[VMEM_SPEC, VMEM_SPEC, HBM_SPEC],
        out_specs=[HBM_SPEC] * 6,
        scratch_shapes=[
            VMEM((token_count, width), F32),
            VMEM((token_count, width), F32),
            VMEM((2, 3, width, UNIT), BF16),
            VMEM((2, 3, width, UNIT), BF16),
            VMEM((token_count, UNIT), BF16),
            VMEM((token_count, 2 * UNIT), BF16),
            VMEM((blocks, ROWS, width), BF16),
            *sum_bufs,
            *sum_sems,
            DMA((2, 3)),
            DMA((2, 3)),
            DMA,
            *Scatter.scratch(scatter_units, depth, rows),
        ],
        compiler_params=pltpu.CompilerParams(
            collective_id=1, has_side_effects=True, vmem_limit_bytes=63 << 20
        ),
        name="feed",
    )(b, cotangent, gathered)


def tensor_sum(partial):
    rows = partial.shape[0] // 2
    core = lax.axis_index("tensor") % 2
    count = lax.axis_size("tensor")
    flip_core = [(i, i ^ 1) for i in range(count)]
    flip_y = [(i, i ^ 2) for i in range(count)]
    mine = lax.dynamic_slice_in_dim(partial, core * rows, rows, axis=0)
    other = lax.dynamic_slice_in_dim(partial, (1 - core) * rows, rows, axis=0)
    received = lax.ppermute(other, "tensor", flip_core)
    chip = (mine.astype(F32) + received.astype(F32)).astype(BF16)
    across = lax.ppermute(chip, "tensor", flip_y)
    total = (chip.astype(F32) + across.astype(F32)).astype(BF16)
    back = lax.ppermute(total, "tensor", flip_core)
    return jnp.where(
        core == 0,
        jnp.concatenate([total, back], axis=0),
        jnp.concatenate([back, total], axis=0),
    )


def norm_parts(stream):
    inverse = lax.rsqrt(jnp.mean(stream * stream, axis=-1, keepdims=True) + EPS_NORM)
    return (stream * inverse, inverse)


def norm_back(grad_normed, gain, normalized_input, inverse):
    scaled = grad_normed * gain[None, :]
    return inverse * (
        scaled - normalized_input * jnp.mean(scaled * normalized_input, axis=-1, keepdims=True)
    )


def rotate_back(value_vectors, cosine, sine):
    half = value_vectors.shape[-1] // 2
    first = value_vectors[..., :half]
    second = value_vectors[..., half:]
    return jnp.concatenate(
        [first * cosine + second * sine, second * cosine - first * sine], axis=-1
    )


def attention_backward(query_vectors, key_vectors, value_vectors, grad_out, allowed):
    token_positions = query_vectors.shape[0]
    rows = 512
    grad_queries = []
    grad_keys = jnp.zeros(key_vectors.shape, F32)
    grad_values = jnp.zeros(value_vectors.shape, F32)
    for begin_row in range(0, token_positions, rows):
        query_block = query_vectors[begin_row : begin_row + rows]
        grad_block = grad_out[begin_row : begin_row + rows]
        scores = jnp.einsum(
            "qkgd,skd->kgqs", query_block, key_vectors, preferred_element_type=F32
        ) * HEAD_SIZE ** (-0.5)
        scores = jnp.where(allowed[begin_row : begin_row + rows][None, None], scores, NEG_FILL)
        probs = jax.nn.softmax(scores, axis=-1)
        grad_probs = jnp.einsum(
            "qkgd,skd->kgqs", grad_block, value_vectors, preferred_element_type=F32
        )
        centre = jnp.sum(probs * grad_probs, axis=-1, keepdims=True)
        grad_scores = (probs * (grad_probs - centre)).astype(BF16)
        grad_queries.append(
            jnp.einsum("kgqs,skd->qkgd", grad_scores, key_vectors, preferred_element_type=F32)
            * HEAD_SIZE ** (-0.5)
        )
        grad_keys = grad_keys + jnp.einsum(
            "kgqs,qkgd->skd", grad_scores, query_block, preferred_element_type=F32
        ) * HEAD_SIZE ** (-0.5)
        grad_values = grad_values + jnp.einsum(
            "kgqs,qkgd->skd", probs.astype(BF16), grad_block, preferred_element_type=F32
        )
    return (jnp.concatenate(grad_queries, axis=0), grad_keys, grad_values)


def gathered_units(mine, arrived):
    total = mine.astype(F32)
    for step in range(1, arrived.shape[1]):
        total = total + arrived[:, step].astype(F32)
    return total


def shards(
    depth,
    tokens,
    attention_gain,
    query_matrix,
    key_matrix,
    value_matrix,
    output_weight,
    feed_gain,
    gate_weight,
    up_weight,
    down_weight,
    sequence_lengths,
    block_mask,
    cotangent,
):
    token_count, width = tokens.shape
    rows, q_width = query_matrix.shape
    kv_width = key_matrix.shape[1]
    heads_kv = kv_width // HEAD_SIZE
    groups = q_width // kv_width
    feed_width = gate_weight.shape[1]
    chunks = feed_width // UNIT
    q_units = q_width // UNIT

    def pair(cols):
        return cols.reshape(-1, heads_kv, groups, HEAD_SIZE).swapaxes(1, 2).reshape(-1, q_width)

    def unpair(cols):
        return cols.reshape(-1, groups, heads_kv, HEAD_SIZE).swapaxes(1, 2).reshape(-1, q_width)

    def split(cols):
        return cols.reshape(rows, -1, UNIT).swapaxes(0, 1)

    feed_units = jnp.stack(
        [split(gate_weight), split(up_weight), split(down_weight.T)], axis=1
    ).reshape(3 * chunks, rows, UNIT)
    own = jnp.concatenate(
        [
            split(pair(query_matrix)),
            split(jnp.concatenate([key_matrix, value_matrix], axis=1)),
            split(pair(output_weight.T)),
            feed_units,
        ],
        axis=0,
    )
    sequence, position, valid = token_layout(sequence_lengths[0], token_count, BLOCK)
    allowed = allowed_pairs(sequence, position, valid, block_mask, BLOCK)
    cosine, sine = rope_tables(position, HEAD_SIZE)
    wide_cos = jnp.concatenate([cosine] * 4, axis=1)
    wide_sin = jnp.concatenate([-sine, sine] * 2, axis=1)
    gain_rows = jnp.concatenate(
        [
            attention_gain.astype(F32)[None],
            feed_gain.astype(F32)[None],
            jnp.zeros((6, rows), F32),
        ],
        axis=0,
    )
    first_unit = 2 * q_units + 1
    gathered, a, q, k, v, att, att_sum, b = attend(
        tokens, own, gain_rows, allowed.astype(F32), wide_cos, wide_sin, depth, q_units, q_units
    )
    grads, _, z_in, kept, out_part, db = feed(
        b, cotangent, gathered, depth, first_unit, chunks, PACE, 3 * chunks
    )
    stream = tokens.astype(F32)
    middle = stream + att_sum.astype(F32)
    block_output = (middle + tensor_sum(out_part).astype(F32)).astype(BF16)
    gain_one = lax.all_gather(attention_gain, "dp", axis=0, tiled=True).astype(F32)
    gain_two = lax.all_gather(feed_gain, "dp", axis=0, tiled=True).astype(F32)
    normed_two, inverse_two = norm_parts(middle)
    grad_normed_two = db.astype(F32)
    feed_gain_full = jnp.sum(grad_normed_two * normed_two, axis=0)
    grad_middle = cotangent.astype(F32) + norm_back(
        grad_normed_two, gain_two, normed_two, inverse_two
    )
    grad_middle_low = grad_middle.astype(BF16)
    out_t = jnp.concatenate([gathered[q_units + 1 + i] for i in range(q_units)], axis=1)
    query_full = jnp.concatenate([gathered[i] for i in range(q_units)], axis=1)
    kv_full = gathered[q_units]
    output_grad = dot_tn(att, grad_middle_low)
    grad_attended = dot(grad_middle_low, out_t).astype(BF16)

    def heads(cols):
        return unpair(cols).reshape(token_count, heads_kv, groups, HEAD_SIZE)

    grad_q, grad_k, grad_v = attention_backward(
        heads(q),
        k.reshape(token_count, heads_kv, HEAD_SIZE),
        v.reshape(token_count, heads_kv, HEAD_SIZE),
        heads(grad_attended),
        allowed,
    )
    grad_q = pair(
        rotate_back(grad_q, cosine[:, None, None, :], sine[:, None, None, :])
        .astype(BF16)
        .reshape(token_count, q_width)
    )
    grad_k = (
        rotate_back(grad_k, cosine[:, None, :], sine[:, None, :])
        .astype(BF16)
        .reshape(token_count, kv_width)
    )
    grad_v = grad_v.astype(BF16).reshape(token_count, kv_width)
    grad_kv = jnp.concatenate([grad_k, grad_v], axis=1)
    query_grad = dot_tn(a, grad_q)
    kv_grad = dot_tn(a, grad_kv)
    da = dot_nt(grad_q, query_full) + dot_nt(grad_kv, kv_full)
    da = tensor_sum(da.astype(BF16)).astype(F32)
    normed_one, inverse_one = norm_parts(stream)
    attention_gain_full = jnp.sum(da * normed_one, axis=0)
    input_grad = grad_middle + norm_back(da, gain_one, normed_one, inverse_one)
    packed = jnp.concatenate([query_grad, kv_grad], axis=1).astype(BF16)
    packed = lax.psum_scatter(packed, "dp", scatter_dimension=0, tiled=True).astype(F32)
    out_grad = lax.psum_scatter(
        output_grad.astype(BF16), "dp", scatter_dimension=1, tiled=True
    ).astype(F32)
    gain_grads = lax.psum_scatter(
        jnp.stack([attention_gain_full, feed_gain_full]).astype(F32),
        "dp",
        scatter_dimension=1,
        tiled=True,
    )
    feed_grads = gathered_units(kept, z_in).reshape(chunks, 3, rows, UNIT)

    def join(which):
        return feed_grads[:, which].swapaxes(0, 1).reshape(rows, feed_width)

    out_grad = out_grad.reshape(groups, heads_kv, HEAD_SIZE, rows).swapaxes(0, 1)
    return (
        block_output,
        input_grad,
        gain_grads[0],
        unpair(packed[:, :q_width]),
        packed[:, q_width : q_width + kv_width],
        packed[:, q_width + kv_width :],
        out_grad.reshape(q_width, rows),
        gain_grads[1],
        join(0),
        join(1),
        join(2).T,
    )


PACE = 3


def solution(mesh):
    in_specs = (
        P("dp", None),
        P("dp"),
        P("dp", "tensor"),
        P("dp", "tensor"),
        P("dp", "tensor"),
        P("tensor", "dp"),
        P("dp"),
        P("dp", "tensor"),
        P("dp", "tensor"),
        P("tensor", "dp"),
        P("dp", None),
        P("dp", None),
        P("dp", None),
    )
    out_specs = (
        P("dp", None),
        P("dp", None),
        P("dp"),
        P("dp", "tensor"),
        P("dp", "tensor"),
        P("dp", "tensor"),
        P("tensor", "dp"),
        P("dp"),
        P("dp", "tensor"),
        P("dp", "tensor"),
        P("tensor", "dp"),
    )
    return jax.shard_map(
        functools.partial(shards, mesh.shape["dp"] // FOLD),
        mesh=mesh,
        in_specs=in_specs,
        out_specs=out_specs,
        check_vma=False,
    )
```

```python
import functools

import jax
import jax.numpy as jnp
from jax import lax
from jax.experimental import pallas as pl
from jax.experimental.pallas import tpu as pltpu
from jax.sharding import PartitionSpec as P

HEAD_SIZE = 64
BLOCK = 128
LANES = 128
EPS_NORM = 1e-05
THETA_BASE = 500000.0
NEG_FILL = -1e30
UNIT = 256
ROWS = 256
FOLD = 2
XFIRST = 6
MESH = pl.DeviceIdType.MESH
VMEM = pltpu.VMEM
DMA = pltpu.SemaphoreType.DMA
HBM_SPEC = pl.BlockSpec(memory_space=pl.ANY)
VMEM_SPEC = pl.BlockSpec(memory_space=pltpu.VMEM)
F32 = jnp.float32
BF16 = jnp.bfloat16


def token_layout(lengths_row, total, block):
    blocks_per = (lengths_row + block - 1) // block
    offsets = jnp.cumsum(blocks_per) - blocks_per
    first_token = offsets * block
    indices = jnp.arange(total, dtype=jnp.int32)
    member = (indices[:, None] >= first_token[None, :]) & (blocks_per[None, :] > 0)
    sequence = jnp.sum(member.astype(jnp.int32), axis=1) - 1
    select = sequence[:, None] == jnp.arange(lengths_row.shape[0], dtype=jnp.int32)[None, :]
    begins = jnp.sum(jnp.where(select, first_token[None, :], 0), axis=1)
    limits = jnp.sum(jnp.where(select, lengths_row[None, :], 0), axis=1)
    position = indices - begins
    return (sequence, position, position < limits)


def allowed_pairs(sequence, position, valid, mask_blocks, block):
    total = sequence.shape[0]
    blocks = total // block
    tiled = jnp.broadcast_to(
        mask_blocks[:, None, :, None] > 0, (blocks, block, blocks, block)
    ).reshape(total, total)
    same = sequence[:, None] == sequence[None, :]
    causal = position[None, :] <= position[:, None]
    row = jnp.arange(total, dtype=jnp.int32)
    diagonal = row[:, None] == row[None, :]
    return tiled & same & causal & valid[None, :] | diagonal


def rope_tables(position, head_dim):
    freqs = THETA_BASE ** (-jnp.arange(head_dim // 2, dtype=F32) * 2.0 / head_dim)
    angles = position.astype(F32)[:, None] * freqs[None, :]
    return (jnp.cos(angles), jnp.sin(angles))


def dot(left, right):
    return jnp.dot(left, right, preferred_element_type=F32)


def dot_nt(left, right):
    return lax.dot_general(left, right, (((1,), (1,)), ((), ())), preferred_element_type=F32)


def dot_tn(left, right):
    return lax.dot_general(left, right, (((0,), (0,)), ((), ())), preferred_element_type=F32)


class Place:
    def __init__(self, depth):
        self.depth = depth
        self.me = lax.axis_index("dp")
        self.z = self.me // FOLD
        self.x = self.me % FOLD
        self.right = self.me + FOLD
        self.left = self.me - FOLD
        self.partner = self.z * FOLD + (1 - self.x)
        member = lax.axis_index("tensor")
        self.core = member % 2
        row = member // 2
        self.other = row * 2 + (1 - self.core)
        self.across = (1 - row) * 2 + self.core

    def enter(self):
        count = self.depth * FOLD
        barrier = pltpu.get_barrier_semaphore()
        for step in range(1, count):
            pl.semaphore_signal(
                barrier,
                1,
                device_id={"dp": lax.rem(self.me + step, count)},
                device_id_type=MESH,
            )
        for peer in (self.other, self.across):
            pl.semaphore_signal(barrier, 1, device_id={"tensor": peer}, device_id_type=MESH)
        pl.semaphore_wait(barrier, count + 1)


class Gather:
    def __init__(self, place, g_ref, rows, units, sems, first=0):
        self.place, self.g, self.rows, self.units, self.first = place, g_ref, rows, units, first
        self.z_send, self.z_recv, self.x_send, self.x_recv = sems

    @staticmethod
    def scratch(units, depth):
        return [
            DMA((units, 2, depth)),
            DMA((units, depth)),
            DMA((units, depth)),
            DMA((units, depth)),
        ]

    def block(self, unit, index, count=1):
        start = pl.multiple_of(index * self.rows, self.rows)
        return self.g.at[unit, pl.ds(start, count * self.rows)]

    def along(self, unit, zz, way, wide):
        p = self.place
        if wide:
            ref = self.block(unit, zz * FOLD, FOLD)
        else:
            ref = self.block(unit, zz * FOLD + p.x)
        return pltpu.make_async_remote_copy(
            ref,
            ref,
            self.z_send.at[unit, way, zz],
            self.z_recv.at[unit, zz],
            device_id={"dp": p.left if way else p.right},
            device_id_type=MESH,
        )

    def over(self, unit, zz, incoming=False):
        p = self.place
        ref = self.block(unit, zz * FOLD + (1 - p.x if incoming else p.x))
        return pltpu.make_async_remote_copy(
            ref,
            ref,
            self.x_send.at[unit, zz],
            self.x_recv.at[unit, zz],
            device_id={"dp": p.partner},
            device_id_type=MESH,
        )

    def send_both(self, unit, zz, wide):
        p, last = self.place, self.place.depth - 1

        @pl.when(p.z < last)
        def _():
            self.along(unit, zz, 0, wide).start()

        @pl.when(p.z > 0)
        def _():
            self.along(unit, zz, 1, wide).start()

    def forward(self, unit, step, wide, across):
        p, last = self.place, self.place.depth - 1

        @pl.when(p.z >= step)
        def _():
            zz = p.z - step
            self.along(unit, zz, 0, wide).wait_recv()

            @pl.when(p.z < last)
            def _():
                self.along(unit, zz, 0, wide).start()

            if across:
                self.over(unit, zz).start()

        @pl.when(p.z + step <= last)
        def _():
            zz = p.z + step
            self.along(unit, zz, 1, wide).wait_recv()

            @pl.when(p.z > 0)
            def _():
                self.along(unit, zz, 1, wide).start()

            if across:
                self.over(unit, zz).start()

    def drain(self, unit, wide):
        p, last = self.place, self.place.depth - 1
        for zz in range(p.depth):

            @pl.when((p.z >= zz) & (p.z < last))
            def _():
                self.along(unit, zz, 0, wide).wait_send()

            @pl.when((p.z <= zz) & (p.z > 0))
            def _():
                self.along(unit, zz, 1, wide).wait_send()

    def stage(self, step, unit):
        p, depth = self.place, self.place.depth

        def slow_first():
            if step == 0:
                self.send_both(unit, p.z, False)
                self.over(unit, p.z).start()
            elif step < depth:
                self.forward(unit, step, False, True)
            else:
                for zz in range(depth):
                    self.over(unit, zz, True).wait_recv()
                for zz in range(depth):
                    self.over(unit, zz).wait_send()
                self.drain(unit, False)

        def fast_first():
            if step == 0:
                self.over(unit, p.z).start()
            elif step == 1:
                self.over(unit, p.z, True).wait_recv()
                self.send_both(unit, p.z, True)
            else:
                self.forward(unit, step - 1, True, False)
                if step == depth:
                    self.over(unit, p.z).wait_send()
                    self.drain(unit, True)

        inside = (unit >= 0) & (unit < self.units)
        fast = lax.rem(unit + self.first, XFIRST) == XFIRST - 1
        pl.when(inside & jnp.logical_not(fast))(slow_first)
        pl.when(inside & fast)(fast_first)

    def latency(self):
        return self.place.depth + 1

    def tick(self, time):
        depth = self.place.depth
        for step in range(depth):
            self.stage(step, time - step)
        self.stage(depth, time - depth - 1)


class TensorSum:
    def __init__(self, place, part, bufs, sems):
        self.place, self.part = place, part
        self.half_in, self.half, self.far_in, self.total, self.back = bufs
        self.sends, self.recvs = sems

    @staticmethod
    def scratch(blocks, half, width):
        return [VMEM((blocks, half, width), BF16)] * 5, [DMA((3, blocks)), DMA((3, blocks))]

    def copy(self, step, src, dst, blk):
        p = self.place
        return pltpu.make_async_remote_copy(
            src,
            dst.at[blk],
            self.sends.at[step, blk],
            self.recvs.at[step, blk],
            device_id={"tensor": p.across if step == 1 else p.other},
            device_id_type=MESH,
        )

    def first(self, blk):
        half = self.half.shape[1]
        start = pl.multiple_of((1 - self.place.core) * half, half)
        return self.copy(0, self.part.at[blk, pl.ds(start, half)], self.half_in, blk)

    def second(self, blk):
        return self.copy(1, self.half.at[blk], self.far_in, blk)

    def third(self, blk):
        return self.copy(2, self.total.at[blk], self.back, blk)

    def begin(self, blk):
        self.first(blk).start()

    def middle(self, blk):
        half = self.half.shape[1]
        self.first(blk).wait_recv()
        start = pl.multiple_of(self.place.core * half, half)
        mine = self.part[blk, pl.ds(start, half), :].astype(F32)
        self.half[blk] = (mine + self.half_in[blk].astype(F32)).astype(BF16)
        self.second(blk).start()

    def late(self, blk):
        self.second(blk).wait_recv()
        self.total[blk] = (self.half[blk].astype(F32) + self.far_in[blk].astype(F32)).astype(BF16)
        self.third(blk).start()

    def end(self, blk):
        half = self.half.shape[1]
        self.third(blk).wait_recv()
        core = self.place.core
        return (
            (pl.multiple_of(blk * 2 * half + core * half, half), self.total),
            (pl.multiple_of(blk * 2 * half + (1 - core) * half, half), self.back),
        )

    def drain(self, blk):
        self.first(blk).wait_send()
        self.second(blk).wait_send()
        self.third(blk).wait_send()


def turn(values, cosine, sine, back=False):
    half = HEAD_SIZE // 2
    lane = lax.broadcasted_iota(jnp.int32, (1, LANES), 1)
    low = lax.rem(lane, HEAD_SIZE) < half
    tiles = []
    for start in range(0, values.shape[1], LANES):
        tile = values[:, start : start + LANES]
        swapped = jnp.where(low, pltpu.roll(tile, LANES - half, 1), pltpu.roll(tile, half, 1))
        if back:
            tiles.append(tile * cosine - swapped * sine)
        else:
            tiles.append(tile * cosine + swapped * sine)
    return tiles[0] if len(tiles) == 1 else jnp.concatenate(tiles, axis=1)


def probabilities(query, keys, allowed):
    scores = dot_nt(query, keys) * HEAD_SIZE ** (-0.5)
    scores = jnp.where(allowed, scores, NEG_FILL)
    expo = jnp.exp(scores - jnp.max(scores, axis=-1, keepdims=True))
    return expo / jnp.sum(expo, axis=-1, keepdims=True)


def normed(stream):
    return stream * lax.rsqrt(jnp.mean(stream * stream, axis=-1, keepdims=True) + EPS_NORM)


def attend_kernel(cfg, *refs):
    (
        x_ref,
        w_ref,
        gain_ref,
        mask_ref,
        cos_ref,
        sin_ref,
        g_ref,
        a_ref,
        q_ref,
        k_ref,
        v_ref,
        att_ref,
        sum_ref,
        b_ref,
        gains,
        gain_in,
        weights,
        part,
        half_in,
        half,
        far_in,
        total,
        back,
        sum_sends,
        sum_recvs,
        z_send,
        z_recv,
        x_send,
        x_recv,
        gain_send,
        gain_recv,
        local_sem,
    ) = refs
    depth, units, q_units, o_units = cfg
    place = Place(depth)
    count = depth * FOLD
    token_count, width = x_ref.shape
    rows = w_ref.shape[1]
    blocks = token_count // ROWS
    fill = pltpu.make_async_copy(
        w_ref, g_ref.at[:, pl.ds(pl.multiple_of(place.me * rows, rows), rows)], local_sem
    )
    fill.start()
    place.enter()
    fill.wait()
    gather = Gather(place, g_ref, rows, units, (z_send, z_recv, x_send, x_recv))
    summer = TensorSum(place, part, (half_in, half, far_in, total, back), (sum_sends, sum_recvs))

    def gain_copy(step):
        return pltpu.make_async_remote_copy(
            gain_ref,
            gain_in.at[place.me],
            gain_send.at[step],
            gain_recv.at[place.me],
            device_id={"dp": lax.rem(place.me + step, count)},
            device_id_type=MESH,
        )

    def gain_arrival(source):
        return pltpu.make_async_remote_copy(
            gain_ref,
            gain_in.at[source],
            gain_send.at[0],
            gain_recv.at[source],
            device_id={"dp": place.partner},
            device_id_type=MESH,
        )

    lane = lax.broadcasted_iota(jnp.int32, (1, LANES), 1)
    low_half = lane < HEAD_SIZE

    def spread_gains():
        gain_in[place.me] = gain_ref[...]
        for step in range(1, count):
            gain_arrival(lax.rem(place.me + step, count)).wait_recv()
        for source in range(count):
            gains[:, source * rows : (source + 1) * rows] = gain_in[source]

    def norm_block(blk):
        rows_at = pl.ds(pl.multiple_of(blk * ROWS, ROWS), ROWS)
        stream = x_ref[rows_at, :].astype(F32)
        a_ref[rows_at, :] = (normed(stream) * gains[0:1, :]).astype(BF16)

    def load(unit):
        copy = pltpu.make_async_copy(g_ref.at[unit], weights.at[unit], local_sem)
        copy.start()
        copy.wait()

    def project(unit):
        load(unit)

        def block(blk, _):
            rows_at = pl.ds(pl.multiple_of(blk * ROWS, ROWS), ROWS)
            cosine, sine = cos_ref[rows_at, :], sin_ref[rows_at, :]
            out = dot(a_ref[rows_at, :], weights[unit])
            if unit < q_units:
                q_ref[rows_at, unit * UNIT : (unit + 1) * UNIT] = turn(out, cosine, sine).astype(
                    BF16
                )
            else:
                kv = k_ref.shape[1]
                k_ref[rows_at, :] = turn(out[:, :kv], cosine, sine).astype(BF16)
                v_ref[rows_at, :] = out[:, kv:].astype(BF16)
            return 0

        lax.fori_loop(0, blocks, block, 0)

    def attend(blk):
        start, stop = blk * ROWS, (blk + 1) * ROWS
        allowed = mask_ref[start:stop, :stop] > 0
        keys, values = k_ref[:stop, :], v_ref[:stop, :]

        def pair(index, _):
            lanes = pl.ds(pl.multiple_of(index * LANES, LANES), LANES)
            query = q_ref[start:stop, lanes]
            outs = []
            for first in (True, False):
                keep = low_half if first else jnp.logical_not(low_half)
                masked = jnp.where(keep, query, jnp.zeros_like(query))
                probs = probabilities(masked, keys, allowed).astype(BF16)
                outs.append(dot(probs, values))
            att_ref[start:stop, lanes] = jnp.where(low_half, outs[0], outs[1]).astype(BF16)
            return 0

        lax.fori_loop(0, q_ref.shape[1] // LANES, pair, 0)

    def emit(blk):
        first = q_units + 1
        out = None
        for number in range(o_units):
            cols = slice(number * UNIT, (number + 1) * UNIT)
            piece = dot_nt(att_ref[blk * ROWS : (blk + 1) * ROWS, cols], weights[first + number])
            out = piece if out is None else out + piece
        part[blk] = out.astype(BF16)
        summer.begin(blk)

    def finish(blk):
        for row, values in summer.end(blk):
            rows_at = pl.ds(row, ROWS // 2)
            added = values[blk]
            sum_ref[rows_at, :] = added
            stream = x_ref[rows_at, :].astype(F32) + added.astype(F32)
            b_ref[rows_at, :] = (normed(stream) * gains[1:2, :]).astype(BF16)

    ready = gather.latency()
    schedule = []
    for unit in range(q_units + 1):
        schedule.append((ready + unit, functools.partial(project, unit)))
    for unit in range(q_units + 1, q_units + 1 + o_units):
        schedule.append((ready + unit, functools.partial(load, unit)))
    base = ready + q_units + 1
    for blk in range(blocks):
        schedule.append((base + blk, functools.partial(attend, blk)))
        schedule.append((base + o_units + blk, functools.partial(emit, blk)))
        schedule.append((base + o_units + blk + 1, functools.partial(summer.middle, blk)))
        schedule.append((base + o_units + blk + 3, functools.partial(summer.late, blk)))
        schedule.append((base + o_units + blk + 4, functools.partial(finish, blk)))
    schedule.sort(key=lambda item: item[0])
    length = max(units + ready, base + o_units + blocks + 4)

    for step in range(1, count):
        gain_copy(step).start()

    def body(time, _):
        gather.tick(time)
        pl.when(time == 0)(spread_gains)

        @pl.when(time < blocks)
        def _():
            norm_block(time)

        for when, work in schedule:
            pl.when(time == when)(work)
        return 0

    lax.fori_loop(0, length, body, 0)
    for blk in range(blocks):
        summer.drain(blk)
    for step in range(1, count):
        gain_copy(step).wait_send()


def attend(tokens, own, gain_rows, mask, cosine, sine, depth, q_units, o_units):
    token_count, width = tokens.shape
    units, rows, cols = own.shape
    blocks, half = token_count // ROWS, ROWS // 2
    q_width = q_units * UNIT
    kv_width = UNIT // 2
    sum_bufs, sum_sems = TensorSum.scratch(blocks, half, width)
    count = depth * FOLD

    def out(*shape):
        return jax.ShapeDtypeStruct(shape, BF16)

    return pl.pallas_call(
        functools.partial(attend_kernel, (depth, units, q_units, o_units)),
        out_shape=(
            out(units, width, cols),
            out(token_count, width),
            out(token_count, q_width),
            out(token_count, kv_width),
            out(token_count, kv_width),
            out(token_count, q_width),
            out(token_count, width),
            out(token_count, width),
            jax.ShapeDtypeStruct((8, width), F32),
        ),
        in_specs=[VMEM_SPEC] * 6,
        out_specs=[HBM_SPEC] + [VMEM_SPEC] * 8,
        scratch_shapes=[
            VMEM((count, 8, rows), F32),
            VMEM((q_units + 1 + o_units, width, cols), BF16),
            VMEM((blocks, ROWS, width), BF16),
            *sum_bufs,
            *sum_sems,
            *Gather.scratch(units, depth),
            DMA((count,)),
            DMA((count,)),
            DMA,
        ],
        compiler_params=pltpu.CompilerParams(
            collective_id=0, has_side_effects=True, vmem_limit_bytes=60 << 20
        ),
        name="attend",
    )(tokens, own, gain_rows, mask, cosine, sine)


class Scatter:
    SLOTS = 4
    LAG = 2

    def __init__(self, place, rows, units, refs, first=0):
        self.place, self.rows, self.units, self.first = place, rows, units, first
        (
            self.grads,
            self.x_in,
            self.z_in,
            self.kept,
            self.mine,
            self.theirs,
            self.summed,
            self.x_send,
            self.x_recv,
            self.z_send,
            self.z_recv,
            self.load_sem,
            self.keep_sem,
        ) = refs

    @staticmethod
    def scratch(units, depth, rows):
        return [
            VMEM((depth, rows, UNIT), BF16),
            VMEM((depth, rows, UNIT), BF16),
            VMEM((Scatter.SLOTS, depth, rows, UNIT), BF16),
            DMA((units, depth)),
            DMA((units, depth)),
            DMA((units, depth)),
            DMA((units, depth)),
            DMA((2, depth)),
            DMA((Scatter.SLOTS,)),
        ]

    @staticmethod
    def outputs(units, depth, rows):
        return (
            jax.ShapeDtypeStruct((units, depth, rows, UNIT), BF16),
            jax.ShapeDtypeStruct((units, depth, rows, UNIT), BF16),
            jax.ShapeDtypeStruct((units, rows, UNIT), BF16),
        )

    def block(self, unit, index):
        start = pl.multiple_of(index * self.rows, self.rows)
        return self.grads.at[unit + self.first, pl.ds(start, self.rows)]

    def over(self, unit, zz):
        p = self.place
        return pltpu.make_async_remote_copy(
            self.block(unit, zz * FOLD + 1 - p.x),
            self.x_in.at[unit, zz],
            self.x_send.at[unit, zz],
            self.x_recv.at[unit, zz],
            device_id={"dp": p.partner},
            device_id_type=MESH,
        )

    def along(self, unit, step):
        p = self.place
        dest = lax.rem(p.z + step, p.depth)
        slot = lax.rem(unit, self.SLOTS)
        return pltpu.make_async_remote_copy(
            self.summed.at[slot, dest],
            self.z_in.at[unit, step],
            self.z_send.at[unit, step],
            self.z_recv.at[unit, step],
            device_id={"dp": dest * FOLD + p.x},
            device_id_type=MESH,
        )

    def keep(self, unit):
        slot = lax.rem(unit, self.SLOTS)
        return pltpu.make_async_copy(
            self.summed.at[slot, self.place.z], self.kept.at[unit], self.keep_sem.at[slot]
        )

    def stage(self, step, unit):
        p = self.place

        @pl.when((unit >= 0) & (unit < self.units))
        def _():
            if step == 0:
                for zz in range(p.depth):
                    self.over(unit, zz).start()
            elif step == 1:
                loads = []
                for zz in range(p.depth):
                    loads.append(
                        pltpu.make_async_copy(
                            self.block(unit, zz * FOLD + p.x),
                            self.mine.at[zz],
                            self.load_sem.at[0, zz],
                        )
                    )
                    loads[-1].start()
                for zz in range(p.depth):
                    self.over(unit, zz).wait_recv()
                    loads.append(
                        pltpu.make_async_copy(
                            self.x_in.at[unit, zz], self.theirs.at[zz], self.load_sem.at[1, zz]
                        )
                    )
                    loads[-1].start()
                for copy in loads:
                    copy.wait()
                slot = lax.rem(unit, self.SLOTS)
                for zz in range(p.depth):
                    self.summed[slot, zz] = (
                        self.mine[zz].astype(F32) + self.theirs[zz].astype(F32)
                    ).astype(BF16)
                for way in range(1, p.depth):
                    self.along(unit, way).start()
                self.keep(unit).start()
            else:
                for zz in range(p.depth):
                    self.over(unit, zz).wait_send()
                for way in range(1, p.depth):
                    self.along(unit, way).wait_send()
                self.keep(unit).wait()

    def tick(self, time):
        self.stage(2, time - self.LAG - (self.SLOTS - 1))
        self.stage(0, time)
        self.stage(1, time - self.LAG)

    def latency(self):
        return self.LAG + self.SLOTS

    def finish(self):
        def unit_end(unit, _):
            for way in range(1, self.place.depth):
                self.along(unit, way).wait_recv()
            return 0

        lax.fori_loop(0, self.units, unit_end, 0)


def feed_kernel(cfg, *refs):
    (
        b_ref,
        cot_ref,
        g_ref,
        grads_ref,
        x_in,
        z_in,
        kept,
        out_ref,
        db_ref,
        acc_out,
        acc_db,
        weights,
        grad_buf,
        hidden,
        dgu,
        part,
        half_in,
        half,
        far_in,
        total,
        back,
        sum_sends,
        sum_recvs,
        weight_sem,
        grad_sem,
        local_sem,
        *scatter_refs,
    ) = refs
    depth, first_unit, chunks, pace, scatter_units = cfg
    place = Place(depth)
    token_count, width = b_ref.shape
    rows = x_in.shape[2]
    blocks = token_count // ROWS
    tall = 2 * ROWS
    scatter = Scatter(place, rows, scatter_units, (grads_ref, x_in, z_in, kept, *scatter_refs))
    summer = TensorSum(place, part, (half_in, half, far_in, total, back), (sum_sends, sum_recvs))

    def load(chunk, matrix):
        slot = lax.rem(chunk, 2)
        return pltpu.make_async_copy(
            g_ref.at[first_unit + 3 * chunk + matrix],
            weights.at[slot, matrix],
            weight_sem.at[slot, matrix],
        )

    def save(chunk, matrix):
        slot = lax.rem(chunk, 2)
        return pltpu.make_async_copy(
            grad_buf.at[slot, matrix],
            grads_ref.at[3 * chunk + matrix],
            grad_sem.at[slot, matrix],
        )

    for matrix in range(3):
        load(0, matrix).start()
    place.enter()

    def clear(blk, _):
        rows_at = pl.ds(pl.multiple_of(blk * ROWS, ROWS), ROWS)
        acc_out[rows_at, :] = jnp.zeros((ROWS, width), F32)
        acc_db[rows_at, :] = jnp.zeros((ROWS, width), F32)
        return 0

    lax.fori_loop(0, blocks, clear, 0)

    def compute(chunk, slot):
        def hidden_rows(blk, _):
            rows_at = pl.ds(pl.multiple_of(blk * tall, tall), tall)
            stream, cot = b_ref[rows_at, :], cot_ref[rows_at, :]
            gate = dot(stream, weights[slot, 0])
            upper = dot(stream, weights[slot, 1])
            grad_hidden = dot(cot, weights[slot, 2])
            sigmoid = jax.nn.sigmoid(gate)
            silu = gate * sigmoid
            hid = (silu * upper).astype(BF16)
            grad_gate = (grad_hidden * upper * sigmoid * (1.0 + gate * (1.0 - sigmoid))).astype(
                BF16
            )
            grad_up = (grad_hidden * silu).astype(BF16)
            hidden[rows_at, :] = hid
            dgu[rows_at, :UNIT] = grad_gate
            dgu[rows_at, UNIT:] = grad_up

            def spread(piece, _):
                cols = pl.ds(pl.multiple_of(piece * tall, tall), tall)
                acc_out[rows_at, cols] += dot_nt(hidden[rows_at, :], weights[slot, 2, cols, :])
                acc_db[rows_at, cols] += dot_nt(
                    dgu[rows_at, :UNIT], weights[slot, 0, cols, :]
                ) + dot_nt(dgu[rows_at, UNIT:], weights[slot, 1, cols, :])
                return 0

            lax.fori_loop(0, width // tall, spread, 0)
            return 0

        lax.fori_loop(0, token_count // tall, hidden_rows, 0)

        def grad_rows(blk, _):
            cols = pl.ds(pl.multiple_of(blk * ROWS, ROWS), ROWS)
            both = dot_tn(b_ref[:, cols], dgu[...])
            grad_buf[slot, 0, cols, :] = both[:, :UNIT].astype(BF16)
            grad_buf[slot, 1, cols, :] = both[:, UNIT:].astype(BF16)
            grad_buf[slot, 2, cols, :] = dot_tn(cot_ref[:, cols], hidden[...]).astype(BF16)
            return 0

        lax.fori_loop(0, width // ROWS, grad_rows, 0)

    def step(chunk, _):
        slot = lax.rem(chunk, 2)
        for matrix in range(3):
            load(chunk, matrix).wait()

        @pl.when(chunk + 1 < chunks)
        def _():
            for matrix in range(3):
                load(chunk + 1, matrix).start()

        compute(chunk, slot)
        for matrix in range(3):
            save(chunk, matrix).start()
        for matrix in range(3):
            save(chunk, matrix).wait()
        for number in range(pace):
            scatter.tick(chunk * pace + number)
        return 0

    lax.fori_loop(0, chunks, step, 0)
    time = chunks * pace
    length = scatter_units + scatter.latency()
    for blk in range(blocks):
        rows_at = slice(blk * ROWS, (blk + 1) * ROWS)
        part[blk] = acc_out[rows_at, :].astype(BF16)
        copy = pltpu.make_async_copy(part.at[blk], out_ref.at[pl.ds(blk * ROWS, ROWS)], local_sem)
        copy.start()
        copy.wait()
        part[blk] = acc_db[rows_at, :].astype(BF16)
        summer.begin(blk)
    schedule = []
    for blk in range(blocks):
        schedule.append((blk, functools.partial(summer.middle, blk)))
        schedule.append((blk + 2, functools.partial(summer.late, blk)))

        def finish(blk=blk):
            copies = []
            for (row, values), sem in zip(summer.end(blk), (0, 1)):
                copies.append(
                    pltpu.make_async_copy(
                        values.at[blk], db_ref.at[pl.ds(row, ROWS // 2)], grad_sem.at[sem, 0]
                    )
                )
                copies[-1].start()
            for copy in copies:
                copy.wait()

        schedule.append((blk + 3, finish))
    schedule.sort(key=lambda item: item[0])

    def tail(now, _):
        scatter.tick(time + now)
        for when, work in schedule:
            pl.when(now == when)(work)
        return 0

    lax.fori_loop(0, max(length - time, blocks + 3), tail, 0)
    scatter.finish()
    for blk in range(blocks):
        summer.drain(blk)


def feed(b, cotangent, gathered, depth, first_unit, chunks, pace, scatter_units, grad_units):
    token_count, width = b.shape
    rows = width // (depth * FOLD)
    blocks, half = token_count // ROWS, ROWS // 2
    sum_bufs, sum_sems = TensorSum.scratch(blocks, half, width)
    full = jax.ShapeDtypeStruct((token_count, width), BF16)
    return pl.pallas_call(
        functools.partial(feed_kernel, (depth, first_unit, chunks, pace, scatter_units)),
        out_shape=(
            jax.ShapeDtypeStruct((grad_units, width, UNIT), BF16),
            *Scatter.outputs(scatter_units, depth, rows),
            full,
            full,
        ),
        in_specs=[VMEM_SPEC, VMEM_SPEC, HBM_SPEC],
        out_specs=[HBM_SPEC] * 6,
        scratch_shapes=[
            VMEM((token_count, width), F32),
            VMEM((token_count, width), F32),
            VMEM((2, 3, width, UNIT), BF16),
            VMEM((2, 3, width, UNIT), BF16),
            VMEM((token_count, UNIT), BF16),
            VMEM((token_count, 2 * UNIT), BF16),
            VMEM((blocks, ROWS, width), BF16),
            *sum_bufs,
            *sum_sems,
            DMA((2, 3)),
            DMA((2, 3)),
            DMA,
            *Scatter.scratch(scatter_units, depth, rows),
        ],
        compiler_params=pltpu.CompilerParams(
            collective_id=1, has_side_effects=True, vmem_limit_bytes=63 << 20
        ),
        name="feed",
    )(b, cotangent, gathered)


def back_kernel(cfg, *refs):
    (
        x_ref,
        q_ref,
        k_ref,
        v_ref,
        att_ref,
        mask_ref,
        cos_ref,
        sin_ref,
        gains,
        cot_ref,
        att_sum_ref,
        db_ref,
        part_out_ref,
        a_ref,
        g_ref,
        _,
        grads_ref,
        x_in,
        z_in,
        kept,
        dx_ref,
        sum_ref,
        gain_ref,
        dx2,
        low,
        weights,
        do,
        dq,
        dkv,
        dk,
        dv,
        part,
        half_in,
        half,
        far_in,
        total,
        back,
        far_first,
        piece,
        grad_buf,
        gain_acc,
        gain_blocks,
        gain_land,
        sum_sends,
        sum_recvs,
        first_sends,
        first_recvs,
        gain_send,
        gain_recv,
        load_sem,
        *scatter_refs,
    ) = refs
    depth, first_grad, scatter_units, q_units, o_units = cfg
    place = Place(depth)
    count = depth * FOLD
    token_count, width = x_ref.shape
    rows = x_in.shape[2]
    kv_width = k_ref.shape[1]
    blocks, short = token_count // ROWS, ROWS // 2
    scatter = Scatter(
        place, rows, scatter_units, (grads_ref, x_in, z_in, kept, *scatter_refs), first_grad
    )
    feed_left = scatter_units - o_units - q_units - 1
    own_grads = first_grad + feed_left
    summer = TensorSum(place, part, (half_in, half, far_in, total, back), (sum_sends, sum_recvs))
    stored = StoredSum(
        place,
        part_out_ref,
        (half_in, half, far_first, total, back),
        (first_sends, first_recvs),
        piece,
        load_sem.at[0],
    )
    lane = lax.broadcasted_iota(jnp.int32, (1, LANES), 1)
    low_half = lane < HEAD_SIZE

    def fetch(pairs):
        copies = [
            pltpu.make_async_copy(src, dst, load_sem.at[number])
            for number, (src, dst) in enumerate(pairs)
        ]
        for copy in copies:
            copy.start()
        for copy in copies:
            copy.wait()

    gain_acc[...] = jnp.zeros_like(gain_acc)
    dk[...] = jnp.zeros_like(dk)
    dv[...] = jnp.zeros_like(dv)
    place.enter()

    def middle_grad(blk):
        at = slice(blk * ROWS, (blk + 1) * ROWS)
        fetch(
            (
                (cot_ref.at[pl.ds(blk * ROWS, ROWS)], part.at[0]),
                (att_sum_ref.at[pl.ds(blk * ROWS, ROWS)], part.at[1]),
                (db_ref.at[pl.ds(blk * ROWS, ROWS)], part.at[2]),
            )
        )
        middle = x_ref[at, :].astype(F32) + part[1].astype(F32)
        inverse = lax.rsqrt(jnp.mean(middle * middle, axis=-1, keepdims=True) + EPS_NORM)
        normal = middle * inverse
        grad = part[2].astype(F32)
        gain_acc[1:2, :] += jnp.sum(grad * normal, axis=0, keepdims=True)
        scaled = grad * gains[1:2, :]
        centre = jnp.mean(scaled * normal, axis=-1, keepdims=True)
        result = part[0].astype(F32) + inverse * (scaled - normal * centre)
        dx2[at, :] = result
        low[at, :] = result.astype(BF16)

    def attended_grad():
        fetch([(g_ref.at[q_units + 1 + unit], weights.at[unit]) for unit in range(o_units)])

        def block(blk, _):
            at = pl.ds(pl.multiple_of(blk * ROWS, ROWS), ROWS)
            for unit in range(o_units):
                do[at, unit * UNIT : (unit + 1) * UNIT] = dot(low[at, :], weights[unit]).astype(
                    BF16
                )
            return 0

        lax.fori_loop(0, blocks, block, 0)

    def save_grad(slot, number, left, right, start):
        def block(blk, _):
            cols = pl.ds(pl.multiple_of(blk * ROWS, ROWS), ROWS)
            grad_buf[slot, cols, :] = dot_tn(
                left[:, cols], right[:, start : start + UNIT]
            ).astype(BF16)
            return 0

        lax.fori_loop(0, width // ROWS, block, 0)
        fetch([(grad_buf.at[slot], grads_ref.at[own_grads + number])])

    def second_weights():
        fetch(
            [(a_ref, low)]
            + [(g_ref.at[unit], weights.at[unit]) for unit in range(q_units + 1)]
        )

    def attention_pairs(blk, first, last):
        start, stop = blk * ROWS, (blk + 1) * ROWS

        def pair(index, _):
            lanes = pl.ds(pl.multiple_of(index * LANES, LANES), LANES)
            query, grad = q_ref[start:stop, lanes], do[start:stop, lanes]
            outs = []
            for one in (True, False):
                keep = low_half if one else jnp.logical_not(low_half)
                query_one = jnp.where(keep, query, jnp.zeros_like(query))
                grad_one = jnp.where(keep, grad, jnp.zeros_like(grad))
                scores = dot_nt(k_ref[:stop, :], query_one) * HEAD_SIZE ** (-0.5)
                allowed = mask_ref[:stop, start:stop].astype(F32) > 0
                scores = jnp.where(allowed, scores, NEG_FILL)
                expo = jnp.exp(scores - jnp.max(scores, axis=0, keepdims=True))
                probs = expo * (1.0 / jnp.sum(expo, axis=0, keepdims=True))
                grad_probs = dot_nt(v_ref[:stop, :], grad_one)
                centre = jnp.sum(probs * grad_probs, axis=0, keepdims=True)
                grad_scores = (probs * (grad_probs - centre)).astype(BF16)
                dv[:stop, :] += dot(probs.astype(BF16), grad_one)
                dk[:stop, :] += dot(grad_scores, query_one)
                outs.append(dot_tn(grad_scores, k_ref[:stop, :]))
            joined = jnp.where(low_half, outs[0], outs[1]) * HEAD_SIZE ** (-0.5)
            dq[start:stop, lanes] = turn(
                joined, cos_ref[start:stop, :], sin_ref[start:stop, :], True
            ).astype(BF16)
            return 0

        lax.fori_loop(first, last, pair, 0)

    def input_part(blk):
        at = slice(blk * ROWS, (blk + 1) * ROWS)
        dkv[at, :kv_width] = turn(
            dk[at, :] * HEAD_SIZE ** (-0.5), cos_ref[at, :], sin_ref[at, :], True
        ).astype(BF16)
        dkv[at, kv_width:] = dv[at, :].astype(BF16)
        out = dot_nt(dkv[at, :], weights[q_units])
        for unit in range(q_units):
            out = out + dot_nt(dq[at, unit * UNIT : (unit + 1) * UNIT], weights[unit])
        part[blk] = out.astype(BF16)
        summer.begin(blk)

    def finish(blk):
        for row, values in summer.end(blk):
            at = pl.ds(row, short)
            grad = values[blk].astype(F32)
            stream = x_ref[at, :].astype(F32)
            inverse = lax.rsqrt(jnp.mean(stream * stream, axis=-1, keepdims=True) + EPS_NORM)
            normal = stream * inverse
            gain_acc[0:1, :] += jnp.sum(grad * normal, axis=0, keepdims=True)
            scaled = grad * gains[0:1, :]
            centre = jnp.mean(scaled * normal, axis=-1, keepdims=True)
            dx2[at, :] += inverse * (scaled - normal * centre)
        fetch([(dx2.at[pl.ds(blk * ROWS, ROWS)], dx_ref.at[pl.ds(blk * ROWS, ROWS)])])

    def stored_end(blk):
        fetch(
            [
                (values.at[blk], sum_ref.at[pl.ds(row, short)])
                for row, values in stored.end(blk)
            ]
        )
        stored.drain(blk)

    pairs = q_ref.shape[1] // LANES
    schedule = []

    def add(when, work, *args):
        schedule.append((when, functools.partial(work, *args)))

    for blk in range(blocks):
        add(blk // 2, middle_grad, blk)
        add(blk, stored.begin, blk)
        add(blk + 1, stored.middle, blk)
        add(blk + 3, stored.late, blk)
        add(blk + 4, stored_end, blk)
    now = blocks // 2
    add(now, attended_grad)
    for unit in range(o_units):
        add(now + 1 + unit, save_grad, unit % 2, unit, low, att_ref, unit * UNIT)
    now += o_units
    add(now, second_weights)
    now += 1
    for blk in reversed(range(blocks)):
        steps = max(1, (blk * 2 + 2) // 3)
        each = -(-pairs // steps)
        for first in range(0, pairs, each):
            add(now, attention_pairs, blk, first, min(pairs, first + each))
            now += 1
        begin = max(now - 1, blk + 5)
        add(begin, input_part, blk)
        add(begin + 1, summer.middle, blk)
        add(begin + 3, summer.late, blk)
        add(begin + 4, finish, blk)
    length = now + 5
    for unit in range(q_units):
        add(now, save_grad, unit % 2, o_units + unit, low, dq, unit * UNIT)
    add(now, save_grad, q_units % 2, o_units + q_units, low, dkv, 0)
    early = now - (feed_left + o_units)
    schedule.sort(key=lambda item: item[0])
    hold = max(0, early + 1)
    length = max(length, scatter_units + hold + scatter.latency())

    def body(time, _):
        for when, work in schedule:
            pl.when(time == when)(work)
        scatter.tick(time - hold)
        return 0

    lax.fori_loop(0, length, body, 0)
    for source in range(count):
        gain_blocks[source] = gain_acc[:, source * rows : (source + 1) * rows]

    def gain_copy(step):
        dest = lax.rem(place.me + step, count)
        return pltpu.make_async_remote_copy(
            gain_blocks.at[dest],
            gain_land.at[place.me],
            gain_send.at[step],
            gain_recv.at[place.me],
            device_id={"dp": dest},
            device_id_type=MESH,
        )

    def gain_arrival(source):
        return pltpu.make_async_remote_copy(
            gain_blocks.at[0],
            gain_land.at[source],
            gain_send.at[0],
            gain_recv.at[source],
            device_id={"dp": place.partner},
            device_id_type=MESH,
        )

    for step in range(1, count):
        gain_copy(step).start()
    summed = gain_blocks[place.me]
    for step in range(1, count):
        source = lax.rem(place.me + step, count)
        gain_arrival(source).wait_recv()
        summed = summed + gain_land[source]
    gain_ref[...] = summed
    for step in range(1, count):
        gain_copy(step).wait_send()
    scatter.finish()
    for blk in range(blocks):
        summer.drain(blk)


class StoredSum(TensorSum):
    def __init__(self, place, part, bufs, sems, piece, sem):
        super().__init__(place, part, bufs, sems)
        self.piece, self.sem = piece, sem

    def rows_of(self, blk, core):
        short = self.half.shape[1]
        return pl.ds(pl.multiple_of(blk * 2 * short + core * short, short), short)

    def first(self, blk):
        src = self.part.at[self.rows_of(blk, 1 - self.place.core)]
        return self.copy(0, src, self.half_in, blk)

    def middle(self, blk):
        copy = pltpu.make_async_copy(
            self.part.at[self.rows_of(blk, self.place.core)], self.piece, self.sem
        )
        copy.start()
        self.first(blk).wait_recv()
        copy.wait()
        self.half[blk] = (self.piece[...].astype(F32) + self.half_in[blk].astype(F32)).astype(BF16)
        self.second(blk).start()


def attend_back(
    tokens, q, k, v, att, mask, cosine, sine, gains, cotangent, att_sum, db, out_part, a,
    gathered, grads, depth, first_grad, q_units, o_units,
):
    token_count, width = tokens.shape
    rows = width // (depth * FOLD)
    blocks, half = token_count // ROWS, ROWS // 2
    q_width, kv_width = q.shape[1], k.shape[1]
    scatter_units = grads.shape[0] - first_grad
    sum_bufs, sum_sems = TensorSum.scratch(blocks, half, width)
    count = depth * FOLD
    wide = max(q_units + 1, o_units)
    return pl.pallas_call(
        functools.partial(back_kernel, (depth, first_grad, scatter_units, q_units, o_units)),
        out_shape=(
            jax.ShapeDtypeStruct(grads.shape, BF16),
            *Scatter.outputs(scatter_units, depth, rows),
            jax.ShapeDtypeStruct((token_count, width), F32),
            jax.ShapeDtypeStruct((token_count, width), BF16),
            jax.ShapeDtypeStruct((8, rows), F32),
        ),
        in_specs=[VMEM_SPEC] * 9 + [HBM_SPEC] * 7,
        out_specs=[HBM_SPEC] * 6 + [VMEM_SPEC],
        scratch_shapes=[
            VMEM((token_count, width), F32),
            VMEM((token_count, width), BF16),
            VMEM((wide, width, UNIT), BF16),
            VMEM((token_count, q_width), BF16),
            VMEM((token_count, q_width), BF16),
            VMEM((token_count, 2 * kv_width), BF16),
            VMEM((token_count, kv_width), F32),
            VMEM((token_count, kv_width), F32),
            VMEM((blocks, ROWS, width), BF16),
            *sum_bufs,
            VMEM((blocks, half, width), BF16),
            VMEM((half, width), BF16),
            VMEM((2, width, UNIT), BF16),
            VMEM((8, width), F32),
            VMEM((count, 8, rows), F32),
            VMEM((count, 8, rows), F32),
            *sum_sems,
            *sum_sems,
            DMA((count,)),
            DMA((count,)),
            DMA((8,)),
            *Scatter.scratch(scatter_units, depth, rows),
        ],
        input_output_aliases={15: 0},
        compiler_params=pltpu.CompilerParams(
            collective_id=2, has_side_effects=True, vmem_limit_bytes=63 << 20
        ),
        name="attend_back",
    )(
        tokens, q, k, v, att, mask, cosine, sine, gains, cotangent, att_sum, db, out_part, a,
        gathered, grads,
    )


def gathered_units(mine, arrived):
    total = mine.astype(F32)
    for step in range(1, arrived.shape[1]):
        total = total + arrived[:, step].astype(F32)
    return total


def shards(
    depth,
    tokens,
    attention_gain,
    query_matrix,
    key_matrix,
    value_matrix,
    output_weight,
    feed_gain,
    gate_weight,
    up_weight,
    down_weight,
    sequence_lengths,
    block_mask,
    cotangent,
):
    token_count, width = tokens.shape
    rows, q_width = query_matrix.shape
    kv_width = key_matrix.shape[1]
    heads_kv = kv_width // HEAD_SIZE
    groups = q_width // kv_width
    feed_width = gate_weight.shape[1]
    chunks = feed_width // UNIT
    q_units = q_width // UNIT

    def pair(cols):
        return cols.reshape(-1, heads_kv, groups, HEAD_SIZE).swapaxes(1, 2).reshape(-1, q_width)

    def unpair(cols):
        return cols.reshape(-1, groups, heads_kv, HEAD_SIZE).swapaxes(1, 2).reshape(-1, q_width)

    def split(cols):
        return cols.reshape(rows, -1, UNIT).swapaxes(0, 1)

    feed_units = jnp.stack(
        [split(gate_weight), split(up_weight), split(down_weight.T)], axis=1
    ).reshape(3 * chunks, rows, UNIT)
    own = jnp.concatenate(
        [
            split(pair(query_matrix)),
            split(jnp.concatenate([key_matrix, value_matrix], axis=1)),
            split(pair(output_weight.T)),
            feed_units,
        ],
        axis=0,
    )
    sequence, position, valid = token_layout(sequence_lengths[0], token_count, BLOCK)
    allowed = allowed_pairs(sequence, position, valid, block_mask, BLOCK)
    cosine, sine = rope_tables(position, HEAD_SIZE)
    wide_cos = jnp.concatenate([cosine] * 4, axis=1)
    wide_sin = jnp.concatenate([-sine, sine] * 2, axis=1)
    gain_rows = jnp.concatenate(
        [
            attention_gain.astype(F32)[None],
            feed_gain.astype(F32)[None],
            jnp.zeros((6, rows), F32),
        ],
        axis=0,
    )
    first_unit = 2 * q_units + 1
    gathered, a, q, k, v, att, att_sum, b, gains = attend(
        tokens, own, gain_rows, allowed.astype(F32), wide_cos, wide_sin, depth, q_units, q_units
    )
    grads, _, z_in, kept, out_part, db = feed(
        b, cotangent, gathered, depth, first_unit, chunks, PACE, EARLY, own.shape[0]
    )
    _, _, z_in_late, kept_late, input_grad, out_sum, gain_grads = attend_back(
        tokens, q, k, v, att, allowed.T.astype(BF16), wide_cos, wide_sin, gains, cotangent,
        att_sum, db, out_part, a, gathered, grads, depth, EARLY, q_units, q_units,
    )
    block_output = (
        tokens.astype(F32) + att_sum.astype(F32) + out_sum.astype(F32)
    ).astype(BF16)
    late = gathered_units(kept_late, z_in_late)
    feed_late = 3 * chunks - EARLY
    feed_grads = jnp.concatenate(
        [gathered_units(kept, z_in), late[:feed_late]], axis=0
    ).reshape(chunks, 3, rows, UNIT)

    def row_of(units):
        return units.swapaxes(0, 1).reshape(rows, -1)

    out_grad = row_of(late[feed_late : feed_late + q_units]).T
    query_grad = row_of(late[feed_late + q_units : feed_late + 2 * q_units])
    kv_grad = late[feed_late + 2 * q_units]

    def join(which):
        return row_of(feed_grads[:, which])

    out_grad = out_grad.reshape(groups, heads_kv, HEAD_SIZE, rows).swapaxes(0, 1)
    return (
        block_output,
        input_grad,
        gain_grads[0],
        unpair(query_grad),
        kv_grad[:, :kv_width],
        kv_grad[:, kv_width:],
        out_grad.reshape(q_width, rows),
        gain_grads[1],
        join(0),
        join(1),
        join(2).T,
    )


PACE = 1
EARLY = 13


def solution(mesh):
    in_specs = (
        P("dp", None),
        P("dp"),
        P("dp", "tensor"),
        P("dp", "tensor"),
        P("dp", "tensor"),
        P("tensor", "dp"),
        P("dp"),
        P("dp", "tensor"),
        P("dp", "tensor"),
        P("tensor", "dp"),
        P("dp", None),
        P("dp", None),
        P("dp", None),
    )
    out_specs = (
        P("dp", None),
        P("dp", None),
        P("dp"),
        P("dp", "tensor"),
        P("dp", "tensor"),
        P("dp", "tensor"),
        P("tensor", "dp"),
        P("dp"),
        P("dp", "tensor"),
        P("dp", "tensor"),
        P("tensor", "dp"),
    )
    return jax.shard_map(
        functools.partial(shards, mesh.shape["dp"] // FOLD),
        mesh=mesh,
        in_specs=in_specs,
        out_specs=out_specs,
        check_vma=False,
    )
```

```python
import functools

import jax
import jax.numpy as jnp
from jax import lax
from jax.experimental import pallas as pl
from jax.experimental.pallas import tpu as pltpu
from jax.sharding import PartitionSpec as P

HEAD_SIZE = 64
BLOCK = 128
LANES = 128
EPS_NORM = 1e-05
THETA_BASE = 500000.0
NEG_FILL = -1e30
UNIT = 256
ROWS = 256
FOLD = 2
XFIRST = 6
MESH = pl.DeviceIdType.MESH
VMEM = pltpu.VMEM
DMA = pltpu.SemaphoreType.DMA
HBM_SPEC = pl.BlockSpec(memory_space=pl.ANY)
VMEM_SPEC = pl.BlockSpec(memory_space=pltpu.VMEM)
F32 = jnp.float32
BF16 = jnp.bfloat16


EARLY_CHUNKS = 6
EARLY_UNITS = 10
SCATTER_EVERY = 2


def split(depth):
    return 2 if depth <= 8 else 1


def token_layout(lengths_row, total, block):
    blocks_per = (lengths_row + block - 1) // block
    offsets = jnp.cumsum(blocks_per) - blocks_per
    first_token = offsets * block
    indices = jnp.arange(total, dtype=jnp.int32)
    member = (indices[:, None] >= first_token[None, :]) & (blocks_per[None, :] > 0)
    sequence = jnp.sum(member.astype(jnp.int32), axis=1) - 1
    select = sequence[:, None] == jnp.arange(lengths_row.shape[0], dtype=jnp.int32)[None, :]
    begins = jnp.sum(jnp.where(select, first_token[None, :], 0), axis=1)
    limits = jnp.sum(jnp.where(select, lengths_row[None, :], 0), axis=1)
    position = indices - begins
    return (sequence, position, position < limits)


def slot_codes(sequence, valid, mask_blocks, block):
    blocks = mask_blocks.shape[0]
    index = jnp.arange(blocks, dtype=jnp.int32)
    own = jnp.max(jnp.where(index[:, None] == index[None, :], mask_blocks, 0), axis=1)
    live = jnp.broadcast_to(own[:, None] > 0, (blocks, block)).reshape(blocks * block)
    query_code = jnp.where(live, sequence, -1)
    key_code = jnp.where(valid, sequence, -2)
    return query_code, key_code


def rope_tables(position, head_dim):
    freqs = THETA_BASE ** (-jnp.arange(head_dim // 2, dtype=F32) * 2.0 / head_dim)
    angles = position.astype(F32)[:, None] * freqs[None, :]
    return (jnp.cos(angles), jnp.sin(angles))


def dot(left, right):
    return jnp.dot(left, right, preferred_element_type=F32)


def dot_nt(left, right):
    return lax.dot_general(left, right, (((1,), (1,)), ((), ())), preferred_element_type=F32)


def dot_tn(left, right):
    return lax.dot_general(left, right, (((0,), (0,)), ((), ())), preferred_element_type=F32)


class Place:
    def __init__(self, depth):
        self.depth = depth
        self.me = lax.axis_index("dp")
        self.z = self.me // FOLD
        self.x = self.me % FOLD
        self.right = self.me + FOLD
        self.left = self.me - FOLD
        self.partner = self.z * FOLD + (1 - self.x)
        member = lax.axis_index("tensor")
        self.core = member % 2
        row = member // 2
        self.other = row * 2 + (1 - self.core)
        self.across = (1 - row) * 2 + self.core

    def enter(self):
        count = self.depth * FOLD
        barrier = pltpu.get_barrier_semaphore()
        for step in range(1, count):
            pl.semaphore_signal(
                barrier,
                1,
                device_id={"dp": lax.rem(self.me + step, count)},
                device_id_type=MESH,
            )
        for peer in (self.other, self.across):
            pl.semaphore_signal(barrier, 1, device_id={"tensor": peer}, device_id_type=MESH)
        pl.semaphore_wait(barrier, count + 1)


class Gather:
    def __init__(self, place, g_ref, rows, pieces, sems, base=0):
        self.place, self.g, self.rows, self.pieces, self.base = place, g_ref, rows, pieces, base
        self.z_send, self.z_recv, self.x_send, self.x_recv = sems

    @staticmethod
    def scratch(pieces, depth):
        return [
            DMA((pieces, 2, depth, FOLD)),
            DMA((pieces, depth, FOLD)),
            DMA((pieces, depth)),
            DMA((pieces, depth)),
        ]

    def block(self, piece, index):
        whole, parts = piece + self.base, split(self.place.depth)
        size = self.rows // parts
        start = pl.multiple_of(index * self.rows + lax.rem(whole, parts) * size, size)
        return self.g.at[whole // parts, pl.ds(start, size)]

    def along(self, piece, zz, xx, way):
        p = self.place
        ref = self.block(piece, zz * FOLD + xx)
        return pltpu.make_async_remote_copy(
            ref,
            ref,
            self.z_send.at[piece, way, zz, xx],
            self.z_recv.at[piece, zz, xx],
            device_id={"dp": p.left if way else p.right},
            device_id_type=MESH,
        )

    def over(self, piece, zz, incoming=False):
        p = self.place
        ref = self.block(piece, zz * FOLD + (1 - p.x if incoming else p.x))
        return pltpu.make_async_remote_copy(
            ref,
            ref,
            self.x_send.at[piece, zz],
            self.x_recv.at[piece, zz],
            device_id={"dp": p.partner},
            device_id_type=MESH,
        )

    def lanes(self, wide):
        return range(FOLD) if wide else (self.place.x,)

    def send_both(self, piece, zz, wide):
        p, last = self.place, self.place.depth - 1

        @pl.when(p.z < last)
        def _():
            for xx in self.lanes(wide):
                self.along(piece, zz, xx, 0).start()

        @pl.when(p.z > 0)
        def _():
            for xx in self.lanes(wide):
                self.along(piece, zz, xx, 1).start()

    def forward(self, piece, step, wide):
        p, last = self.place, self.place.depth - 1

        @pl.when(p.z >= step)
        def _():
            zz = p.z - step
            for xx in self.lanes(wide):
                self.along(piece, zz, xx, 0).wait_recv()

            @pl.when(p.z < last)
            def _():
                for xx in self.lanes(wide):
                    self.along(piece, zz, xx, 0).start()

            if not wide:
                self.over(piece, zz).start()

        @pl.when(p.z + step <= last)
        def _():
            zz = p.z + step
            for xx in self.lanes(wide):
                self.along(piece, zz, xx, 1).wait_recv()

            @pl.when(p.z > 0)
            def _():
                for xx in self.lanes(wide):
                    self.along(piece, zz, xx, 1).start()

            if not wide:
                self.over(piece, zz).start()

    def drain(self, piece, wide):
        p, last = self.place, self.place.depth - 1
        for zz in range(p.depth):

            @pl.when((p.z >= zz) & (p.z < last))
            def _():
                for xx in self.lanes(wide):
                    self.along(piece, zz, xx, 0).wait_send()

            @pl.when((p.z <= zz) & (p.z > 0))
            def _():
                for xx in self.lanes(wide):
                    self.along(piece, zz, xx, 1).wait_send()

    def stage(self, step, piece):
        p, depth = self.place, self.place.depth

        def slow_first():
            if step == 0:
                self.send_both(piece, p.z, False)
                self.over(piece, p.z).start()
            elif step < depth:
                self.forward(piece, step, False)
            else:
                for zz in range(depth):
                    self.over(piece, zz, True).wait_recv()
                for zz in range(depth):
                    self.over(piece, zz).wait_send()
                self.drain(piece, False)

        def fast_first():
            if step == 0:
                self.over(piece, p.z).start()
            elif step == 1:
                self.over(piece, p.z, True).wait_recv()
                self.send_both(piece, p.z, True)
            else:
                self.forward(piece, step - 1, True)
                if step == depth:
                    self.over(piece, p.z).wait_send()
                    self.drain(piece, True)

        inside = (piece >= 0) & (piece < self.pieces)
        fast = lax.rem(piece + self.base, XFIRST) == XFIRST - 1
        pl.when(inside & jnp.logical_not(fast))(slow_first)
        pl.when(inside & fast)(fast_first)

    def latency(self):
        return self.place.depth + 1

    def tick(self, time):
        depth = self.place.depth
        for step in range(depth):
            self.stage(step, time - step)
        self.stage(depth, time - depth - 1)


class TensorSum:
    def __init__(self, place, part, bufs, sems):
        self.place, self.part = place, part
        self.half_in, self.half, self.far_in, self.total, self.back = bufs
        self.sends, self.recvs = sems

    @staticmethod
    def scratch(blocks, half, width):
        return [VMEM((blocks, half, width), BF16)] * 5, [DMA((3, blocks)), DMA((3, blocks))]

    def copy(self, step, src, dst, blk):
        p = self.place
        return pltpu.make_async_remote_copy(
            src,
            dst.at[blk],
            self.sends.at[step, blk],
            self.recvs.at[step, blk],
            device_id={"tensor": p.across if step == 1 else p.other},
            device_id_type=MESH,
        )

    def first(self, blk):
        half = self.half.shape[1]
        start = pl.multiple_of((1 - self.place.core) * half, half)
        return self.copy(0, self.part.at[blk, pl.ds(start, half)], self.half_in, blk)

    def second(self, blk):
        return self.copy(1, self.half.at[blk], self.far_in, blk)

    def third(self, blk):
        return self.copy(2, self.total.at[blk], self.back, blk)

    def begin(self, blk):
        self.first(blk).start()

    def middle(self, blk):
        half = self.half.shape[1]
        self.first(blk).wait_recv()
        start = pl.multiple_of(self.place.core * half, half)
        mine = self.part[blk, pl.ds(start, half), :].astype(F32)
        self.half[blk] = (mine + self.half_in[blk].astype(F32)).astype(BF16)
        self.second(blk).start()

    def late(self, blk):
        self.second(blk).wait_recv()
        self.total[blk] = (self.half[blk].astype(F32) + self.far_in[blk].astype(F32)).astype(BF16)
        self.third(blk).start()

    def end(self, blk):
        half = self.half.shape[1]
        self.third(blk).wait_recv()
        core = self.place.core
        return (
            (pl.multiple_of(blk * 2 * half + core * half, half), self.total),
            (pl.multiple_of(blk * 2 * half + (1 - core) * half, half), self.back),
        )

    def drain(self, blk):
        self.first(blk).wait_send()
        self.second(blk).wait_send()
        self.third(blk).wait_send()


class StoredSum(TensorSum):
    def __init__(self, place, part, bufs, sems, piece, sem):
        super().__init__(place, part, bufs, sems)
        self.piece, self.sem = piece, sem

    def rows_of(self, blk, core):
        short = self.half.shape[1]
        return pl.ds(pl.multiple_of(blk * 2 * short + core * short, short), short)

    def first(self, blk):
        src = self.part.at[self.rows_of(blk, 1 - self.place.core)]
        return self.copy(0, src, self.half_in, blk)

    def middle(self, blk):
        copy = pltpu.make_async_copy(
            self.part.at[self.rows_of(blk, self.place.core)], self.piece, self.sem
        )
        copy.start()
        self.first(blk).wait_recv()
        copy.wait()
        self.half[blk] = (self.piece[...].astype(F32) + self.half_in[blk].astype(F32)).astype(BF16)
        self.second(blk).start()


def turn(values, cosine, sine, back=False):
    half = HEAD_SIZE // 2
    lane = lax.broadcasted_iota(jnp.int32, (1, LANES), 1)
    low = lax.rem(lane, HEAD_SIZE) < half
    tiles = []
    for start in range(0, values.shape[1], LANES):
        tile = values[:, start : start + LANES]
        swapped = jnp.where(low, pltpu.roll(tile, LANES - half, 1), pltpu.roll(tile, half, 1))
        if back:
            tiles.append(tile * cosine - swapped * sine)
        else:
            tiles.append(tile * cosine + swapped * sine)
    return tiles[0] if len(tiles) == 1 else jnp.concatenate(tiles, axis=1)


def normed(stream):
    return stream * lax.rsqrt(jnp.mean(stream * stream, axis=-1, keepdims=True) + EPS_NORM)


def attend_kernel(cfg, *refs):
    (
        x_ref,
        w_ref,
        gain_ref,
        cols_ref,
        rows_ref,
        cos_ref,
        sin_ref,
        g_ref,
        a_ref,
        q_ref,
        k_ref,
        v_ref,
        att_ref,
        sum_ref,
        b_ref,
        gains,
        gain_in,
        weights,
        mask,
        part,
        half_in,
        half,
        far_in,
        total,
        back,
        sum_sends,
        sum_recvs,
        z_send,
        z_recv,
        x_send,
        x_recv,
        gain_send,
        gain_recv,
        local_sem,
    ) = refs
    depth, pieces, q_units, o_units = cfg
    place = Place(depth)
    count = depth * FOLD
    token_count, width = x_ref.shape
    rows = w_ref.shape[1]
    blocks = token_count // ROWS
    fill = pltpu.make_async_copy(
        w_ref, g_ref.at[:, pl.ds(pl.multiple_of(place.me * rows, rows), rows)], local_sem
    )
    fill.start()
    place.enter()
    fill.wait()
    gather = Gather(place, g_ref, rows, pieces, (z_send, z_recv, x_send, x_recv))
    summer = TensorSum(place, part, (half_in, half, far_in, total, back), (sum_sends, sum_recvs))

    def gain_copy(step):
        return pltpu.make_async_remote_copy(
            gain_ref,
            gain_in.at[place.me],
            gain_send.at[step],
            gain_recv.at[place.me],
            device_id={"dp": lax.rem(place.me + step, count)},
            device_id_type=MESH,
        )

    def gain_arrival(source):
        return pltpu.make_async_remote_copy(
            gain_ref,
            gain_in.at[source],
            gain_send.at[0],
            gain_recv.at[source],
            device_id={"dp": place.partner},
            device_id_type=MESH,
        )

    lane = lax.broadcasted_iota(jnp.int32, (1, LANES), 1)
    low_half = lane < HEAD_SIZE

    def spread_gains():
        gain_in[place.me] = gain_ref[...]
        for step in range(1, count):
            gain_arrival(lax.rem(place.me + step, count)).wait_recv()
        for source in range(count):
            gains[:, source * rows : (source + 1) * rows] = gain_in[source]

    def norm_block(blk):
        rows_at = pl.ds(pl.multiple_of(blk * ROWS, ROWS), ROWS)
        stream = x_ref[rows_at, :].astype(F32)
        a_ref[rows_at, :] = (normed(stream) * gains[0:1, :]).astype(BF16)

    def load(unit):
        copy = pltpu.make_async_copy(g_ref.at[unit], weights.at[unit], local_sem)
        copy.start()
        copy.wait()

    def project(unit):
        load(unit)

        def block(blk, _):
            rows_at = pl.ds(pl.multiple_of(blk * ROWS, ROWS), ROWS)
            cosine, sine = cos_ref[rows_at, :], sin_ref[rows_at, :]
            out = dot(a_ref[rows_at, :], weights[unit])
            if unit < q_units:
                q_ref[rows_at, unit * UNIT : (unit + 1) * UNIT] = turn(out, cosine, sine).astype(
                    BF16
                )
            else:
                kv = k_ref.shape[1]
                k_ref[rows_at, :] = turn(out[:, :kv], cosine, sine).astype(BF16)
                v_ref[rows_at, :] = out[:, kv:].astype(BF16)
            return 0

        lax.fori_loop(0, blocks, block, 0)

    def attend(blk, first, last):
        start, stop = blk * ROWS, (blk + 1) * ROWS
        if first == 0:
            key = lax.broadcasted_iota(jnp.int32, (ROWS, stop), 1)
            query_at = lax.broadcasted_iota(jnp.int32, (ROWS, stop), 0) + start
            same = cols_ref[start:stop, 0:1] == rows_ref[1:2, :stop]
            allowed = (same & (key <= query_at)) | (key == query_at)
            mask[:, :stop] = jnp.where(allowed, 0.0, NEG_FILL)

        def pair(index, _):
            lanes = pl.ds(pl.multiple_of(index * LANES, LANES), LANES)
            query = q_ref[start:stop, lanes]
            outs = []
            for one in (True, False):
                keep = low_half if one else jnp.logical_not(low_half)
                masked = jnp.where(keep, query, jnp.zeros_like(query))
                scores = dot_nt(masked, k_ref[:stop, :]) * HEAD_SIZE ** (-0.5)
                scores = jnp.where(mask[:, :stop] < 0, NEG_FILL, scores)
                expo = jnp.exp(scores - jnp.max(scores, axis=-1, keepdims=True))
                probs = expo * (1.0 / jnp.sum(expo, axis=-1, keepdims=True))
                outs.append(dot(probs.astype(BF16), v_ref[:stop, :]))
            att_ref[start:stop, lanes] = jnp.where(low_half, outs[0], outs[1]).astype(BF16)
            return 0

        lax.fori_loop(first, last, pair, 0)

    def emit(blk):
        first = q_units + 1
        out = None
        for number in range(o_units):
            cols = slice(number * UNIT, (number + 1) * UNIT)
            piece = dot_nt(att_ref[blk * ROWS : (blk + 1) * ROWS, cols], weights[first + number])
            out = piece if out is None else out + piece
        part[blk] = out.astype(BF16)
        summer.begin(blk)

    def finish(blk):
        for row, values in summer.end(blk):
            rows_at = pl.ds(row, ROWS // 2)
            added = values[blk]
            sum_ref[rows_at, :] = added
            stream = x_ref[rows_at, :].astype(F32) + added.astype(F32)
            b_ref[rows_at, :] = (normed(stream) * gains[1:2, :]).astype(BF16)

    def ready(unit):
        return split(depth) * (unit + 1) - 1 + gather.latency()

    pairs = q_ref.shape[1] // LANES
    schedule = []
    for unit in range(q_units + 1):
        schedule.append((ready(unit), functools.partial(project, unit)))
    for unit in range(q_units + 1, q_units + 1 + o_units):
        schedule.append((ready(unit), functools.partial(load, unit)))
    now = ready(q_units) + 1
    sent = ready(q_units + o_units)
    for blk in range(blocks):
        steps = 1 + blk // 2
        each = -(-pairs // steps)
        for first in range(0, pairs, each):
            schedule.append(
                (now, functools.partial(attend, blk, first, min(pairs, first + each)))
            )
            now += 1
        sent = max(sent + 1, now)
        schedule.append((sent, functools.partial(emit, blk)))
        schedule.append((sent + 1, functools.partial(summer.middle, blk)))
        schedule.append((sent + 4, functools.partial(summer.late, blk)))
        schedule.append((sent + 5, functools.partial(finish, blk)))
    schedule.sort(key=lambda item: item[0])
    length = max(pieces + gather.latency() + 1, sent + 6)

    for step in range(1, count):
        gain_copy(step).start()

    def body(time, _):
        gather.tick(time)
        pl.when(time == 0)(spread_gains)

        @pl.when(time < blocks)
        def _():
            norm_block(time)

        for when, work in schedule:
            pl.when(time == when)(work)
        return 0

    lax.fori_loop(0, length, body, 0)
    for blk in range(blocks):
        summer.drain(blk)
    for step in range(1, count):
        gain_copy(step).wait_send()


def attend(tokens, own, gain_rows, cols, rows_of, cosine, sine, depth, pieces, q_units, o_units):
    token_count, width = tokens.shape
    units, rows, _ = own.shape
    blocks, half = token_count // ROWS, ROWS // 2
    q_width = q_units * UNIT
    kv_width = UNIT // 2
    sum_bufs, sum_sems = TensorSum.scratch(blocks, half, width)
    count = depth * FOLD

    def out(*shape):
        return jax.ShapeDtypeStruct(shape, BF16)

    return pl.pallas_call(
        functools.partial(attend_kernel, (depth, pieces, q_units, o_units)),
        out_shape=(
            out(units, width, UNIT),
            out(token_count, width),
            out(token_count, q_width),
            out(token_count, kv_width),
            out(token_count, kv_width),
            out(token_count, q_width),
            out(token_count, width),
            out(token_count, width),
            jax.ShapeDtypeStruct((8, width), F32),
        ),
        in_specs=[VMEM_SPEC] * 7,
        out_specs=[HBM_SPEC] + [VMEM_SPEC] * 8,
        scratch_shapes=[
            VMEM((count, 8, rows), F32),
            VMEM((q_units + 1 + o_units, width, UNIT), BF16),
            VMEM((ROWS, token_count), F32),
            VMEM((blocks, ROWS, width), BF16),
            *sum_bufs,
            *sum_sems,
            *Gather.scratch(pieces, depth),
            DMA((count,)),
            DMA((count,)),
            DMA,
        ],
        compiler_params=pltpu.CompilerParams(
            collective_id=0, has_side_effects=True, vmem_limit_bytes=60 << 20
        ),
        name="attend",
    )(tokens, own, gain_rows, cols, rows_of, cosine, sine)


class Scatter:
    SLOTS = 4

    def __init__(self, place, rows, units, refs, lag, first=0):
        self.lag = lag
        self.place, self.rows, self.units, self.first = place, rows, units, first
        (
            self.grads,
            self.x_in,
            self.z_in,
            self.kept,
            self.mine,
            self.theirs,
            self.summed,
            self.x_send,
            self.x_recv,
            self.z_send,
            self.z_recv,
            self.load_sem,
            self.keep_sem,
        ) = refs

    @staticmethod
    def scratch(units, depth, rows):
        return [
            VMEM((depth, rows, UNIT), BF16),
            VMEM((depth, rows, UNIT), BF16),
            VMEM((Scatter.SLOTS, depth, rows, UNIT), BF16),
            DMA((units, depth)),
            DMA((units, depth)),
            DMA((units, depth)),
            DMA((units, depth)),
            DMA((2, depth)),
            DMA((Scatter.SLOTS,)),
        ]

    @staticmethod
    def outputs(units, everything, depth, rows):
        return (
            jax.ShapeDtypeStruct((units, depth, rows, UNIT), BF16),
            jax.ShapeDtypeStruct((everything, depth - 1, rows, UNIT), BF16),
            jax.ShapeDtypeStruct((everything, rows, UNIT), BF16),
        )

    def block(self, unit, index):
        start = pl.multiple_of(index * self.rows, self.rows)
        return self.grads.at[unit + self.first, pl.ds(start, self.rows)]

    def over(self, unit, zz):
        p = self.place
        return pltpu.make_async_remote_copy(
            self.block(unit, zz * FOLD + 1 - p.x),
            self.x_in.at[unit, zz],
            self.x_send.at[unit, zz],
            self.x_recv.at[unit, zz],
            device_id={"dp": p.partner},
            device_id_type=MESH,
        )

    def along(self, unit, step):
        p = self.place
        dest = lax.rem(p.z + step, p.depth)
        slot = lax.rem(unit, self.SLOTS)
        return pltpu.make_async_remote_copy(
            self.summed.at[slot, dest],
            self.z_in.at[unit + self.first, step - 1],
            self.z_send.at[unit, step],
            self.z_recv.at[unit, step],
            device_id={"dp": dest * FOLD + p.x},
            device_id_type=MESH,
        )

    def keep(self, unit):
        slot = lax.rem(unit, self.SLOTS)
        return pltpu.make_async_copy(
            self.summed.at[slot, self.place.z], self.kept.at[unit + self.first], self.keep_sem.at[slot]
        )

    def stage(self, step, unit):
        p = self.place

        @pl.when((unit >= 0) & (unit < self.units))
        def _():
            if step == 0:
                for zz in range(p.depth):
                    self.over(unit, zz).start()
            elif step == 1:
                loads = []
                for zz in range(p.depth):
                    loads.append(
                        pltpu.make_async_copy(
                            self.block(unit, zz * FOLD + p.x),
                            self.mine.at[zz],
                            self.load_sem.at[0, zz],
                        )
                    )
                    loads[-1].start()
                for zz in range(p.depth):
                    self.over(unit, zz).wait_recv()
                    loads.append(
                        pltpu.make_async_copy(
                            self.x_in.at[unit, zz], self.theirs.at[zz], self.load_sem.at[1, zz]
                        )
                    )
                    loads[-1].start()
                for copy in loads:
                    copy.wait()
                slot = lax.rem(unit, self.SLOTS)
                for zz in range(p.depth):
                    self.summed[slot, zz] = (
                        self.mine[zz].astype(F32) + self.theirs[zz].astype(F32)
                    ).astype(BF16)
                for way in range(1, p.depth):
                    self.along(unit, way).start()
                self.keep(unit).start()
            else:
                for zz in range(p.depth):
                    self.over(unit, zz).wait_send()
                for way in range(1, p.depth):
                    self.along(unit, way).wait_send()
                self.keep(unit).wait()

    def tick(self, time):
        self.stage(2, time - self.lag - 2)
        self.stage(0, time)
        self.stage(1, time - self.lag)

    def latency(self):
        return self.lag + 3

    def finish(self):
        def unit_end(unit, _):
            for way in range(1, self.place.depth):
                self.along(unit, way).wait_recv()
            return 0

        lax.fori_loop(0, self.units, unit_end, 0)


def feed_kernel(cfg, *refs):
    (
        b_ref,
        cot_ref,
        _,
        g_ref,
        grads_ref,
        x_in,
        z_in,
        kept,
        out_ref,
        db_ref,
        acc_out,
        acc_db,
        weights,
        grad_buf,
        hidden,
        dgu,
        part,
        weight_sem,
        grad_sem,
        z_send,
        z_recv,
        x_send,
        x_recv,
        *scatter_refs,
    ) = refs
    depth, first_unit, chunks, early, base, scatter_units, scatter_every = cfg
    place = Place(depth)
    token_count, width = b_ref.shape
    rows = x_in.shape[2]
    blocks = token_count // ROWS
    tall = 2 * ROWS
    scatter = Scatter(place, rows, scatter_units, (grads_ref, x_in, z_in, kept, *scatter_refs), 1)
    pieces = split(depth) * g_ref.shape[0] - base
    gather = Gather(place, g_ref, rows, pieces, (z_send, z_recv, x_send, x_recv), base)

    def load(chunk, matrix):
        slot = lax.rem(chunk, 2)
        return pltpu.make_async_copy(
            g_ref.at[first_unit + 3 * chunk + matrix],
            weights.at[slot, matrix],
            weight_sem.at[slot, matrix],
        )

    def save(chunk, matrix):
        slot = lax.rem(chunk, 2)
        return pltpu.make_async_copy(
            grad_buf.at[slot, matrix],
            grads_ref.at[3 * chunk + matrix],
            grad_sem.at[slot, matrix],
        )

    for matrix in range(3):
        load(0, matrix).start()
    place.enter()

    def clear(blk, _):
        rows_at = pl.ds(pl.multiple_of(blk * ROWS, ROWS), ROWS)
        acc_out[rows_at, :] = jnp.zeros((ROWS, width), F32)
        acc_db[rows_at, :] = jnp.zeros((ROWS, width), F32)
        return 0

    def hidden_rows(chunk, blk):
        slot = lax.rem(chunk, 2)
        rows_at = pl.ds(pl.multiple_of(blk * tall, tall), tall)
        stream, cot = b_ref[rows_at, :], cot_ref[rows_at, :]
        gate = dot(stream, weights[slot, 0])
        upper = dot(stream, weights[slot, 1])
        grad_hidden = dot(cot, weights[slot, 2])
        sigmoid = jax.nn.sigmoid(gate)
        silu = gate * sigmoid
        hid = (silu * upper).astype(BF16)
        grad_gate = (grad_hidden * upper * sigmoid * (1.0 + gate * (1.0 - sigmoid))).astype(BF16)
        grad_up = (grad_hidden * silu).astype(BF16)
        hidden[rows_at, :] = hid
        dgu[rows_at, :UNIT] = grad_gate
        dgu[rows_at, UNIT:] = grad_up

        def spread(piece, _):
            cols = pl.ds(pl.multiple_of(piece * tall, tall), tall)
            acc_out[rows_at, cols] += dot_nt(hidden[rows_at, :], weights[slot, 2, cols, :])
            acc_db[rows_at, cols] += dot_nt(dgu[rows_at, :UNIT], weights[slot, 0, cols, :]) + dot_nt(
                dgu[rows_at, UNIT:], weights[slot, 1, cols, :]
            )
            return 0

        lax.fori_loop(0, width // tall, spread, 0)

    def weight_grads(chunk):
        slot = lax.rem(chunk, 2)

        def grad_rows(blk, _):
            cols = pl.ds(pl.multiple_of(blk * ROWS, ROWS), ROWS)
            both = dot_tn(b_ref[:, cols], dgu[...])
            grad_buf[slot, 0, cols, :] = both[:, :UNIT].astype(BF16)
            grad_buf[slot, 1, cols, :] = both[:, UNIT:].astype(BF16)
            grad_buf[slot, 2, cols, :] = dot_tn(cot_ref[:, cols], hidden[...]).astype(BF16)
            return 0

        lax.fori_loop(0, width // ROWS, grad_rows, 0)
        for matrix in range(3):
            save(chunk, matrix).start()
        for matrix in range(3):
            save(chunk, matrix).wait()

    halves = token_count // tall
    steps = halves + 1
    ready = [3 * split(depth) * (late + 1) + gather.latency() for late in range(chunks - early)]
    start = max(ready[0], steps * early)
    spread_ticks = steps
    while any(start + spread_ticks * late < when for late, when in enumerate(ready)):
        spread_ticks += 1

    def stored_at(chunk):
        return steps * (chunk + 1) - 1 if chunk < early else (
            start + spread_ticks * (chunk - early) + steps - 1
        )

    scatter_from = max(
        stored_at(unit // 3) - scatter_every * unit for unit in range(scatter_units)
    )
    length = start + spread_ticks * (chunks - early - 1) + steps
    full_turns = -(-(length - scatter_from) // scatter_every)
    scatter_time = length + max(0, scatter_units + scatter.latency() - full_turns)

    def body(time, _):
        gather.tick(time)
        soon = time < steps * early
        since = time - start
        chunk = jnp.where(soon, time // steps, early + since // spread_ticks)
        step = jnp.where(soon, lax.rem(time, steps), lax.rem(since, spread_ticks))
        active = soon | ((since >= 0) & (step < steps) & (chunk < chunks))

        @pl.when(time == 0)
        def _():
            lax.fori_loop(0, blocks, clear, 0)

        @pl.when(active & (step == 0))
        def _():
            for matrix in range(3):
                load(chunk, matrix).wait()

        @pl.when(soon & (step == 0) & (chunk + 1 < early))
        def _():
            for matrix in range(3):
                load(chunk + 1, matrix).start()

        coming = since + 1

        @pl.when((coming >= 0) & (lax.rem(coming, spread_ticks) == 0))
        def _():
            later = early + coming // spread_ticks

            @pl.when(later < chunks)
            def _():
                for matrix in range(3):
                    load(later, matrix).start()

        @pl.when(active & (step < halves))
        def _():
            hidden_rows(chunk, step)

        @pl.when(active & (step == halves))
        def _():
            weight_grads(chunk)

        turn_at = time - scatter_from

        over = time - length

        @pl.when((over >= 0) | ((turn_at >= 0) & (lax.rem(turn_at, scatter_every) == 0)))
        def _():
            scatter.tick(jnp.where(over >= 0, full_turns + over, turn_at // scatter_every))

        return 0

    lax.fori_loop(0, max(length, scatter_time), body, 0)
    for which, (acc, target) in enumerate(((acc_db, db_ref), (acc_out, out_ref))):
        copies = []
        for blk in range(blocks):
            slot = blk % 2
            if blk >= 2:
                copies[blk - 2].wait()
            part[slot] = acc[blk * ROWS : (blk + 1) * ROWS, :].astype(BF16)
            copies.append(
                pltpu.make_async_copy(
                    part.at[slot], target.at[pl.ds(blk * ROWS, ROWS)], grad_sem.at[which, slot]
                )
            )
            copies[-1].start()
        for copy in copies[-2:]:
            copy.wait()
    scatter.finish()


def feed(b, cotangent, gathered, depth, cfg):
    first_unit, chunks, early, base, scatter_units, scatter_every = cfg
    token_count, width = b.shape
    everything = gathered.shape[0]
    rows = width // (depth * FOLD)
    full = jax.ShapeDtypeStruct((token_count, width), BF16)
    pieces = split(depth) * everything - base
    return pl.pallas_call(
        functools.partial(feed_kernel, (depth, *cfg)),
        out_shape=(
            jax.ShapeDtypeStruct(gathered.shape, BF16),
            jax.ShapeDtypeStruct((everything, width, UNIT), BF16),
            *Scatter.outputs(scatter_units, everything, depth, rows),
            full,
            full,
        ),
        in_specs=[VMEM_SPEC, VMEM_SPEC, HBM_SPEC],
        out_specs=[HBM_SPEC] * 7,
        scratch_shapes=[
            VMEM((token_count, width), F32),
            VMEM((token_count, width), F32),
            VMEM((2, 3, width, UNIT), BF16),
            VMEM((2, 3, width, UNIT), BF16),
            VMEM((token_count, UNIT), BF16),
            VMEM((token_count, 2 * UNIT), BF16),
            VMEM((2, ROWS, width), BF16),
            DMA((2, 3)),
            DMA((2, 3)),
            *Gather.scratch(pieces, depth),
            *Scatter.scratch(scatter_units, depth, rows),
        ],
        input_output_aliases={2: 0},
        compiler_params=pltpu.CompilerParams(
            collective_id=1, has_side_effects=True, vmem_limit_bytes=63 << 20
        ),
        name="feed",
    )(b, cotangent, gathered)


def back_kernel(cfg, *refs):
    (
        x_ref,
        q_ref,
        k_ref,
        v_ref,
        att_ref,
        cols_ref,
        rows_ref,
        cos_ref,
        sin_ref,
        gains,
        cot_ref,
        att_sum_ref,
        part_db_ref,
        part_out_ref,
        a_ref,
        g_ref,
        _,
        _,
        _,
        grads_ref,
        x_in,
        z_in,
        kept,
        dx_ref,
        sum_ref,
        gain_ref,
        dx2,
        low,
        weights,
        do,
        dq,
        dkv,
        dk,
        dv,
        part,
        half_in,
        half,
        far_in,
        total,
        back,
        far_db,
        far_out,
        piece,
        mask,
        grad_buf,
        right,
        gain_acc,
        gain_blocks,
        gain_land,
        sum_sends,
        sum_recvs,
        db_sends,
        db_recvs,
        out_sends,
        out_recvs,
        gain_send,
        gain_recv,
        load_sem,
        *scatter_refs,
    ) = refs
    depth, first_grad, scatter_units, q_units, o_units = cfg
    place = Place(depth)
    count = depth * FOLD
    token_count, width = x_ref.shape
    rows = x_in.shape[2]
    kv_width = k_ref.shape[1]
    blocks, short = token_count // ROWS, ROWS // 2
    scatter = Scatter(
        place, rows, scatter_units, (grads_ref, x_in, z_in, kept, *scatter_refs), 2, first_grad
    )
    feed_left = scatter_units - o_units - q_units - 1
    own_grads = first_grad + feed_left
    summer = TensorSum(place, part, (half_in, half, far_in, total, back), (sum_sends, sum_recvs))
    db_sum = StoredSum(
        place,
        part_db_ref,
        (half_in, half, far_db, total, back),
        (db_sends, db_recvs),
        piece,
        load_sem.at[0],
    )
    out_sum = StoredSum(
        place,
        part_out_ref,
        (half_in, half, far_out, total, back),
        (out_sends, out_recvs),
        piece,
        load_sem.at[0],
    )
    lane = lax.broadcasted_iota(jnp.int32, (1, LANES), 1)

    def fetch(pairs):
        copies = [
            pltpu.make_async_copy(src, dst, load_sem.at[number])
            for number, (src, dst) in enumerate(pairs)
        ]
        for copy in copies:
            copy.start()
        for copy in copies:
            copy.wait()

    gain_acc[...] = jnp.zeros_like(gain_acc)
    dk[...] = jnp.zeros_like(dk)
    dv[...] = jnp.zeros_like(dv)
    place.enter()

    def span(blk):
        return pl.ds(pl.multiple_of(blk * ROWS, ROWS), ROWS)

    def middle_grad(blk):
        fetch(
            ((cot_ref.at[span(blk)], part.at[0]), (att_sum_ref.at[span(blk)], part.at[1]))
        )
        for (row, values), inner in zip(db_sum.end(blk), (place.core, 1 - place.core)):
            at = pl.ds(row, short)
            inside = pl.ds(pl.multiple_of(inner * short, short), short)
            middle = x_ref[at, :].astype(F32) + part[1, inside, :].astype(F32)
            inverse = lax.rsqrt(jnp.mean(middle * middle, axis=-1, keepdims=True) + EPS_NORM)
            normal = middle * inverse
            grad = values[blk].astype(F32)
            gain_acc[1:2, :] += jnp.sum(grad * normal, axis=0, keepdims=True)
            scaled = grad * gains[1:2, :]
            centre = jnp.mean(scaled * normal, axis=-1, keepdims=True)
            result = part[0, inside, :].astype(F32) + inverse * (scaled - normal * centre)
            dx2[at, :] = result
            low[at, :] = result.astype(BF16)
        db_sum.drain(blk)
        at = span(blk)
        for unit in range(o_units):
            do[at, unit * UNIT : (unit + 1) * UNIT] = dot(low[at, :], weights[unit]).astype(BF16)

    def first_weights():
        fetch([(g_ref.at[q_units + 1 + unit], weights.at[unit]) for unit in range(o_units)])

    def save_grad(number):
        for unit in range(o_units):

            @pl.when(number == unit)
            def _():
                right[...] = att_ref[:, unit * UNIT : (unit + 1) * UNIT]

        for unit in range(q_units):

            @pl.when(number == o_units + unit)
            def _():
                right[...] = dq[:, unit * UNIT : (unit + 1) * UNIT]

        @pl.when(number == o_units + q_units)
        def _():
            right[...] = dkv[...]

        def block(blk, _):
            cols = span(blk)
            grad_buf[cols, :] = dot_tn(low[:, cols], right[...]).astype(BF16)
            return 0

        lax.fori_loop(0, width // ROWS, block, 0)
        fetch([(grad_buf, grads_ref.at[own_grads + number])])

    def second_weights():
        fetch(
            [(a_ref, low)]
            + [(g_ref.at[unit], weights.at[unit]) for unit in range(q_units + 1)]
        )

    def attention_heads(blk, first, last, stop):
        at = span(blk)

        @pl.when(first == 0)
        def _():
            key = lax.broadcasted_iota(jnp.int32, (stop, ROWS), 0)
            query_at = lax.broadcasted_iota(jnp.int32, (stop, ROWS), 1) + blk * ROWS
            same = cols_ref[:stop, 1:2] == rows_ref[0:1, at]
            allowed = (same & (key <= query_at)) | (key == query_at)
            mask[:stop, :] = jnp.where(allowed, 0.0, NEG_FILL)

        def head(index, _):
            lanes = pl.ds(pl.multiple_of(index // 2 * LANES, LANES), LANES)
            keep = lane // HEAD_SIZE == lax.rem(index, 2)
            query, grad = q_ref[at, lanes], do[at, lanes]
            query = jnp.where(keep, query, jnp.zeros_like(query))
            grad = jnp.where(keep, grad, jnp.zeros_like(grad))
            scores = dot_nt(k_ref[:stop, :], query) * HEAD_SIZE ** (-0.5)
            scores = jnp.where(mask[:stop, :] < 0, NEG_FILL, scores)
            expo = jnp.exp(scores - jnp.max(scores, axis=0, keepdims=True))
            probs = expo * (1.0 / jnp.sum(expo, axis=0, keepdims=True))
            grad_probs = dot_nt(v_ref[:stop, :], grad)
            centre = jnp.sum(probs * grad_probs, axis=0, keepdims=True)
            grad_scores = (probs * (grad_probs - centre)).astype(BF16)
            dv[:stop, :] += dot(probs.astype(BF16), grad)
            dk[:stop, :] += dot(grad_scores, query)
            out = dot_tn(grad_scores, k_ref[:stop, :]) * HEAD_SIZE ** (-0.5)
            out = turn(out, cos_ref[at, :], sin_ref[at, :], True).astype(BF16)
            dq[at, lanes] = jnp.where(keep, out, dq[at, lanes])
            return 0

        lax.fori_loop(first, last, head, 0)

    def input_part(blk):
        at = span(blk)
        dkv[at, :kv_width] = turn(
            dk[at, :] * HEAD_SIZE ** (-0.5), cos_ref[at, :], sin_ref[at, :], True
        ).astype(BF16)
        dkv[at, kv_width:] = dv[at, :].astype(BF16)
        out = dot_nt(dkv[at, :], weights[q_units])
        for unit in range(q_units):
            out = out + dot_nt(dq[at, unit * UNIT : (unit + 1) * UNIT], weights[unit])
        part[blk] = out.astype(BF16)
        summer.begin(blk)

    def finish(blk):
        for row, values in summer.end(blk):
            at = pl.ds(row, short)
            grad = values[blk].astype(F32)
            stream = x_ref[at, :].astype(F32)
            inverse = lax.rsqrt(jnp.mean(stream * stream, axis=-1, keepdims=True) + EPS_NORM)
            normal = stream * inverse
            gain_acc[0:1, :] += jnp.sum(grad * normal, axis=0, keepdims=True)
            scaled = grad * gains[0:1, :]
            centre = jnp.mean(scaled * normal, axis=-1, keepdims=True)
            dx2[at, :] += inverse * (scaled - normal * centre)
        summer.drain(blk)
        part[blk] = dx2[span(blk), :].astype(BF16)
        fetch([(part.at[blk], dx_ref.at[span(blk)])])

    def out_end(blk):
        fetch([(att_sum_ref.at[span(blk)], part.at[blk])])
        for (row, values), inner in zip(out_sum.end(blk), (place.core, 1 - place.core)):
            inside = pl.ds(pl.multiple_of(inner * short, short), short)
            part[blk, inside, :] = (
                x_ref[pl.ds(row, short), :].astype(F32)
                + part[blk, inside, :].astype(F32)
                + values[blk].astype(F32)
            ).astype(BF16)
        out_sum.drain(blk)
        fetch([(part.at[blk], sum_ref.at[span(blk)])])

    heads = q_ref.shape[1] // HEAD_SIZE
    swapped = 1 + blocks + o_units
    attention_at = 3
    parts_at = max(2 + blocks + attention_at - 1, swapped, 7)
    second_at = attention_at + 2 * blocks
    kv_at = max(second_at + q_units, parts_at + blocks)
    hold = max(
        0,
        swapped + 1 - feed_left,
        second_at + 1 - (feed_left + o_units),
        kv_at + 1 - (scatter_units - 1),
    )
    gains_at = parts_at + blocks + 4
    length = max(gains_at + 1, scatter_units + hold + scatter.latency())

    def each_block(work):
        def step(number, _):
            work(blocks - 1 - number)
            return 0

        lax.fori_loop(0, blocks, step, 0)

    def open_sums():
        each_block(db_sum.begin)
        first_weights()
        each_block(db_sum.middle)

    def attention_step(time):
        index = time - attention_at
        blk = blocks - 1 - index // 2
        first = lax.rem(index, 2) * (heads // 2)
        half_way = blocks // 2

        @pl.when(blk >= half_way)
        def _():
            attention_heads(blk, first, first + heads // 2, token_count)

        @pl.when(blk < half_way)
        def _():
            attention_heads(blk, first, first + heads // 2, token_count // 2)

    def steps(time):
        def blockwise(start, work):
            @pl.when((time >= start) & (time < start + blocks))
            def _():
                work(blocks - 1 - (time - start))

        pl.when(time == 0)(open_sums)
        blockwise(1, db_sum.late)
        blockwise(2, middle_grad)
        blockwise(3, out_sum.begin)
        blockwise(4, out_sum.middle)
        blockwise(6, out_sum.late)
        blockwise(7, out_end)

        @pl.when((time >= attention_at) & (time < second_at))
        def _():
            attention_step(time)

        o_at = swapped - o_units + 1
        number = jnp.where(
            time < second_at,
            time - o_at,
            jnp.where(time < second_at + q_units, time - second_at + o_units, o_units + q_units),
        )

        @pl.when(
            ((time >= o_at) & (time < o_at + o_units))
            | ((time >= second_at) & (time < second_at + q_units))
            | (time == kv_at)
        )
        def _():
            save_grad(number)

        pl.when(time == swapped)(second_weights)
        blockwise(parts_at, input_part)
        blockwise(parts_at + 1, summer.middle)
        blockwise(parts_at + 3, summer.late)
        blockwise(parts_at + 4, finish)

    def gain_copy(step):
        dest = lax.rem(place.me + step, count)
        return pltpu.make_async_remote_copy(
            gain_blocks.at[dest],
            gain_land.at[place.me],
            gain_send.at[step],
            gain_recv.at[place.me],
            device_id={"dp": dest},
            device_id_type=MESH,
        )

    def gain_arrival(source):
        return pltpu.make_async_remote_copy(
            gain_blocks.at[0],
            gain_land.at[source],
            gain_send.at[0],
            gain_recv.at[source],
            device_id={"dp": place.partner},
            device_id_type=MESH,
        )

    def send_gains():
        for source in range(count):
            gain_blocks[source] = gain_acc[:, source * rows : (source + 1) * rows]
        for step in range(1, count):
            gain_copy(step).start()

    def body(time, _):
        scatter.tick(time - hold)
        steps(time)
        pl.when(time == gains_at)(send_gains)
        return 0

    lax.fori_loop(0, length, body, 0)
    summed = gain_blocks[place.me]
    for step in range(1, count):
        source = lax.rem(place.me + step, count)
        gain_arrival(source).wait_recv()
        summed = summed + gain_land[source]
    gain_ref[...] = summed
    for step in range(1, count):
        gain_copy(step).wait_send()
    scatter.finish()


def attend_back(
    tokens, q, k, v, att, cols, rows_of, cosine, sine, gains, cotangent, att_sum, part_db,
    part_out, a, gathered, grads, z_in, kept, depth, first_grad, q_units, o_units,
):
    token_count, width = tokens.shape
    rows = width // (depth * FOLD)
    blocks, half = token_count // ROWS, ROWS // 2
    q_width, kv_width = q.shape[1], k.shape[1]
    scatter_units = grads.shape[0] - first_grad
    sum_bufs, sum_sems = TensorSum.scratch(blocks, half, width)
    count = depth * FOLD
    wide = max(q_units + 1, o_units)
    return pl.pallas_call(
        functools.partial(back_kernel, (depth, first_grad, scatter_units, q_units, o_units)),
        out_shape=(
            jax.ShapeDtypeStruct(grads.shape, BF16),
            *Scatter.outputs(scatter_units, grads.shape[0], depth, rows),
            jax.ShapeDtypeStruct((token_count, width), BF16),
            jax.ShapeDtypeStruct((token_count, width), BF16),
            jax.ShapeDtypeStruct((8, rows), F32),
        ),
        in_specs=[VMEM_SPEC] * 10 + [HBM_SPEC] * 9,
        out_specs=[HBM_SPEC] * 6 + [VMEM_SPEC],
        scratch_shapes=[
            VMEM((token_count, width), F32),
            VMEM((token_count, width), BF16),
            VMEM((wide, width, UNIT), BF16),
            VMEM((token_count, q_width), BF16),
            VMEM((token_count, q_width), BF16),
            VMEM((token_count, 2 * kv_width), BF16),
            VMEM((token_count, kv_width), F32),
            VMEM((token_count, kv_width), F32),
            VMEM((blocks, ROWS, width), BF16),
            *sum_bufs,
            VMEM((blocks, half, width), BF16),
            VMEM((blocks, half, width), BF16),
            VMEM((half, width), BF16),
            VMEM((token_count, ROWS), F32),
            VMEM((width, UNIT), BF16),
            VMEM((token_count, UNIT), BF16),
            VMEM((8, width), F32),
            VMEM((count, 8, rows), F32),
            VMEM((count, 8, rows), F32),
            *sum_sems,
            *sum_sems,
            *sum_sems,
            DMA((count,)),
            DMA((count,)),
            DMA((8,)),
            *Scatter.scratch(scatter_units, depth, rows),
        ],
        input_output_aliases={16: 0, 17: 2, 18: 3},
        compiler_params=pltpu.CompilerParams(
            collective_id=2, has_side_effects=True, vmem_limit_bytes=63 << 20
        ),
        name="attend_back",
    )(
        tokens, q, k, v, att, cols, rows_of, cosine, sine, gains, cotangent, att_sum, part_db,
        part_out, a, gathered, grads, z_in, kept,
    )


def settle_kernel(kept_ref, z_ref, gate_ref, up_ref, down_ref):
    steps = z_ref.shape[1]
    for number, out_ref in enumerate((gate_ref, up_ref, down_ref)):
        total = kept_ref[number].astype(F32)
        for step in range(steps):
            total = total + z_ref[number, step].astype(F32)
        out_ref[...] = total if number < 2 else total.T


def settle(kept, z_in, chunks):
    _, rows, cols = kept.shape
    steps = z_in.shape[1]
    wide = pl.BlockSpec((rows, cols), lambda i: (0, i))
    return pl.pallas_call(
        settle_kernel,
        grid=(chunks,),
        out_shape=(
            jax.ShapeDtypeStruct((rows, chunks * cols), F32),
            jax.ShapeDtypeStruct((rows, chunks * cols), F32),
            jax.ShapeDtypeStruct((chunks * cols, rows), F32),
        ),
        in_specs=[
            pl.BlockSpec((3, rows, cols), lambda i: (i, 0, 0)),
            pl.BlockSpec((3, steps, rows, cols), lambda i: (i, 0, 0, 0)),
        ],
        out_specs=[wide, wide, pl.BlockSpec((cols, rows), lambda i: (i, 0))],
        name="settle",
    )(kept, z_in)


def shards(
    depth,
    tokens,
    attention_gain,
    query_matrix,
    key_matrix,
    value_matrix,
    output_weight,
    feed_gain,
    gate_weight,
    up_weight,
    down_weight,
    sequence_lengths,
    block_mask,
    cotangent,
):
    token_count, width = tokens.shape
    rows, q_width = query_matrix.shape
    kv_width = key_matrix.shape[1]
    heads_kv = kv_width // HEAD_SIZE
    groups = q_width // kv_width
    feed_width = gate_weight.shape[1]
    chunks = feed_width // UNIT
    q_units = q_width // UNIT

    def pair(cols):
        return cols.reshape(-1, heads_kv, groups, HEAD_SIZE).swapaxes(1, 2).reshape(-1, q_width)

    def unpair(cols):
        return cols.reshape(-1, groups, heads_kv, HEAD_SIZE).swapaxes(1, 2).reshape(-1, q_width)

    def units_of(cols):
        return cols.reshape(rows, -1, UNIT).swapaxes(0, 1)

    feed_units = jnp.stack(
        [units_of(gate_weight), units_of(up_weight), units_of(down_weight.T)], axis=1
    ).reshape(3 * chunks, rows, UNIT)
    own = jnp.concatenate(
        [
            units_of(pair(query_matrix)),
            units_of(jnp.concatenate([key_matrix, value_matrix], axis=1)),
            units_of(pair(output_weight.T)),
            feed_units,
        ],
        axis=0,
    )
    sequence, position, valid = token_layout(sequence_lengths[0], token_count, BLOCK)
    query_code, key_code = slot_codes(sequence, valid, block_mask, BLOCK)
    cols = jnp.stack([query_code, key_code], axis=1)
    rows_of = jnp.stack([query_code, key_code], axis=0)
    cosine, sine = rope_tables(position, HEAD_SIZE)
    wide_cos = jnp.concatenate([cosine] * 4, axis=1)
    wide_sin = jnp.concatenate([-sine, sine] * 2, axis=1)
    gain_rows = jnp.concatenate(
        [
            attention_gain.astype(F32)[None],
            feed_gain.astype(F32)[None],
            jnp.zeros((6, rows), F32),
        ],
        axis=0,
    )
    first_unit = 2 * q_units + 1
    pieces = split(depth) * (first_unit + 3 * EARLY_CHUNKS)
    gathered, a, q, k, v, att, att_sum, b, gains = attend(
        tokens, own, gain_rows, cols, rows_of, wide_cos, wide_sin, depth, pieces, q_units, q_units
    )
    gathered, grads, _, z_in, kept, part_out, part_db = feed(
        b,
        cotangent,
        gathered,
        depth,
        (first_unit, chunks, EARLY_CHUNKS, pieces, EARLY_UNITS, SCATTER_EVERY),
    )
    _, _, z_in, kept, input_grad, block_output, gain_grads = attend_back(
        tokens, q, k, v, att, cols, rows_of, wide_cos, wide_sin, gains, cotangent, att_sum,
        part_db, part_out, a, gathered, grads, z_in, kept, depth, EARLY_UNITS, q_units, q_units,
    )
    gate_grad, up_grad, down_grad = settle(kept, z_in, chunks)
    late = kept[3 * chunks :].astype(F32) + jnp.sum(z_in[3 * chunks :].astype(F32), axis=1)

    def row_of(units):
        return units.swapaxes(0, 1).reshape(rows, -1)

    out_grad = row_of(late[:q_units]).T
    kv_grad = late[2 * q_units]
    out_grad = out_grad.reshape(groups, heads_kv, HEAD_SIZE, rows).swapaxes(0, 1)
    return (
        block_output,
        input_grad.astype(F32),
        gain_grads[0],
        unpair(row_of(late[q_units : 2 * q_units])),
        kv_grad[:, :kv_width],
        kv_grad[:, kv_width:],
        out_grad.reshape(q_width, rows),
        gain_grads[1],
        gate_grad,
        up_grad,
        down_grad,
    )


def solution(mesh):
    in_specs = (
        P("dp", None),
        P("dp"),
        P("dp", "tensor"),
        P("dp", "tensor"),
        P("dp", "tensor"),
        P("tensor", "dp"),
        P("dp"),
        P("dp", "tensor"),
        P("dp", "tensor"),
        P("tensor", "dp"),
        P("dp", None),
        P("dp", None),
        P("dp", None),
    )
    out_specs = (
        P("dp", None),
        P("dp", None),
        P("dp"),
        P("dp", "tensor"),
        P("dp", "tensor"),
        P("dp", "tensor"),
        P("tensor", "dp"),
        P("dp"),
        P("dp", "tensor"),
        P("dp", "tensor"),
        P("tensor", "dp"),
    )
    return jax.shard_map(
        functools.partial(shards, mesh.shape["dp"] // FOLD),
        mesh=mesh,
        in_specs=in_specs,
        out_specs=out_specs,
        check_vma=False,
    )
```

```python
import functools

import jax
import jax.numpy as jnp
from jax import lax
from jax.experimental import pallas as pl
from jax.experimental.pallas import tpu as pltpu
from jax.sharding import PartitionSpec as P

HEAD_SIZE = 64
BLOCK = 128
LANES = 128
EPS_NORM = 1e-05
THETA_BASE = 500000.0
NEG_FILL = -1e30
UNIT = 256
ROWS = 256
FOLD = 2
XFIRST = 6
MESH = pl.DeviceIdType.MESH
VMEM = pltpu.VMEM
DMA = pltpu.SemaphoreType.DMA
HBM_SPEC = pl.BlockSpec(memory_space=pl.ANY)
VMEM_SPEC = pl.BlockSpec(memory_space=pltpu.VMEM)
F32 = jnp.float32
BF16 = jnp.bfloat16


EARLY_CHUNKS = 7
EARLY_UNITS = 10
ATTENTION_STEPS = 3
SCATTER_EVERY = 2


def split(depth):
    return 2 if depth <= 8 else 1


def token_layout(lengths_row, total, block):
    blocks_per = (lengths_row + block - 1) // block
    offsets = jnp.cumsum(blocks_per) - blocks_per
    first_token = offsets * block
    indices = jnp.arange(total, dtype=jnp.int32)
    member = (indices[:, None] >= first_token[None, :]) & (blocks_per[None, :] > 0)
    sequence = jnp.sum(member.astype(jnp.int32), axis=1) - 1
    select = sequence[:, None] == jnp.arange(lengths_row.shape[0], dtype=jnp.int32)[None, :]
    begins = jnp.sum(jnp.where(select, first_token[None, :], 0), axis=1)
    limits = jnp.sum(jnp.where(select, lengths_row[None, :], 0), axis=1)
    position = indices - begins
    return (sequence, position, position < limits)


def slot_codes(sequence, valid, mask_blocks, block):
    blocks = mask_blocks.shape[0]
    index = jnp.arange(blocks, dtype=jnp.int32)
    own = jnp.max(jnp.where(index[:, None] == index[None, :], mask_blocks, 0), axis=1)
    live = jnp.broadcast_to(own[:, None] > 0, (blocks, block)).reshape(blocks * block)
    query_code = jnp.where(live, sequence, -1)
    key_code = jnp.where(valid, sequence, -2)
    return query_code, key_code


def rope_tables(position, head_dim):
    freqs = THETA_BASE ** (-jnp.arange(head_dim // 2, dtype=F32) * 2.0 / head_dim)
    angles = position.astype(F32)[:, None] * freqs[None, :]
    return (jnp.cos(angles), jnp.sin(angles))


def dot(left, right):
    return jnp.dot(left, right, preferred_element_type=F32)


def dot_nt(left, right):
    return lax.dot_general(left, right, (((1,), (1,)), ((), ())), preferred_element_type=F32)


def dot_tn(left, right):
    return lax.dot_general(left, right, (((0,), (0,)), ((), ())), preferred_element_type=F32)


class Place:
    def __init__(self, depth):
        self.depth = depth
        self.me = lax.axis_index("dp")
        self.z = self.me // FOLD
        self.x = self.me % FOLD
        self.right = self.me + FOLD
        self.left = self.me - FOLD
        self.partner = self.z * FOLD + (1 - self.x)
        member = lax.axis_index("tensor")
        self.core = member % 2
        row = member // 2
        self.other = row * 2 + (1 - self.core)
        self.across = (1 - row) * 2 + self.core

    def enter(self):
        count = self.depth * FOLD
        barrier = pltpu.get_barrier_semaphore()
        for step in range(1, count):
            pl.semaphore_signal(
                barrier,
                1,
                device_id={"dp": lax.rem(self.me + step, count)},
                device_id_type=MESH,
            )
        for peer in (self.other, self.across):
            pl.semaphore_signal(barrier, 1, device_id={"tensor": peer}, device_id_type=MESH)
        pl.semaphore_wait(barrier, count + 1)


class Gather:
    def __init__(self, place, g_ref, rows, pieces, sems, base=0):
        self.place, self.g, self.rows, self.pieces, self.base = place, g_ref, rows, pieces, base
        self.z_send, self.z_recv, self.x_send, self.x_recv = sems

    @staticmethod
    def scratch(pieces, depth):
        return [
            DMA((pieces, 2, depth, FOLD)),
            DMA((pieces, depth, FOLD)),
            DMA((pieces, depth)),
            DMA((pieces, depth)),
        ]

    def block(self, piece, index):
        whole, parts = piece + self.base, split(self.place.depth)
        size = self.rows // parts
        start = pl.multiple_of(index * self.rows + lax.rem(whole, parts) * size, size)
        return self.g.at[whole // parts, pl.ds(start, size)]

    def along(self, piece, zz, xx, way):
        p = self.place
        ref = self.block(piece, zz * FOLD + xx)
        return pltpu.make_async_remote_copy(
            ref,
            ref,
            self.z_send.at[piece, way, zz, xx],
            self.z_recv.at[piece, zz, xx],
            device_id={"dp": p.left if way else p.right},
            device_id_type=MESH,
        )

    def over(self, piece, zz, incoming=False):
        p = self.place
        ref = self.block(piece, zz * FOLD + (1 - p.x if incoming else p.x))
        return pltpu.make_async_remote_copy(
            ref,
            ref,
            self.x_send.at[piece, zz],
            self.x_recv.at[piece, zz],
            device_id={"dp": p.partner},
            device_id_type=MESH,
        )

    def lanes(self, wide):
        return range(FOLD) if wide else (self.place.x,)

    def send_both(self, piece, zz, wide):
        p, last = self.place, self.place.depth - 1

        @pl.when(p.z < last)
        def _():
            for xx in self.lanes(wide):
                self.along(piece, zz, xx, 0).start()

        @pl.when(p.z > 0)
        def _():
            for xx in self.lanes(wide):
                self.along(piece, zz, xx, 1).start()

    def forward(self, piece, step, wide):
        p, last = self.place, self.place.depth - 1

        @pl.when(p.z >= step)
        def _():
            zz = p.z - step
            for xx in self.lanes(wide):
                self.along(piece, zz, xx, 0).wait_recv()

            @pl.when(p.z < last)
            def _():
                for xx in self.lanes(wide):
                    self.along(piece, zz, xx, 0).start()

            if not wide:
                self.over(piece, zz).start()

        @pl.when(p.z + step <= last)
        def _():
            zz = p.z + step
            for xx in self.lanes(wide):
                self.along(piece, zz, xx, 1).wait_recv()

            @pl.when(p.z > 0)
            def _():
                for xx in self.lanes(wide):
                    self.along(piece, zz, xx, 1).start()

            if not wide:
                self.over(piece, zz).start()

    def drain(self, piece, wide):
        p, last = self.place, self.place.depth - 1
        for zz in range(p.depth):

            @pl.when((p.z >= zz) & (p.z < last))
            def _():
                for xx in self.lanes(wide):
                    self.along(piece, zz, xx, 0).wait_send()

            @pl.when((p.z <= zz) & (p.z > 0))
            def _():
                for xx in self.lanes(wide):
                    self.along(piece, zz, xx, 1).wait_send()

    def stage(self, step, piece):
        p, depth = self.place, self.place.depth

        def slow_first():
            if step == 0:
                self.send_both(piece, p.z, False)
                self.over(piece, p.z).start()
            elif step < depth:
                self.forward(piece, step, False)
            else:
                for zz in range(depth):
                    self.over(piece, zz, True).wait_recv()
                for zz in range(depth):
                    self.over(piece, zz).wait_send()
                self.drain(piece, False)

        def fast_first():
            if step == 0:
                self.over(piece, p.z).start()
            elif step == 1:
                self.over(piece, p.z, True).wait_recv()
                self.send_both(piece, p.z, True)
            else:
                self.forward(piece, step - 1, True)
                if step == depth:
                    self.over(piece, p.z).wait_send()
                    self.drain(piece, True)

        inside = (piece >= 0) & (piece < self.pieces)
        fast = lax.rem(piece + self.base, XFIRST) == XFIRST - 1
        pl.when(inside & jnp.logical_not(fast))(slow_first)
        pl.when(inside & fast)(fast_first)

    def latency(self):
        return self.place.depth + 1

    def tick(self, time):
        depth = self.place.depth
        for step in range(depth):
            self.stage(step, time - step)
        self.stage(depth, time - depth - 1)


class TensorSum:
    def __init__(self, place, part, bufs, sems):
        self.place, self.part = place, part
        self.half_in, self.half, self.far_in, self.total, self.back = bufs
        self.sends, self.recvs = sems

    @staticmethod
    def scratch(blocks, half, width):
        return [VMEM((blocks, half, width), BF16)] * 5, [DMA((3, blocks)), DMA((3, blocks))]

    def copy(self, step, src, dst, blk):
        p = self.place
        return pltpu.make_async_remote_copy(
            src,
            dst.at[blk],
            self.sends.at[step, blk],
            self.recvs.at[step, blk],
            device_id={"tensor": p.across if step == 1 else p.other},
            device_id_type=MESH,
        )

    def first(self, blk):
        half = self.half.shape[1]
        start = pl.multiple_of((1 - self.place.core) * half, half)
        return self.copy(0, self.part.at[blk, pl.ds(start, half)], self.half_in, blk)

    def second(self, blk):
        return self.copy(1, self.half.at[blk], self.far_in, blk)

    def third(self, blk):
        return self.copy(2, self.total.at[blk], self.back, blk)

    def begin(self, blk):
        self.first(blk).start()

    def middle(self, blk):
        half = self.half.shape[1]
        self.first(blk).wait_recv()
        start = pl.multiple_of(self.place.core * half, half)
        mine = self.part[blk, pl.ds(start, half), :].astype(F32)
        self.half[blk] = (mine + self.half_in[blk].astype(F32)).astype(BF16)
        self.second(blk).start()

    def late(self, blk):
        self.second(blk).wait_recv()
        self.total[blk] = (self.half[blk].astype(F32) + self.far_in[blk].astype(F32)).astype(BF16)
        self.third(blk).start()

    def end(self, blk):
        half = self.half.shape[1]
        self.third(blk).wait_recv()
        core = self.place.core
        return (
            (pl.multiple_of(blk * 2 * half + core * half, half), self.total),
            (pl.multiple_of(blk * 2 * half + (1 - core) * half, half), self.back),
        )

    def drain(self, blk):
        self.first(blk).wait_send()
        self.second(blk).wait_send()
        self.third(blk).wait_send()


class StoredSum(TensorSum):
    def __init__(self, place, part, bufs, sems, piece, sem):
        super().__init__(place, part, bufs, sems)
        self.piece, self.sem = piece, sem

    def rows_of(self, blk, core):
        short = self.half.shape[1]
        return pl.ds(pl.multiple_of(blk * 2 * short + core * short, short), short)

    def first(self, blk):
        src = self.part.at[self.rows_of(blk, 1 - self.place.core)]
        return self.copy(0, src, self.half_in, blk)

    def middle(self, blk):
        copy = pltpu.make_async_copy(
            self.part.at[self.rows_of(blk, self.place.core)], self.piece, self.sem
        )
        copy.start()
        self.first(blk).wait_recv()
        copy.wait()
        self.half[blk] = (self.piece[...].astype(F32) + self.half_in[blk].astype(F32)).astype(BF16)
        self.second(blk).start()


def turn(values, cosine, sine, back=False):
    half = HEAD_SIZE // 2
    lane = lax.broadcasted_iota(jnp.int32, (1, LANES), 1)
    low = lax.rem(lane, HEAD_SIZE) < half
    tiles = []
    for start in range(0, values.shape[1], LANES):
        tile = values[:, start : start + LANES]
        swapped = jnp.where(low, pltpu.roll(tile, LANES - half, 1), pltpu.roll(tile, half, 1))
        if back:
            tiles.append(tile * cosine - swapped * sine)
        else:
            tiles.append(tile * cosine + swapped * sine)
    return tiles[0] if len(tiles) == 1 else jnp.concatenate(tiles, axis=1)


def normed(stream):
    return stream * lax.rsqrt(jnp.mean(stream * stream, axis=-1, keepdims=True) + EPS_NORM)


def attend_kernel(cfg, *refs):
    (
        x_ref,
        w_ref,
        gain_ref,
        cols_ref,
        rows_ref,
        cos_ref,
        sin_ref,
        g_ref,
        a_ref,
        q_ref,
        k_ref,
        v_ref,
        att_ref,
        sum_ref,
        b_ref,
        gains,
        gain_in,
        weights,
        mask,
        part,
        half_in,
        half,
        far_in,
        total,
        back,
        sum_sends,
        sum_recvs,
        z_send,
        z_recv,
        x_send,
        x_recv,
        gain_send,
        gain_recv,
        local_sem,
    ) = refs
    depth, pieces, q_units, o_units = cfg
    place = Place(depth)
    count = depth * FOLD
    token_count, width = x_ref.shape
    rows = w_ref.shape[1]
    blocks = token_count // ROWS
    fill = pltpu.make_async_copy(
        w_ref, g_ref.at[:, pl.ds(pl.multiple_of(place.me * rows, rows), rows)], local_sem
    )
    fill.start()
    place.enter()
    fill.wait()
    gather = Gather(place, g_ref, rows, pieces, (z_send, z_recv, x_send, x_recv))
    summer = TensorSum(place, part, (half_in, half, far_in, total, back), (sum_sends, sum_recvs))

    def gain_copy(step):
        return pltpu.make_async_remote_copy(
            gain_ref,
            gain_in.at[place.me],
            gain_send.at[step],
            gain_recv.at[place.me],
            device_id={"dp": lax.rem(place.me + step, count)},
            device_id_type=MESH,
        )

    def gain_arrival(source):
        return pltpu.make_async_remote_copy(
            gain_ref,
            gain_in.at[source],
            gain_send.at[0],
            gain_recv.at[source],
            device_id={"dp": place.partner},
            device_id_type=MESH,
        )

    lane = lax.broadcasted_iota(jnp.int32, (1, LANES), 1)
    low_half = lane < HEAD_SIZE

    def spread_gains():
        gain_in[place.me] = gain_ref[...]
        for step in range(1, count):
            gain_arrival(lax.rem(place.me + step, count)).wait_recv()
        for source in range(count):
            gains[:, source * rows : (source + 1) * rows] = gain_in[source]

    def norm_block(blk):
        rows_at = pl.ds(pl.multiple_of(blk * ROWS, ROWS), ROWS)
        stream = x_ref[rows_at, :].astype(F32)
        a_ref[rows_at, :] = (normed(stream) * gains[0:1, :]).astype(BF16)

    def load(unit):
        copy = pltpu.make_async_copy(g_ref.at[unit], weights.at[unit], local_sem)
        copy.start()
        copy.wait()

    def project(unit):
        load(unit)

        def block(blk, _):
            rows_at = pl.ds(pl.multiple_of(blk * ROWS, ROWS), ROWS)
            cosine, sine = cos_ref[rows_at, :], sin_ref[rows_at, :]
            out = dot(a_ref[rows_at, :], weights[unit])
            if unit < q_units:
                q_ref[rows_at, unit * UNIT : (unit + 1) * UNIT] = turn(out, cosine, sine).astype(
                    BF16
                )
            else:
                kv = k_ref.shape[1]
                k_ref[rows_at, :] = turn(out[:, :kv], cosine, sine).astype(BF16)
                v_ref[rows_at, :] = out[:, kv:].astype(BF16)
            return 0

        lax.fori_loop(0, blocks, block, 0)

    def attend(blk, first, last):
        start, stop = blk * ROWS, (blk + 1) * ROWS
        if first == 0:
            key = lax.broadcasted_iota(jnp.int32, (ROWS, stop), 1)
            query_at = lax.broadcasted_iota(jnp.int32, (ROWS, stop), 0) + start
            same = cols_ref[start:stop, 0:1] == rows_ref[1:2, :stop]
            allowed = (same & (key <= query_at)) | (key == query_at)
            mask[:, :stop] = jnp.where(allowed, 0.0, NEG_FILL)

        def pair(index, _):
            lanes = pl.ds(pl.multiple_of(index * LANES, LANES), LANES)
            query = q_ref[start:stop, lanes]
            outs = []
            for one in (True, False):
                keep = low_half if one else jnp.logical_not(low_half)
                masked = jnp.where(keep, query, jnp.zeros_like(query))
                scores = dot_nt(masked, k_ref[:stop, :]) * HEAD_SIZE ** (-0.5)
                scores = jnp.where(mask[:, :stop] < 0, NEG_FILL, scores)
                expo = jnp.exp(scores - jnp.max(scores, axis=-1, keepdims=True))
                probs = expo * (1.0 / jnp.sum(expo, axis=-1, keepdims=True))
                outs.append(dot(probs.astype(BF16), v_ref[:stop, :]))
            att_ref[start:stop, lanes] = jnp.where(low_half, outs[0], outs[1]).astype(BF16)
            return 0

        lax.fori_loop(first, last, pair, 0)

    def emit(blk):
        first = q_units + 1
        out = None
        for number in range(o_units):
            cols = slice(number * UNIT, (number + 1) * UNIT)
            piece = dot_nt(att_ref[blk * ROWS : (blk + 1) * ROWS, cols], weights[first + number])
            out = piece if out is None else out + piece
        part[blk] = out.astype(BF16)
        summer.begin(blk)

    def finish(blk):
        for row, values in summer.end(blk):
            rows_at = pl.ds(row, ROWS // 2)
            added = values[blk]
            sum_ref[rows_at, :] = added
            stream = x_ref[rows_at, :].astype(F32) + added.astype(F32)
            b_ref[rows_at, :] = (normed(stream) * gains[1:2, :]).astype(BF16)

    def ready(unit):
        return split(depth) * (unit + 1) - 1 + gather.latency()

    pairs = q_ref.shape[1] // LANES
    schedule = []
    for unit in range(q_units + 1):
        schedule.append((ready(unit), functools.partial(project, unit)))
    for unit in range(q_units + 1, q_units + 1 + o_units):
        schedule.append((ready(unit), functools.partial(load, unit)))
    now = ready(q_units) + 1
    sent = ready(q_units + o_units)
    for blk in range(blocks):
        steps = 1 + blk // 2
        each = -(-pairs // steps)
        for first in range(0, pairs, each):
            schedule.append(
                (now, functools.partial(attend, blk, first, min(pairs, first + each)))
            )
            now += 1
        sent = max(sent + 1, now)
        schedule.append((sent, functools.partial(emit, blk)))
        schedule.append((sent + 1, functools.partial(summer.middle, blk)))
        schedule.append((sent + 4, functools.partial(summer.late, blk)))
        schedule.append((sent + 5, functools.partial(finish, blk)))
    schedule.sort(key=lambda item: item[0])
    length = max(pieces + gather.latency() + 1, sent + 6)

    for step in range(1, count):
        gain_copy(step).start()

    def body(time, _):
        gather.tick(time)
        pl.when(time == 0)(spread_gains)

        @pl.when(time < blocks)
        def _():
            norm_block(time)

        for when, work in schedule:
            pl.when(time == when)(work)
        return 0

    lax.fori_loop(0, length, body, 0)
    for blk in range(blocks):
        summer.drain(blk)
    for step in range(1, count):
        gain_copy(step).wait_send()


def attend(tokens, own, gain_rows, cols, rows_of, cosine, sine, depth, pieces, q_units, o_units):
    token_count, width = tokens.shape
    units, rows, _ = own.shape
    blocks, half = token_count // ROWS, ROWS // 2
    q_width = q_units * UNIT
    kv_width = UNIT // 2
    sum_bufs, sum_sems = TensorSum.scratch(blocks, half, width)
    count = depth * FOLD

    def out(*shape):
        return jax.ShapeDtypeStruct(shape, BF16)

    return pl.pallas_call(
        functools.partial(attend_kernel, (depth, pieces, q_units, o_units)),
        out_shape=(
            out(units, width, UNIT),
            out(token_count, width),
            out(token_count, q_width),
            out(token_count, kv_width),
            out(token_count, kv_width),
            out(token_count, q_width),
            out(token_count, width),
            out(token_count, width),
            jax.ShapeDtypeStruct((8, width), F32),
        ),
        in_specs=[VMEM_SPEC] * 7,
        out_specs=[HBM_SPEC] + [VMEM_SPEC] * 8,
        scratch_shapes=[
            VMEM((count, 8, rows), F32),
            VMEM((q_units + 1 + o_units, width, UNIT), BF16),
            VMEM((ROWS, token_count), F32),
            VMEM((blocks, ROWS, width), BF16),
            *sum_bufs,
            *sum_sems,
            *Gather.scratch(pieces, depth),
            DMA((count,)),
            DMA((count,)),
            DMA,
        ],
        compiler_params=pltpu.CompilerParams(
            collective_id=0, has_side_effects=True, vmem_limit_bytes=60 << 20
        ),
        name="attend",
    )(tokens, own, gain_rows, cols, rows_of, cosine, sine)


class Scatter:
    SLOTS = 4

    def __init__(self, place, rows, units, refs, lag, first=0):
        self.lag = lag
        self.place, self.rows, self.units, self.first = place, rows, units, first
        (
            self.grads,
            self.x_in,
            self.z_in,
            self.kept,
            self.mine,
            self.theirs,
            self.summed,
            self.x_send,
            self.x_recv,
            self.z_send,
            self.z_recv,
            self.load_sem,
            self.keep_sem,
        ) = refs

    @staticmethod
    def scratch(units, depth, rows):
        return [
            VMEM((depth, rows, UNIT), BF16),
            VMEM((depth, rows, UNIT), BF16),
            VMEM((Scatter.SLOTS, depth, rows, UNIT), BF16),
            DMA((units, depth)),
            DMA((units, depth)),
            DMA((units, depth)),
            DMA((units, depth)),
            DMA((2, depth)),
            DMA((Scatter.SLOTS,)),
        ]

    @staticmethod
    def outputs(units, everything, depth, rows):
        return (
            jax.ShapeDtypeStruct((units, depth, rows, UNIT), BF16),
            jax.ShapeDtypeStruct((everything, depth - 1, rows, UNIT), BF16),
            jax.ShapeDtypeStruct((everything, rows, UNIT), BF16),
        )

    def block(self, unit, index):
        start = pl.multiple_of(index * self.rows, self.rows)
        return self.grads.at[unit + self.first, pl.ds(start, self.rows)]

    def over(self, unit, zz):
        p = self.place
        return pltpu.make_async_remote_copy(
            self.block(unit, zz * FOLD + 1 - p.x),
            self.x_in.at[unit, zz],
            self.x_send.at[unit, zz],
            self.x_recv.at[unit, zz],
            device_id={"dp": p.partner},
            device_id_type=MESH,
        )

    def along(self, unit, step):
        p = self.place
        dest = lax.rem(p.z + step, p.depth)
        slot = lax.rem(unit, self.SLOTS)
        return pltpu.make_async_remote_copy(
            self.summed.at[slot, dest],
            self.z_in.at[unit + self.first, step - 1],
            self.z_send.at[unit, step],
            self.z_recv.at[unit, step],
            device_id={"dp": dest * FOLD + p.x},
            device_id_type=MESH,
        )

    def keep(self, unit):
        slot = lax.rem(unit, self.SLOTS)
        return pltpu.make_async_copy(
            self.summed.at[slot, self.place.z], self.kept.at[unit + self.first], self.keep_sem.at[slot]
        )

    def stage(self, step, unit):
        p = self.place

        @pl.when((unit >= 0) & (unit < self.units))
        def _():
            if step == 0:
                for zz in range(p.depth):
                    self.over(unit, zz).start()
            elif step == 1:
                loads = []
                for zz in range(p.depth):
                    loads.append(
                        pltpu.make_async_copy(
                            self.block(unit, zz * FOLD + p.x),
                            self.mine.at[zz],
                            self.load_sem.at[0, zz],
                        )
                    )
                    loads[-1].start()
                for zz in range(p.depth):
                    self.over(unit, zz).wait_recv()
                    loads.append(
                        pltpu.make_async_copy(
                            self.x_in.at[unit, zz], self.theirs.at[zz], self.load_sem.at[1, zz]
                        )
                    )
                    loads[-1].start()
                for copy in loads:
                    copy.wait()
                slot = lax.rem(unit, self.SLOTS)
                for zz in range(p.depth):
                    self.summed[slot, zz] = (
                        self.mine[zz].astype(F32) + self.theirs[zz].astype(F32)
                    ).astype(BF16)
                for way in range(1, p.depth):
                    self.along(unit, way).start()
                self.keep(unit).start()
            else:
                for zz in range(p.depth):
                    self.over(unit, zz).wait_send()
                for way in range(1, p.depth):
                    self.along(unit, way).wait_send()
                self.keep(unit).wait()

    def tick(self, time):
        self.stage(2, time - self.lag - 2)
        self.stage(0, time)
        self.stage(1, time - self.lag)

    def latency(self):
        return self.lag + 3

    def finish(self):
        def unit_end(unit, _):
            for way in range(1, self.place.depth):
                self.along(unit, way).wait_recv()
            return 0

        lax.fori_loop(0, self.units, unit_end, 0)


def feed_kernel(cfg, *refs):
    (
        b_ref,
        cot_ref,
        _,
        g_ref,
        grads_ref,
        x_in,
        z_in,
        kept,
        out_ref,
        db_ref,
        acc_out,
        acc_db,
        weights,
        grad_buf,
        hidden,
        dgu,
        part,
        weight_sem,
        grad_sem,
        z_send,
        z_recv,
        x_send,
        x_recv,
        *scatter_refs,
    ) = refs
    depth, first_unit, chunks, early, base, scatter_units, scatter_every = cfg
    place = Place(depth)
    token_count, width = b_ref.shape
    rows = x_in.shape[2]
    blocks = token_count // ROWS
    tall = 2 * ROWS
    scatter = Scatter(place, rows, scatter_units, (grads_ref, x_in, z_in, kept, *scatter_refs), 1)
    pieces = split(depth) * g_ref.shape[0] - base
    gather = Gather(place, g_ref, rows, pieces, (z_send, z_recv, x_send, x_recv), base)

    def load(chunk, matrix):
        slot = lax.rem(chunk, 2)
        return pltpu.make_async_copy(
            g_ref.at[first_unit + 3 * chunk + matrix],
            weights.at[slot, matrix],
            weight_sem.at[slot, matrix],
        )

    def save(chunk, matrix):
        slot = lax.rem(chunk, 2)
        return pltpu.make_async_copy(
            grad_buf.at[slot, matrix],
            grads_ref.at[3 * chunk + matrix],
            grad_sem.at[slot, matrix],
        )

    for matrix in range(3):
        load(0, matrix).start()
    place.enter()

    def clear(blk, _):
        rows_at = pl.ds(pl.multiple_of(blk * ROWS, ROWS), ROWS)
        acc_out[rows_at, :] = jnp.zeros((ROWS, width), F32)
        acc_db[rows_at, :] = jnp.zeros((ROWS, width), F32)
        return 0

    def hidden_rows(chunk, blk):
        slot = lax.rem(chunk, 2)
        rows_at = pl.ds(pl.multiple_of(blk * tall, tall), tall)
        stream, cot = b_ref[rows_at, :], cot_ref[rows_at, :]
        gate = dot(stream, weights[slot, 0])
        upper = dot(stream, weights[slot, 1])
        grad_hidden = dot(cot, weights[slot, 2])
        sigmoid = jax.nn.sigmoid(gate)
        silu = gate * sigmoid
        hid = (silu * upper).astype(BF16)
        grad_gate = (grad_hidden * upper * sigmoid * (1.0 + gate * (1.0 - sigmoid))).astype(BF16)
        grad_up = (grad_hidden * silu).astype(BF16)
        hidden[rows_at, :] = hid
        dgu[rows_at, :UNIT] = grad_gate
        dgu[rows_at, UNIT:] = grad_up

        def spread(piece, _):
            cols = pl.ds(pl.multiple_of(piece * tall, tall), tall)
            acc_out[rows_at, cols] += dot_nt(hidden[rows_at, :], weights[slot, 2, cols, :])
            acc_db[rows_at, cols] += dot_nt(dgu[rows_at, :UNIT], weights[slot, 0, cols, :]) + dot_nt(
                dgu[rows_at, UNIT:], weights[slot, 1, cols, :]
            )
            return 0

        lax.fori_loop(0, width // tall, spread, 0)

    def weight_grads(chunk):
        slot = lax.rem(chunk, 2)

        def grad_rows(blk, _):
            cols = pl.ds(pl.multiple_of(blk * ROWS, ROWS), ROWS)
            both = dot_tn(b_ref[:, cols], dgu[...])
            grad_buf[slot, 0, cols, :] = both[:, :UNIT].astype(BF16)
            grad_buf[slot, 1, cols, :] = both[:, UNIT:].astype(BF16)
            grad_buf[slot, 2, cols, :] = dot_tn(cot_ref[:, cols], hidden[...]).astype(BF16)
            return 0

        lax.fori_loop(0, width // ROWS, grad_rows, 0)
        for matrix in range(3):
            save(chunk, matrix).start()
        for matrix in range(3):
            save(chunk, matrix).wait()

    halves = token_count // tall
    steps = halves + 1
    ready = [3 * split(depth) * (late + 1) + gather.latency() for late in range(chunks - early)]
    start = max(ready[0], steps * early)
    spread_ticks = steps
    while any(start + spread_ticks * late < when for late, when in enumerate(ready)):
        spread_ticks += 1

    def stored_at(chunk):
        return steps * (chunk + 1) - 1 if chunk < early else (
            start + spread_ticks * (chunk - early) + steps - 1
        )

    scatter_from = max(
        stored_at(unit // 3) - scatter_every * unit for unit in range(scatter_units)
    )
    length = start + spread_ticks * (chunks - early - 1) + steps
    full_turns = -(-(length - scatter_from) // scatter_every)
    scatter_time = length + max(0, scatter_units + scatter.latency() - full_turns)

    def body(time, _):
        gather.tick(time)
        soon = time < steps * early
        since = time - start
        chunk = jnp.where(soon, time // steps, early + since // spread_ticks)
        step = jnp.where(soon, lax.rem(time, steps), lax.rem(since, spread_ticks))
        active = soon | ((since >= 0) & (step < steps) & (chunk < chunks))

        @pl.when(time == 0)
        def _():
            lax.fori_loop(0, blocks, clear, 0)

        @pl.when(active & (step == 0))
        def _():
            for matrix in range(3):
                load(chunk, matrix).wait()

        @pl.when(soon & (step == 0) & (chunk + 1 < early))
        def _():
            for matrix in range(3):
                load(chunk + 1, matrix).start()

        coming = since + 1

        @pl.when((coming >= 0) & (lax.rem(coming, spread_ticks) == 0))
        def _():
            later = early + coming // spread_ticks

            @pl.when(later < chunks)
            def _():
                for matrix in range(3):
                    load(later, matrix).start()

        @pl.when(active & (step < halves))
        def _():
            hidden_rows(chunk, step)

        @pl.when(active & (step == halves))
        def _():
            weight_grads(chunk)

        turn_at = time - scatter_from

        over = time - length

        @pl.when((over >= 0) | ((turn_at >= 0) & (lax.rem(turn_at, scatter_every) == 0)))
        def _():
            scatter.tick(jnp.where(over >= 0, full_turns + over, turn_at // scatter_every))

        return 0

    lax.fori_loop(0, max(length, scatter_time), body, 0)
    for which, (acc, target) in enumerate(((acc_db, db_ref), (acc_out, out_ref))):
        copies = []
        for blk in range(blocks):
            slot = blk % 2
            if blk >= 2:
                copies[blk - 2].wait()
            part[slot] = acc[blk * ROWS : (blk + 1) * ROWS, :].astype(BF16)
            copies.append(
                pltpu.make_async_copy(
                    part.at[slot], target.at[pl.ds(blk * ROWS, ROWS)], grad_sem.at[which, slot]
                )
            )
            copies[-1].start()
        for copy in copies[-2:]:
            copy.wait()
    scatter.finish()


def feed(b, cotangent, gathered, depth, cfg):
    first_unit, chunks, early, base, scatter_units, scatter_every = cfg
    token_count, width = b.shape
    everything = gathered.shape[0]
    rows = width // (depth * FOLD)
    full = jax.ShapeDtypeStruct((token_count, width), BF16)
    pieces = split(depth) * everything - base
    return pl.pallas_call(
        functools.partial(feed_kernel, (depth, *cfg)),
        out_shape=(
            jax.ShapeDtypeStruct(gathered.shape, BF16),
            jax.ShapeDtypeStruct((everything, width, UNIT), BF16),
            *Scatter.outputs(scatter_units, everything, depth, rows),
            full,
            full,
        ),
        in_specs=[VMEM_SPEC, VMEM_SPEC, HBM_SPEC],
        out_specs=[HBM_SPEC] * 7,
        scratch_shapes=[
            VMEM((token_count, width), F32),
            VMEM((token_count, width), F32),
            VMEM((2, 3, width, UNIT), BF16),
            VMEM((2, 3, width, UNIT), BF16),
            VMEM((token_count, UNIT), BF16),
            VMEM((token_count, 2 * UNIT), BF16),
            VMEM((2, ROWS, width), BF16),
            DMA((2, 3)),
            DMA((2, 3)),
            *Gather.scratch(pieces, depth),
            *Scatter.scratch(scatter_units, depth, rows),
        ],
        input_output_aliases={2: 0},
        compiler_params=pltpu.CompilerParams(
            collective_id=1, has_side_effects=True, vmem_limit_bytes=63 << 20
        ),
        name="feed",
    )(b, cotangent, gathered)


def back_kernel(cfg, *refs):
    (
        x_ref,
        q_ref,
        k_ref,
        v_ref,
        att_ref,
        cols_ref,
        rows_ref,
        cos_ref,
        sin_ref,
        gains,
        cot_ref,
        att_sum_ref,
        part_db_ref,
        part_out_ref,
        a_ref,
        g_ref,
        _,
        _,
        _,
        grads_ref,
        x_in,
        z_in,
        kept,
        dx_ref,
        sum_ref,
        gain_ref,
        dx2,
        low,
        weights,
        do,
        dq,
        dkv,
        dk,
        dv,
        part,
        half_in,
        half,
        far_in,
        total,
        back,
        far_db,
        far_out,
        piece,
        mask,
        grad_buf,
        right,
        gain_acc,
        gain_blocks,
        gain_land,
        sum_sends,
        sum_recvs,
        db_sends,
        db_recvs,
        out_sends,
        out_recvs,
        gain_send,
        gain_recv,
        load_sem,
        *scatter_refs,
    ) = refs
    depth, first_grad, scatter_units, q_units, o_units = cfg
    place = Place(depth)
    count = depth * FOLD
    token_count, width = x_ref.shape
    rows = x_in.shape[2]
    kv_width = k_ref.shape[1]
    blocks, short = token_count // ROWS, ROWS // 2
    scatter = Scatter(
        place, rows, scatter_units, (grads_ref, x_in, z_in, kept, *scatter_refs), 2, first_grad
    )
    feed_left = scatter_units - o_units - q_units - 1
    own_grads = first_grad + feed_left
    summer = TensorSum(place, part, (half_in, half, far_in, total, back), (sum_sends, sum_recvs))
    db_sum = StoredSum(
        place,
        part_db_ref,
        (half_in, half, far_db, total, back),
        (db_sends, db_recvs),
        piece,
        load_sem.at[0],
    )
    out_sum = StoredSum(
        place,
        part_out_ref,
        (half_in, half, far_out, total, back),
        (out_sends, out_recvs),
        piece,
        load_sem.at[0],
    )
    lane = lax.broadcasted_iota(jnp.int32, (1, LANES), 1)

    def fetch(pairs):
        copies = [
            pltpu.make_async_copy(src, dst, load_sem.at[number])
            for number, (src, dst) in enumerate(pairs)
        ]
        for copy in copies:
            copy.start()
        for copy in copies:
            copy.wait()

    gain_acc[...] = jnp.zeros_like(gain_acc)
    dk[...] = jnp.zeros_like(dk)
    dv[...] = jnp.zeros_like(dv)
    place.enter()

    def span(blk):
        return pl.ds(pl.multiple_of(blk * ROWS, ROWS), ROWS)

    def middle_grad(blk):
        fetch(
            ((cot_ref.at[span(blk)], part.at[0]), (att_sum_ref.at[span(blk)], part.at[1]))
        )
        for (row, values), inner in zip(db_sum.end(blk), (place.core, 1 - place.core)):
            at = pl.ds(row, short)
            inside = pl.ds(pl.multiple_of(inner * short, short), short)
            middle = x_ref[at, :].astype(F32) + part[1, inside, :].astype(F32)
            inverse = lax.rsqrt(jnp.mean(middle * middle, axis=-1, keepdims=True) + EPS_NORM)
            normal = middle * inverse
            grad = values[blk].astype(F32)
            gain_acc[1:2, :] += jnp.sum(grad * normal, axis=0, keepdims=True)
            scaled = grad * gains[1:2, :]
            centre = jnp.mean(scaled * normal, axis=-1, keepdims=True)
            result = part[0, inside, :].astype(F32) + inverse * (scaled - normal * centre)
            dx2[at, :] = result
            low[at, :] = result.astype(BF16)
        db_sum.drain(blk)
        at = span(blk)
        for unit in range(o_units):
            do[at, unit * UNIT : (unit + 1) * UNIT] = dot(low[at, :], weights[unit]).astype(BF16)

    def first_weights():
        fetch([(g_ref.at[q_units + 1 + unit], weights.at[unit]) for unit in range(o_units)])

    def save_grad(number):
        for unit in range(o_units):

            @pl.when(number == unit)
            def _():
                right[...] = att_ref[:, unit * UNIT : (unit + 1) * UNIT]

        for unit in range(q_units):

            @pl.when(number == o_units + unit)
            def _():
                right[...] = dq[:, unit * UNIT : (unit + 1) * UNIT]

        @pl.when(number == o_units + q_units)
        def _():
            right[...] = dkv[...]

        def block(blk, _):
            cols = span(blk)
            grad_buf[cols, :] = dot_tn(low[:, cols], right[...]).astype(BF16)
            return 0

        lax.fori_loop(0, width // ROWS, block, 0)
        fetch([(grad_buf, grads_ref.at[own_grads + number])])

    def second_weights():
        fetch(
            [(a_ref, low)]
            + [(g_ref.at[unit], weights.at[unit]) for unit in range(q_units + 1)]
        )

    def attention_heads(blk, first, last, stop):
        at = span(blk)

        @pl.when(first == 0)
        def _():
            key = lax.broadcasted_iota(jnp.int32, (stop, ROWS), 0)
            query_at = lax.broadcasted_iota(jnp.int32, (stop, ROWS), 1) + blk * ROWS
            same = cols_ref[:stop, 1:2] == rows_ref[0:1, at]
            allowed = (same & (key <= query_at)) | (key == query_at)
            mask[:stop, :] = jnp.where(allowed, 0.0, NEG_FILL)

        def head(index, _):
            lanes = pl.ds(pl.multiple_of(index // 2 * LANES, LANES), LANES)
            keep = lane // HEAD_SIZE == lax.rem(index, 2)
            query, grad = q_ref[at, lanes], do[at, lanes]
            query = jnp.where(keep, query, jnp.zeros_like(query))
            grad = jnp.where(keep, grad, jnp.zeros_like(grad))
            scores = dot_nt(k_ref[:stop, :], query) * HEAD_SIZE ** (-0.5)
            scores = jnp.where(mask[:stop, :] < 0, NEG_FILL, scores)
            expo = jnp.exp(scores - jnp.max(scores, axis=0, keepdims=True))
            probs = expo * (1.0 / jnp.sum(expo, axis=0, keepdims=True))
            grad_probs = dot_nt(v_ref[:stop, :], grad)
            centre = jnp.sum(probs * grad_probs, axis=0, keepdims=True)
            grad_scores = (probs * (grad_probs - centre)).astype(BF16)
            dv[:stop, :] += dot(probs.astype(BF16), grad)
            dk[:stop, :] += dot(grad_scores, query)
            out = dot_tn(grad_scores, k_ref[:stop, :]) * HEAD_SIZE ** (-0.5)
            out = turn(out, cos_ref[at, :], sin_ref[at, :], True).astype(BF16)
            dq[at, lanes] = jnp.where(keep, out, dq[at, lanes])
            return 0

        lax.fori_loop(first, last, head, 0)

    def input_part(blk):
        at = span(blk)
        dkv[at, :kv_width] = turn(
            dk[at, :] * HEAD_SIZE ** (-0.5), cos_ref[at, :], sin_ref[at, :], True
        ).astype(BF16)
        dkv[at, kv_width:] = dv[at, :].astype(BF16)
        out = dot_nt(dkv[at, :], weights[q_units])
        for unit in range(q_units):
            out = out + dot_nt(dq[at, unit * UNIT : (unit + 1) * UNIT], weights[unit])
        part[blk] = out.astype(BF16)
        summer.begin(blk)

    def finish(blk):
        for row, values in summer.end(blk):
            at = pl.ds(row, short)
            grad = values[blk].astype(F32)
            stream = x_ref[at, :].astype(F32)
            inverse = lax.rsqrt(jnp.mean(stream * stream, axis=-1, keepdims=True) + EPS_NORM)
            normal = stream * inverse
            gain_acc[0:1, :] += jnp.sum(grad * normal, axis=0, keepdims=True)
            scaled = grad * gains[0:1, :]
            centre = jnp.mean(scaled * normal, axis=-1, keepdims=True)
            dx2[at, :] += inverse * (scaled - normal * centre)
        summer.drain(blk)
        part[blk] = dx2[span(blk), :].astype(BF16)
        fetch([(part.at[blk], dx_ref.at[span(blk)])])

    def out_end(blk):
        fetch([(att_sum_ref.at[span(blk)], part.at[blk])])
        for (row, values), inner in zip(out_sum.end(blk), (place.core, 1 - place.core)):
            inside = pl.ds(pl.multiple_of(inner * short, short), short)
            part[blk, inside, :] = (
                x_ref[pl.ds(row, short), :].astype(F32)
                + part[blk, inside, :].astype(F32)
                + values[blk].astype(F32)
            ).astype(BF16)
        out_sum.drain(blk)
        fetch([(part.at[blk], sum_ref.at[span(blk)])])

    heads = q_ref.shape[1] // HEAD_SIZE
    swapped = 1 + blocks + o_units
    attention_at = 3
    parts_at = max(attention_at + (ATTENTION_STEPS - 1) * blocks, swapped, 7)
    second_at = attention_at + ATTENTION_STEPS * blocks
    kv_at = max(second_at + q_units, parts_at + blocks)
    hold = max(
        0,
        swapped + 1 - feed_left,
        second_at + 1 - (feed_left + o_units),
        kv_at + 1 - (scatter_units - 1),
    )
    gains_at = parts_at + blocks + 4
    length = max(gains_at + 1, scatter_units + hold + scatter.latency())

    def each_block(work):
        def step(number, _):
            work(blocks - 1 - number)
            return 0

        lax.fori_loop(0, blocks, step, 0)

    def open_sums():
        each_block(db_sum.begin)
        first_weights()
        each_block(db_sum.middle)

    def attention_step(time):
        index = time - attention_at
        blk = blocks - 1 - index // ATTENTION_STEPS
        some = -(-heads // ATTENTION_STEPS)
        first = lax.rem(index, ATTENTION_STEPS) * some
        last = jnp.minimum(first + some, heads)
        half_way = blocks // 2

        @pl.when(blk >= half_way)
        def _():
            attention_heads(blk, first, last, token_count)

        @pl.when(blk < half_way)
        def _():
            attention_heads(blk, first, last, token_count // 2)

    def steps(time):
        def blockwise(start, work):
            @pl.when((time >= start) & (time < start + blocks))
            def _():
                work(blocks - 1 - (time - start))

        pl.when(time == 0)(open_sums)
        blockwise(1, db_sum.late)
        blockwise(2, middle_grad)
        blockwise(3, out_sum.begin)
        blockwise(4, out_sum.middle)
        blockwise(6, out_sum.late)
        blockwise(7, out_end)

        @pl.when((time >= attention_at) & (time < second_at))
        def _():
            attention_step(time)

        o_at = swapped - o_units + 1
        number = jnp.where(
            time < second_at,
            time - o_at,
            jnp.where(time < second_at + q_units, time - second_at + o_units, o_units + q_units),
        )

        @pl.when(
            ((time >= o_at) & (time < o_at + o_units))
            | ((time >= second_at) & (time < second_at + q_units))
            | (time == kv_at)
        )
        def _():
            save_grad(number)

        pl.when(time == swapped)(second_weights)
        blockwise(parts_at, input_part)
        blockwise(parts_at + 1, summer.middle)
        blockwise(parts_at + 3, summer.late)
        blockwise(parts_at + 4, finish)

    def gain_copy(step):
        dest = lax.rem(place.me + step, count)
        return pltpu.make_async_remote_copy(
            gain_blocks.at[dest],
            gain_land.at[place.me],
            gain_send.at[step],
            gain_recv.at[place.me],
            device_id={"dp": dest},
            device_id_type=MESH,
        )

    def gain_arrival(source):
        return pltpu.make_async_remote_copy(
            gain_blocks.at[0],
            gain_land.at[source],
            gain_send.at[0],
            gain_recv.at[source],
            device_id={"dp": place.partner},
            device_id_type=MESH,
        )

    def send_gains():
        for source in range(count):
            gain_blocks[source] = gain_acc[:, source * rows : (source + 1) * rows]
        for step in range(1, count):
            gain_copy(step).start()

    def body(time, _):
        scatter.tick(time - hold)
        steps(time)
        pl.when(time == gains_at)(send_gains)
        return 0

    lax.fori_loop(0, length, body, 0)
    summed = gain_blocks[place.me]
    for step in range(1, count):
        source = lax.rem(place.me + step, count)
        gain_arrival(source).wait_recv()
        summed = summed + gain_land[source]
    gain_ref[...] = summed
    for step in range(1, count):
        gain_copy(step).wait_send()
    scatter.finish()


def attend_back(
    tokens, q, k, v, att, cols, rows_of, cosine, sine, gains, cotangent, att_sum, part_db,
    part_out, a, gathered, grads, z_in, kept, depth, first_grad, q_units, o_units,
):
    token_count, width = tokens.shape
    rows = width // (depth * FOLD)
    blocks, half = token_count // ROWS, ROWS // 2
    q_width, kv_width = q.shape[1], k.shape[1]
    scatter_units = grads.shape[0] - first_grad
    sum_bufs, sum_sems = TensorSum.scratch(blocks, half, width)
    count = depth * FOLD
    wide = max(q_units + 1, o_units)
    return pl.pallas_call(
        functools.partial(back_kernel, (depth, first_grad, scatter_units, q_units, o_units)),
        out_shape=(
            jax.ShapeDtypeStruct(grads.shape, BF16),
            *Scatter.outputs(scatter_units, grads.shape[0], depth, rows),
            jax.ShapeDtypeStruct((token_count, width), BF16),
            jax.ShapeDtypeStruct((token_count, width), BF16),
            jax.ShapeDtypeStruct((8, rows), F32),
        ),
        in_specs=[VMEM_SPEC] * 10 + [HBM_SPEC] * 9,
        out_specs=[HBM_SPEC] * 6 + [VMEM_SPEC],
        scratch_shapes=[
            VMEM((token_count, width), F32),
            VMEM((token_count, width), BF16),
            VMEM((wide, width, UNIT), BF16),
            VMEM((token_count, q_width), BF16),
            VMEM((token_count, q_width), BF16),
            VMEM((token_count, 2 * kv_width), BF16),
            VMEM((token_count, kv_width), F32),
            VMEM((token_count, kv_width), F32),
            VMEM((blocks, ROWS, width), BF16),
            *sum_bufs,
            VMEM((blocks, half, width), BF16),
            VMEM((blocks, half, width), BF16),
            VMEM((half, width), BF16),
            VMEM((token_count, ROWS), F32),
            VMEM((width, UNIT), BF16),
            VMEM((token_count, UNIT), BF16),
            VMEM((8, width), F32),
            VMEM((count, 8, rows), F32),
            VMEM((count, 8, rows), F32),
            *sum_sems,
            *sum_sems,
            *sum_sems,
            DMA((count,)),
            DMA((count,)),
            DMA((8,)),
            *Scatter.scratch(scatter_units, depth, rows),
        ],
        input_output_aliases={16: 0, 17: 2, 18: 3},
        compiler_params=pltpu.CompilerParams(
            collective_id=2, has_side_effects=True, vmem_limit_bytes=63 << 20
        ),
        name="attend_back",
    )(
        tokens, q, k, v, att, cols, rows_of, cosine, sine, gains, cotangent, att_sum, part_db,
        part_out, a, gathered, grads, z_in, kept,
    )


def settle_kernel(kept_ref, z_ref, gate_ref, up_ref, down_ref):
    steps = z_ref.shape[1]
    for number, out_ref in enumerate((gate_ref, up_ref, down_ref)):
        total = kept_ref[number].astype(F32)
        for step in range(steps):
            total = total + z_ref[number, step].astype(F32)
        out_ref[...] = total if number < 2 else total.T


def settle(kept, z_in, chunks):
    _, rows, cols = kept.shape
    steps = z_in.shape[1]
    wide = pl.BlockSpec((rows, cols), lambda i: (0, i))
    return pl.pallas_call(
        settle_kernel,
        grid=(chunks,),
        out_shape=(
            jax.ShapeDtypeStruct((rows, chunks * cols), F32),
            jax.ShapeDtypeStruct((rows, chunks * cols), F32),
            jax.ShapeDtypeStruct((chunks * cols, rows), F32),
        ),
        in_specs=[
            pl.BlockSpec((3, rows, cols), lambda i: (i, 0, 0)),
            pl.BlockSpec((3, steps, rows, cols), lambda i: (i, 0, 0, 0)),
        ],
        out_specs=[wide, wide, pl.BlockSpec((cols, rows), lambda i: (i, 0))],
        name="settle",
    )(kept, z_in)


def shards(
    depth,
    tokens,
    attention_gain,
    query_matrix,
    key_matrix,
    value_matrix,
    output_weight,
    feed_gain,
    gate_weight,
    up_weight,
    down_weight,
    sequence_lengths,
    block_mask,
    cotangent,
):
    token_count, width = tokens.shape
    rows, q_width = query_matrix.shape
    kv_width = key_matrix.shape[1]
    heads_kv = kv_width // HEAD_SIZE
    groups = q_width // kv_width
    feed_width = gate_weight.shape[1]
    chunks = feed_width // UNIT
    q_units = q_width // UNIT

    def pair(cols):
        return cols.reshape(-1, heads_kv, groups, HEAD_SIZE).swapaxes(1, 2).reshape(-1, q_width)

    def unpair(cols):
        return cols.reshape(-1, groups, heads_kv, HEAD_SIZE).swapaxes(1, 2).reshape(-1, q_width)

    def units_of(cols):
        return cols.reshape(rows, -1, UNIT).swapaxes(0, 1)

    feed_units = jnp.stack(
        [units_of(gate_weight), units_of(up_weight), units_of(down_weight.T)], axis=1
    ).reshape(3 * chunks, rows, UNIT)
    own = jnp.concatenate(
        [
            units_of(pair(query_matrix)),
            units_of(jnp.concatenate([key_matrix, value_matrix], axis=1)),
            units_of(pair(output_weight.T)),
            feed_units,
        ],
        axis=0,
    )
    sequence, position, valid = token_layout(sequence_lengths[0], token_count, BLOCK)
    query_code, key_code = slot_codes(sequence, valid, block_mask, BLOCK)
    cols = jnp.stack([query_code, key_code], axis=1)
    rows_of = jnp.stack([query_code, key_code], axis=0)
    cosine, sine = rope_tables(position, HEAD_SIZE)
    wide_cos = jnp.concatenate([cosine] * 4, axis=1)
    wide_sin = jnp.concatenate([-sine, sine] * 2, axis=1)
    gain_rows = jnp.concatenate(
        [
            attention_gain.astype(F32)[None],
            feed_gain.astype(F32)[None],
            jnp.zeros((6, rows), F32),
        ],
        axis=0,
    )
    first_unit = 2 * q_units + 1
    pieces = split(depth) * (first_unit + 3 * EARLY_CHUNKS)
    gathered, a, q, k, v, att, att_sum, b, gains = attend(
        tokens, own, gain_rows, cols, rows_of, wide_cos, wide_sin, depth, pieces, q_units, q_units
    )
    gathered, grads, _, z_in, kept, part_out, part_db = feed(
        b,
        cotangent,
        gathered,
        depth,
        (first_unit, chunks, EARLY_CHUNKS, pieces, EARLY_UNITS, SCATTER_EVERY),
    )
    _, _, z_in, kept, input_grad, block_output, gain_grads = attend_back(
        tokens, q, k, v, att, cols, rows_of, wide_cos, wide_sin, gains, cotangent, att_sum,
        part_db, part_out, a, gathered, grads, z_in, kept, depth, EARLY_UNITS, q_units, q_units,
    )
    gate_grad, up_grad, down_grad = settle(kept, z_in, chunks)
    late = kept[3 * chunks :].astype(F32) + jnp.sum(z_in[3 * chunks :].astype(F32), axis=1)

    def row_of(units):
        return units.swapaxes(0, 1).reshape(rows, -1)

    out_grad = row_of(late[:q_units]).T
    kv_grad = late[2 * q_units]
    out_grad = out_grad.reshape(groups, heads_kv, HEAD_SIZE, rows).swapaxes(0, 1)
    return (
        block_output,
        input_grad.astype(F32),
        gain_grads[0],
        unpair(row_of(late[q_units : 2 * q_units])),
        kv_grad[:, :kv_width],
        kv_grad[:, kv_width:],
        out_grad.reshape(q_width, rows),
        gain_grads[1],
        gate_grad,
        up_grad,
        down_grad,
    )


def solution(mesh):
    in_specs = (
        P("dp", None),
        P("dp"),
        P("dp", "tensor"),
        P("dp", "tensor"),
        P("dp", "tensor"),
        P("tensor", "dp"),
        P("dp"),
        P("dp", "tensor"),
        P("dp", "tensor"),
        P("tensor", "dp"),
        P("dp", None),
        P("dp", None),
        P("dp", None),
    )
    out_specs = (
        P("dp", None),
        P("dp", None),
        P("dp"),
        P("dp", "tensor"),
        P("dp", "tensor"),
        P("dp", "tensor"),
        P("tensor", "dp"),
        P("dp"),
        P("dp", "tensor"),
        P("dp", "tensor"),
        P("tensor", "dp"),
    )
    return jax.shard_map(
        functools.partial(shards, mesh.shape["dp"] // FOLD),
        mesh=mesh,
        in_specs=in_specs,
        out_specs=out_specs,
        check_vma=False,
    )
```
